32 devices in a mesh: dp: 8 (over z, y), tensor: 4 (over x, core).
Axes of the slice: x: 2, y: 2, z: 4, core: 2. Of those that a mesh axis runs over, the one named last changes fastest.
Arguments:
- tokens: bfloat16 [16384, 768], P('dp'), may hold values from -6 to 6
- w_query: bfloat16 [768, 768], P(None, 'tensor'), may hold values from -0.21875 to 0.21875
- w_key: bfloat16 [768, 768], P(None, 'tensor'), may hold values from -0.21875 to 0.21875
- w_value: bfloat16 [768, 768], P(None, 'tensor'), may hold values from -0.21875 to 0.21875
- b_query: float32 [768], P('tensor'), may hold values from -4 to 4
- b_value: float32 [768], P('tensor'), may hold values from -3 to 3
- conv_taps: float32 [12, 33], P('tensor'), may hold values from -0.3 to 0.3
- w_out: bfloat16 [768, 768], P('tensor'), may hold values from -0.875 to 0.875
- b_out: float32 [768], replicated, may hold values from -3 to 3
- gain_one: float32 [768], replicated, may hold values from 0.5 to 1.5
- shift_one: float32 [768], replicated, may hold values from -3 to 3
- w_up: bfloat16 [768, 3072], P(None, 'tensor'), may hold values from -0.21875 to 0.21875
- b_up: float32 [3072], P('tensor'), may hold values from -3 to 3
- w_down: bfloat16 [3072, 768], P('tensor'), may hold values from -0.109375 to 0.109375
- b_down: float32 [768], replicated, may hold values from -3 to 3
- gain_two: float32 [768], replicated, may hold values from 0.5 to 1.5
- shift_two: float32 [768], replicated, may hold values from -3 to 3
- cotangent: bfloat16 [16384, 768], P(('dp', 'tensor')), may hold values from -6 to 6
- segment_ids: int32 [16384], P('dp'), may hold values from 0 to 7, as said below
- landmark_ids: int32 [16384], P('dp'), may hold values from 0 to 63, as said below
Outputs:
- layer_out: bfloat16 [16384, 768], P(('dp', 'tensor'))
- input_grad: float32 [16384, 768], P(('dp', 'tensor'))
- grad_w_query: float32 [768, 768], P(None, 'tensor')
- grad_w_key: float32 [768, 768], P(None, 'tensor')
- grad_w_value: float32 [768, 768], P(None, 'tensor')
- grad_b_query: float32 [768], P('tensor')
- grad_b_value: float32 [768], P('tensor')
- grad_conv: float32 [12, 33], P('tensor')
- grad_w_out: float32 [768, 768], P('tensor')
- grad_b_out: float32 [768], replicated
- grad_gain_one: float32 [768], replicated
- grad_shift_one: float32 [768], replicated
- grad_w_up: float32 [768, 3072], P(None, 'tensor')
- grad_b_up: float32 [3072], P('tensor')
- grad_w_down: float32 [3072, 768], P('tensor')
- grad_b_down: float32 [768], replicated
- grad_gain_two: float32 [768], replicated
- grad_shift_two: float32 [768], replicated
The draws below stay inside these ranges and needn't reach their ends.
Inputs may be any that keep to these rules, and one draw needn't show every extreme that they name: `segment_ids`: within each sequence of 1024 tokens the ids never fall and take every value from 0 to 7; every document holds 64 tokens or more. `landmark_ids`: within each sequence every id from 0 to 63 occurs, and the tokens with id j form one run inside document j // 8.
All inputs are finite; a program needn't handle non-finite values.
Results may differ from the reference program's by a relative error of at most 0.015.
Values may be sent and summed in bfloat16 or wider, within the bound.
No kernel may reach another device: no remote copies, remote signals or barrier semaphores. Data moves between devices by JAX's collectives and lax.ppermute only.
A program may use at most 256 MiB of HBM per device.

```python
import jax
import jax.numpy as jnp
from jax import lax

D = 768
HEADS = 12
HEAD_DIM = 64
FF = 3072
LANDMARKS = 64
CONV_TAPS = 33
PINV_STEPS = 6
DOCS = 8
SEQ_LEN = 1024
SEQS = 16
TOKENS = 16384


def document_layout(key):
    least = SEQ_LEN // (2 * DOCS)
    spare = SEQ_LEN - DOCS * least
    cuts = jnp.sort(jax.random.randint(key, (SEQS, DOCS - 1), 0, spare + 1), axis=1)
    padded_cuts = jnp.concatenate([jnp.zeros((SEQS, 1), jnp.int32), cuts.astype(jnp.int32), jnp.full((SEQS, 1), spare, jnp.int32)], axis=1)
    starts = padded_cuts[:, :DOCS] + least * jnp.arange(DOCS, dtype=jnp.int32)[None, :]
    doc_lengths = padded_cuts[:, 1:] - padded_cuts[:, :DOCS] + least
    positions = jnp.arange(SEQ_LEN, dtype=jnp.int32)
    segment = jnp.sum((positions[None, :, None] >= starts[:, None, 1:]).astype(jnp.int32), axis=2)
    begin = jnp.take_along_axis(starts, segment, axis=1)
    extent = jnp.take_along_axis(doc_lengths, segment, axis=1)
    per_doc = LANDMARKS // DOCS
    landmark = segment * per_doc + (positions[None, :] - begin) * per_doc // extent
    return (segment.reshape(-1), landmark.reshape(-1))


def draw_segment_ids(key, part):
    return document_layout(jax.random.fold_in(key, 17))[0]


def draw_landmark_ids(key, part):
    return document_layout(jax.random.fold_in(key, 17))[1]


def block_scale(own_key, shape, cuts, low, top_value):
    gain = 1.0
    for dim, blocks in cuts:
        steps = jax.random.uniform(jax.random.fold_in(jax.random.fold_in(own_key, 6), dim), (blocks,), jnp.float32, low / len(cuts), top_value / len(cuts))
        gain = gain * jnp.repeat(jnp.exp(steps), shape[dim] // blocks).reshape((-1,) + (1,) * (len(shape) - 1 - dim))
    return gain


def bell_draw(stream_key, shape, width, bound, cuts=(), kind=jnp.bfloat16):
    entries = jax.random.normal(stream_key, shape, jnp.float32) * width
    if len(cuts) > 0:
        entries = block_scale(stream_key, shape, cuts, -0.22, 0.18) * entries
    return jnp.clip(entries, min=-bound, max=bound).astype(kind)


def setup_inputs(seed: int = 0) -> dict:
    key_of = jax.random.split(jax.random.key(seed), 21)
    return {
        "tokens": bell_draw(key_of[0], (TOKENS, D), 1.0, 6.0, ((0, 8),)),
        "w_query": bell_draw(key_of[1], (D, D), D ** -0.5, 0.21875, ((1, 4),)),
        "w_key": bell_draw(key_of[2], (D, D), D ** -0.5, 0.21875, ((1, 4),)),
        "w_value": bell_draw(key_of[3], (D, D), D ** -0.5, 0.21875, ((1, 4),)),
        "b_query": bell_draw(key_of[4], (D,), 1.0, 4.0, ((0, 4),), jnp.float32),
        "b_value": bell_draw(key_of[5], (D,), 0.5, 3.0, ((0, 4),), jnp.float32),
        "conv_taps": bell_draw(key_of[6], (HEADS, CONV_TAPS), 0.05, 0.3, ((0, 4),), jnp.float32),
        "w_out": bell_draw(key_of[7], (D, D), (D // 16) ** -0.5, 0.875, ((0, 4),)),
        "b_out": bell_draw(key_of[8], (D,), 0.5, 3.0, (), jnp.float32),
        "gain_one": jnp.clip(1.0 + 0.1 * jax.random.normal(key_of[9], (D,), jnp.float32), 0.5, 1.5),
        "shift_one": bell_draw(key_of[10], (D,), 0.5, 3.0, (), jnp.float32),
        "w_up": bell_draw(key_of[11], (D, FF), D ** -0.5, 0.21875, ((1, 4),)),
        "b_up": bell_draw(key_of[12], (FF,), 0.5, 3.0, ((0, 4),), jnp.float32),
        "w_down": bell_draw(key_of[13], (FF, D), FF ** -0.5, 0.109375, ((0, 4),)),
        "b_down": bell_draw(key_of[14], (D,), 0.5, 3.0, (), jnp.float32),
        "gain_two": jnp.clip(1.0 + 0.1 * jax.random.normal(key_of[15], (D,), jnp.float32), 0.5, 1.5),
        "shift_two": bell_draw(key_of[16], (D,), 0.5, 3.0, (), jnp.float32),
        "cotangent": bell_draw(key_of[17], (TOKENS, D), 1.0, 6.0, ((0, 32),)),
        "segment_ids": draw_segment_ids(jax.random.fold_in(key_of[20], 71), 0),
        "landmark_ids": draw_landmark_ids(jax.random.fold_in(key_of[20], 71), 0),
    }


HIGH = lax.Precision.HIGHEST
EPSILON = 1e-05

@jax.custom_vjp
def low(v):
    return lax.optimization_barrier(v.astype(jnp.bfloat16)).astype(jnp.float32)

@jax.custom_vjp
def low_back(v):
    return v

def low_keep(v):
    return (low(v), None)

def low_pass(kept, grad):
    return (grad,)

def back_keep(v):
    return (v, None)

def back_low(kept, grad):
    return (low(grad),)
low.defvjp(low_keep, low_pass)
low_back.defvjp(back_keep, back_low)

def rounded(value):
    return low(low_back(value))

def softmax_masked(scores, allowed):
    masked = jnp.where(allowed, scores, -1e+30)
    highest = lax.optimization_barrier(jnp.max(masked, axis=-1, keepdims=True))
    expo = jnp.exp(masked - highest)
    return expo / lax.optimization_barrier(jnp.sum(expo, axis=-1, keepdims=True))

def layer_norm(inputs, scaling, offsets):
    centered = inputs - lax.optimization_barrier(jnp.mean(inputs, axis=-1, keepdims=True))
    variance = lax.optimization_barrier(jnp.mean(centered * centered, axis=-1, keepdims=True))
    return centered * lax.rsqrt(variance + EPSILON) * scaling + offsets

def nystrom(queries, key_rows, values, conv_weights, segment, landmark):
    row_count = queries.shape[0]
    head_count = queries.shape[1]
    score_scale = queries.shape[2] ** (-0.5)
    one_hot = (landmark[None, :] == jnp.arange(LANDMARKS, dtype=jnp.int32)[:, None]).astype(queries.dtype)
    pooling = one_hot / lax.optimization_barrier(jnp.sum(one_hot, axis=1, keepdims=True))
    land_doc = jnp.arange(LANDMARKS, dtype=jnp.int32) // (LANDMARKS // DOCS)
    near_mask = segment[:, None] == land_doc[None, :]
    mark_mask = land_doc[:, None] == land_doc[None, :]
    key_marks = jnp.einsum('jt,the->jhe', pooling, key_rows, precision=HIGH)
    query_marks = jnp.einsum('jt,the->jhe', pooling, queries, precision=HIGH)
    kernel_one = softmax_masked(jnp.einsum('the,jhe->htj', queries, key_marks, precision=HIGH) * score_scale, near_mask[None])
    middle = softmax_masked(jnp.einsum('ihe,jhe->hij', query_marks, key_marks, precision=HIGH) * score_scale, mark_mask[None])
    kernel_last = softmax_masked(jnp.einsum('jhe,the->hjt', query_marks, key_rows, precision=HIGH) * score_scale, near_mask.T[None])
    column_most = lax.optimization_barrier(jnp.max(lax.optimization_barrier(jnp.sum(middle, axis=1)), axis=1))
    row_most = lax.optimization_barrier(jnp.max(lax.optimization_barrier(jnp.sum(middle, axis=2)), axis=1))
    inverse = jnp.swapaxes(middle, 1, 2) / (column_most * row_most)[:, None, None]
    identity = jnp.eye(LANDMARKS, dtype=middle.dtype)
    for sweep in range(PINV_STEPS):
        product = jnp.einsum('hij,hjk->hik', middle, inverse, precision=HIGH)
        inner_term = 7.0 * identity - product
        inner_term = 15.0 * identity - jnp.einsum('hij,hjk->hik', product, inner_term, precision=HIGH)
        inner_term = 13.0 * identity - jnp.einsum('hij,hjk->hik', product, inner_term, precision=HIGH)
        inverse = 0.25 * jnp.einsum('hij,hjk->hik', inverse, inner_term, precision=HIGH)
    context = jnp.einsum('hjt,the->hje', kernel_last, values, precision=HIGH)
    blended = jnp.einsum('hij,hje->hie', inverse, context, precision=HIGH)
    attended = jnp.einsum('htj,hje->the', kernel_one, blended, precision=HIGH)
    half_width = CONV_TAPS // 2
    padded = jnp.pad(values, ((half_width, half_width), (0, 0), (0, 0)))
    seg_pad = jnp.pad(segment, (half_width, half_width), constant_values=-1)
    for offset in range(CONV_TAPS):
        same_doc = (seg_pad[offset:offset + row_count] == segment).astype(values.dtype)
        attended = attended + conv_weights[:, offset][None, :, None] * padded[offset:offset + row_count] * same_doc[:, None, None]
    return attended.reshape(row_count, head_count * values.shape[2])

def forward(params, inputs, segment, landmark):
    w_query, w_key, w_value, b_query, b_value, conv_weights, w_out, b_out, gain_one, shift_one, w_up, b_up, w_down, b_down, gain_two, shift_two = params
    queries = rounded(jnp.dot(inputs, w_query, precision=HIGH) + b_query)
    key_rows = rounded(jnp.dot(inputs, w_key, precision=HIGH))
    values = rounded(jnp.dot(inputs, w_value, precision=HIGH) + b_value)
    shaped = (inputs.shape[0], HEADS, HEAD_DIM)
    attended = low(nystrom(queries.reshape(shaped), key_rows.reshape(shaped), values.reshape(shaped), conv_weights, segment, landmark))
    summed = low_back(jnp.dot(attended, w_out, precision=HIGH))
    normed = layer_norm(inputs + summed + b_out, gain_one, shift_one)
    hidden = low_back(jnp.dot(rounded(normed), w_up, precision=HIGH) + b_up)
    activated = low(jax.nn.gelu(hidden, approximate=False))
    branch = low_back(jnp.dot(activated, w_down, precision=HIGH))
    return layer_norm(normed + branch + b_down, gain_two, shift_two)

def reference(tokens, w_query, w_key, w_value, b_query, b_value, conv_taps, w_out, b_out, gain_one, shift_one, w_up, b_up, w_down, b_down, gain_two, shift_two, cotangent, segment_ids, landmark_ids):
    params = jax.tree.map(lambda weight: weight.astype(jnp.float32), (w_query, w_key, w_value, b_query, b_value, conv_taps, w_out, b_out, gain_one, shift_one, w_up, b_up, w_down, b_down, gain_two, shift_two))
    seq_total = tokens.shape[0] // SEQ_LEN
    token_blocks = tokens.astype(jnp.float32).reshape(seq_total, SEQ_LEN, D)
    grad_blocks = cotangent.astype(jnp.float32).reshape(seq_total, SEQ_LEN, D)
    seg_blocks = segment_ids.reshape(seq_total, SEQ_LEN)
    mark_blocks = landmark_ids.reshape(seq_total, SEQ_LEN)

    def one_sequence(totals, pieces):
        sequence, grad_out, segment, landmark = pieces
        output, pullback = jax.vjp(lambda weights, inputs: forward(weights, inputs, segment, landmark), params, sequence)
        gradients, grad_in = pullback(grad_out)
        totals = jax.tree.map(lambda total, gradient: total + gradient, totals, gradients)
        return (totals, (output.astype(jnp.bfloat16), grad_in))
    zeros = jax.tree.map(jnp.zeros_like, params)
    totals, (outputs, grad_inputs) = lax.scan(one_sequence, zeros, (token_blocks, grad_blocks, seg_blocks, mark_blocks))
    return (outputs.reshape(tokens.shape[0], D), grad_inputs.reshape(tokens.shape[0], D), totals[0], totals[1], totals[2], totals[3], totals[4], totals[5], totals[6], totals[7], totals[8], totals[9], totals[10], totals[11], totals[12], totals[13], totals[14], totals[15])
```

```python
import jax
import jax.numpy as jnp
from jax import lax
from jax.experimental import pallas as pl
from jax.experimental.pallas import tpu as pltpu
from jax.sharding import PartitionSpec as P

HEAD_DIM = 64
LANDMARKS = 64
CONV_TAPS = 33
PINV_STEPS = 6
DOCS = 8
PER_DOC = LANDMARKS // DOCS
SEQ_LEN = 1024
EPSILON = 1e-05
SCALE = HEAD_DIM ** -0.5
HALF = CONV_TAPS // 2
BLOCK = 128
WINDOW = 256
F32 = jnp.float32
BF16 = jnp.bfloat16
NN = (((1,), (0,)), ((), ()))
NT = (((1,), (1,)), ((), ()))
TN = (((0,), (0,)), ((), ()))


def mm(left, right, dims=NN):
    return lax.dot_general(left, right, dims, preferred_element_type=F32)


def split(value):
    high = value.astype(BF16)
    return high, (value - high.astype(F32)).astype(BF16)


def mm3(left, right, dims=NN):
    lh, ll = left
    rh, rl = right
    return mm(lh, rh, dims) + mm(ll, rh, dims) + mm(lh, rl, dims)


def iota(shape, dim):
    return lax.broadcasted_iota(jnp.int32, shape, dim)


def head_count(width):
    return width // HEAD_DIM


def block_mask(heads):
    shape = (heads * LANDMARKS, heads * HEAD_DIM)
    return iota(shape, 0) // LANDMARKS == iota(shape, 1) // HEAD_DIM


def spread(rows, heads):
    return jnp.where(block_mask(heads), jnp.concatenate([rows] * heads, axis=0), 0.0)


def fold(full, heads):
    return jnp.concatenate(
        [full[h * 64 : (h + 1) * 64, h * 64 : (h + 1) * 64] for h in range(heads)], axis=0
    )


def stack(rows, heads):
    return jnp.concatenate([rows[:, h * 64 : (h + 1) * 64] for h in range(heads)], axis=0)


def unstack(rows, heads):
    return jnp.concatenate([rows[h * 64 : (h + 1) * 64] for h in range(heads)], axis=1)


def block_diag(rows, heads):
    return jnp.where(block_mask(heads), jnp.concatenate([rows] * heads, axis=1), 0.0)


def doc_masks(segment):
    return [jnp.broadcast_to(segment == d, (PER_DOC, segment.shape[1])) for d in range(DOCS)]


def pick(full, masks, heads):
    out = []
    for h in range(heads):
        kept = jnp.zeros(masks[0].shape, F32)
        for d in range(DOCS):
            row = h * LANDMARKS + d * PER_DOC
            kept = jnp.where(masks[d], full[row : row + PER_DOC], kept)
        out.append(kept)
    return out


def place(compact, masks, heads):
    return jnp.concatenate(
        [jnp.where(masks[d], compact[h], 0.0) for h in range(heads) for d in range(DOCS)], axis=0
    )


def per_doc(rows, masks):
    out = jnp.zeros(masks[0].shape, F32)
    for d in range(DOCS):
        out = jnp.where(masks[d], rows[d * PER_DOC : (d + 1) * PER_DOC], out)
    return out


def rows_to_lanes(full, scratch, heads):
    rows = heads * LANDMARKS
    lane_doc = (iota((rows, 128), 1) // PER_DOC) % DOCS
    row_doc = (iota((rows, 128), 0) // PER_DOC) % DOCS
    kept = jnp.where(lane_doc == row_doc, full, 0.0)
    for shift in (8, 16, 32):
        kept = kept + pltpu.roll(kept, shift, 1)
    scratch[0:rows, :] = kept
    count = heads * DOCS
    group = iota((count, 128), 1) // PER_DOC
    out = jnp.zeros((count, 128), F32)
    for i in range(PER_DOC):
        out = jnp.where(group == i, scratch[pl.ds(i, count, stride=PER_DOC), :], out)
    return jnp.concatenate([out, jnp.zeros((128 - count, 128), F32)], axis=0).T[0:64]


def lanes_to_rows(blocks, heads):
    full = jnp.concatenate([blocks, jnp.zeros((64, 128), F32)], axis=0).T
    return full[0 : heads * DOCS]


def apply_blocks(coef, operand_ref, result_ref, heads, transposed):
    count = heads * DOCS
    pieces = [operand_ref[pl.ds(j, count, stride=PER_DOC), :] for j in range(PER_DOC)]
    for i in range(PER_DOC):
        total = jnp.zeros(pieces[0].shape, F32)
        for j in range(PER_DOC):
            k = j * PER_DOC + i if transposed else i * PER_DOC + j
            total = total + coef[:, k : k + 1] * pieces[j]
        result_ref[pl.ds(i, count, stride=PER_DOC), :] = total


def bm(left, right):
    a = left.reshape(8, 8, -1)
    b = right.reshape(8, 8, -1)
    total = a[:, 0:1] * b[0:1]
    for k in range(1, 8):
        total = total + a[:, k : k + 1] * b[k : k + 1]
    return total.reshape(64, -1)


def bm_tn(left, right):
    rows = []
    for i in range(8):
        total = left[i : i + 1] * right[0:8]
        for k in range(1, 8):
            total = total + left[k * 8 + i : k * 8 + i + 1] * right[k * 8 : k * 8 + 8]
        rows.append(total)
    return jnp.concatenate(rows, axis=0)


def flip(blocks, scratch):
    scratch[0:64, :] = blocks
    return jnp.concatenate([scratch[pl.ds(i, 8, stride=8), :] for i in range(8)], axis=0)


def lane_eye():
    row = iota((64, 128), 0)
    return jnp.where(row // 8 == row % 8, 1.0, 0.0)


def column_sums(blocks):
    total = blocks[0:8]
    for i in range(1, 8):
        total = total + blocks[i * 8 : i * 8 + 8]
    return total


def row_sums(blocks):
    return jnp.concatenate(
        [jnp.sum(blocks[i * 8 : i * 8 + 8], axis=0, keepdims=True) for i in range(8)], axis=0
    )


def head_lanes(h):
    return iota((8, 128), 1) // DOCS == h


def head_most(sums, heads):
    out = jnp.ones((1, 128), F32)
    for h in range(heads):
        mask = head_lanes(h)
        most = jnp.max(jnp.max(jnp.where(mask, sums, -1e30), axis=1, keepdims=True), axis=0, keepdims=True)
        out = jnp.where(mask[0:1], most, out)
    return out


def head_total(values, heads):
    out = jnp.zeros((1, 128), F32)
    for h in range(heads):
        mask = head_lanes(h)
        total = jnp.sum(jnp.sum(jnp.where(mask, values, 0.0), axis=1, keepdims=True), axis=0, keepdims=True)
        out = jnp.where(mask[0:1], total, out)
    return out


def same_document(segment, seg_pad, start):
    rows = jnp.broadcast_to(segment[:, start : start + BLOCK], (BLOCK, BLOCK)).T
    return jnp.concatenate([rows, rows], axis=1) == seg_pad[0:1, start : start + WINDOW]


def toeplitz(taps_row):
    return pltpu.roll(jnp.broadcast_to(taps_row, (BLOCK, WINDOW)), 0, 1, stride=1, stride_axis=0)


def attend_forward_kernel(
    where_ref, tokens_ref, wq_ref, wk_ref, wv_ref, bq_ref, bv_ref, taps_ref, w_out_ref, seg_ref, mark_ref,
    keep_ref, send_ref, q_ref, k_ref, v_ref, att_ref, p1_ref, p3_ref, qm_ref, km_ref, ctx_ref, bl_ref, count_ref, mid_ref, steps_ref,
    padded, seg_pad, scratch, band,
):
    width = wq_ref.shape[0]
    heads = head_count(width)
    tokens = tokens_ref.at[0]
    rows = 256

    def project(i, carry):
        at = pl.ds(pl.multiple_of(i * rows, rows), rows)
        x = tokens[at, :]
        q_ref[at, :] = (mm(x, wq_ref[...], NT) + bq_ref[...]).astype(BF16)
        k_ref[at, :] = mm(x, wk_ref[...], NT).astype(BF16)
        value = (mm(x, wv_ref[...], NT) + bv_ref[...]).astype(BF16)
        v_ref[at, :] = value
        padded[pl.ds(pl.multiple_of(i * rows + HALF, 16), rows), :] = value
        return carry

    padded[0:HALF, :] = jnp.zeros((HALF, width), BF16)
    padded[SEQ_LEN + HALF :, :] = jnp.zeros((WINDOW - HALF, width), BF16)
    lax.fori_loop(0, SEQ_LEN // rows, project, 0)

    segment = seg_ref[0].astype(F32)
    masks = doc_masks(segment)
    one_hot = mark_ref[0] == iota((LANDMARKS, SEQ_LEN), 0)
    counts = jnp.sum(one_hot.astype(F32), axis=1, keepdims=True)
    pool = one_hot.astype(BF16)
    q_marks = mm(pool, q_ref[...]) / counts
    k_marks = mm(pool, k_ref[...]) / counts
    count_ref[...] = jnp.broadcast_to(counts, (LANDMARKS, 128))
    qm_ref[...] = q_marks
    km_ref[...] = k_marks
    k_block = split(spread(k_marks, heads))
    q_wide = spread(q_marks, heads)
    q_block = split(q_wide)

    queries = q_ref[...]
    scores = pick(mm(k_block[0], queries, NT) + mm(k_block[1], queries, NT), masks, heads)
    first = []
    for h in range(heads):
        s = scores[h] * SCALE
        e = jnp.exp(s - jnp.max(s, axis=0, keepdims=True))
        first.append(e / jnp.sum(e, axis=0, keepdims=True))
    p1_ref[...] = jnp.concatenate(first, axis=0)

    keys = k_ref[...]
    scores = pick(mm(q_block[0], keys, NT) + mm(q_block[1], keys, NT), masks, heads)
    last = []
    for h in range(heads):
        s = scores[h] * SCALE
        most = jnp.concatenate(
            [jnp.max(jnp.where(masks[d], s, -1e30), axis=1, keepdims=True) for d in range(DOCS)], axis=0
        )
        e = jnp.exp(s - per_doc(most, masks))
        total = jnp.concatenate(
            [jnp.sum(jnp.where(masks[d], e, 0.0), axis=1, keepdims=True) for d in range(DOCS)], axis=0
        )
        last.append(e / per_doc(total, masks))
    p3_ref[...] = jnp.concatenate(last, axis=0)

    weights = split(place(last, masks, heads))
    values = v_ref[...]
    context = fold(mm(weights[0], values) + mm(weights[1], values), heads)
    ctx_ref[...] = context

    twice = jnp.concatenate([k_marks, k_marks], axis=0)
    grid = lax.dot_general(q_wide, twice, NT, precision=lax.Precision.HIGHEST, preferred_element_type=F32)
    scores = (rows_to_lanes(grid, scratch, heads) * SCALE).reshape(8, 8, 128)
    e = jnp.exp(scores - jnp.max(scores, axis=1, keepdims=True))
    middle = (e / jnp.sum(e, axis=1, keepdims=True)).reshape(64, 128)
    used = iota((64, 128), 1) < heads * DOCS
    middle = jnp.where(used, middle, 0.0)
    mid_ref[...] = middle
    norm = head_most(column_sums(middle), heads) * head_most(row_sums(middle), heads)
    eye = lane_eye()

    def step(n, inverse):
        product = bm(middle, inverse)
        second = 15.0 * eye - bm(product, 7.0 * eye - product)
        third = 13.0 * eye - bm(product, second)
        steps_ref[n, 0] = inverse
        steps_ref[n, 1] = product
        steps_ref[n, 2] = second
        steps_ref[n, 3] = third
        return 0.25 * bm(inverse, third)

    inverse = lax.fori_loop(0, PINV_STEPS, step, flip(middle, scratch) / norm)
    steps_ref[PINV_STEPS, 0] = inverse
    coef = lanes_to_rows(inverse, heads)
    apply_blocks(coef, ctx_ref, bl_ref, heads, False)
    blended = split(block_diag(bl_ref[...], heads))
    weights = split(place(first, masks, heads))
    attended = mm3(weights, blended, TN)

    for h in range(heads):
        tap = split(toeplitz(taps_ref[h : h + 1, :]))
        band[h, 0] = tap[0]
        band[h, 1] = tap[1]
    seg_pad[:, 0:128] = jnp.zeros((8, 128), F32)
    seg_pad[:, 0:SEQ_LEN] = jnp.broadcast_to(pltpu.roll(segment, HALF, 1), (8, SEQ_LEN))
    seg_pad[:, SEQ_LEN:] = jnp.broadcast_to(segment[:, SEQ_LEN - 1 : SEQ_LEN], (8, WINDOW))
    att_ref[...] = attended.astype(BF16)
    lane_head = iota((BLOCK, width), 1) // HEAD_DIM
    scratch_f = attended

    for b in range(SEQ_LEN // BLOCK):
        start = b * BLOCK
        rows_at = pl.ds(start, BLOCK)
        same = same_document(segment, seg_pad, start)
        window = padded[pl.ds(start, WINDOW), :]
        total = scratch_f[start : start + BLOCK]
        for h in range(heads):
            part = mm(jnp.where(same, band[h, 0], 0), window) + mm(jnp.where(same, band[h, 1], 0), window)
            total = total + jnp.where(lane_head == h, part, 0.0)
        att_ref[rows_at, :] = total.astype(BF16)

    half = SEQ_LEN // 2
    core = where_ref[1]
    weight = w_out_ref[...]
    for i in range(half // rows):
        at = pl.ds(pl.multiple_of(core * half + i * rows, rows), rows)
        keep_ref[i * rows : (i + 1) * rows, :] = mm(att_ref[at, :], weight).astype(BF16)
        at = pl.ds(pl.multiple_of((1 - core) * half + i * rows, rows), rows)
        send_ref[i * rows : (i + 1) * rows, :] = mm(att_ref[at, :], weight).astype(BF16)


def attend_forward(where, tokens, wq, wk, wv, bq, bv, taps, w_out, segments, marks):
    dim = tokens.shape[2]
    width = wq.shape[0]
    heads = head_count(width)
    half = SEQ_LEN // 2

    def whole(*shape):
        return pl.BlockSpec(shape, lambda i, w: (0,) * len(shape))

    def one(*shape):
        return pl.BlockSpec((1,) + shape, lambda i, w: (w[0],) + (0,) * len(shape))

    outs = [
        ((half, dim), BF16), ((half, dim), BF16),
        ((SEQ_LEN, width), BF16), ((SEQ_LEN, width), BF16), ((SEQ_LEN, width), BF16), ((SEQ_LEN, width), BF16),
        ((heads * 8, SEQ_LEN), F32), ((heads * 8, SEQ_LEN), F32),
        ((LANDMARKS, width), F32), ((LANDMARKS, width), F32),
        ((heads * LANDMARKS, HEAD_DIM), F32), ((heads * LANDMARKS, HEAD_DIM), F32),
        ((LANDMARKS, 128), F32), ((64, 128), F32), ((PINV_STEPS + 1, 4, 64, 128), F32),
    ]
    return pl.pallas_call(
        attend_forward_kernel,
        out_shape=[jax.ShapeDtypeStruct(s, t) for s, t in outs],
        grid_spec=pltpu.PrefetchScalarGridSpec(
            num_scalar_prefetch=1,
            grid=(1,),
            in_specs=[
                one(SEQ_LEN, dim), whole(width, dim), whole(width, dim), whole(width, dim), whole(1, width), whole(1, width),
                whole(heads, WINDOW), whole(width, dim), one(1, SEQ_LEN), one(1, SEQ_LEN),
            ],
            out_specs=[whole(*s) for s, t in outs],
            scratch_shapes=[
                pltpu.VMEM((SEQ_LEN + WINDOW, width), BF16),
                pltpu.VMEM((8, SEQ_LEN + WINDOW), F32),
                pltpu.VMEM((heads * LANDMARKS, 128), F32),
                pltpu.VMEM((heads, 2, BLOCK, WINDOW), BF16),
            ],
        ),
        compiler_params=pltpu.CompilerParams(vmem_limit_bytes=56 << 20),
        cost_estimate=pl.CostEstimate(flops=6_000_000_000, bytes_accessed=8_000_000, transcendentals=100_000),
    )(where, tokens, wq, wk, wv, bq, bv, taps, w_out, segments, marks)


def diagonal_sums(band):
    row = iota(band.shape, 0)
    for bit in range(7):
        shift = 1 << bit
        moved = pltpu.roll(band, WINDOW - shift, 1)
        band = jnp.where((row // shift) % 2 == 1, moved, band)
    return jnp.sum(band, axis=0, keepdims=True)


def attend_backward_kernel(
    where_ref, mine_ref, theirs_ref, tokens_ref, wq_ref, wk_ref, wv_ref, taps_ref, w_out_ref, seg_ref, mark_ref,
    q_ref, k_ref, v_ref, att_ref, p1_ref, p3_ref, qm_ref, km_ref, ctx_ref, bl_ref, count_ref, mid_ref, steps_ref, prev_ref, prev_small_ref,
    keep_ref, send_ref, weights_ref, small_ref,
    grad_ref, up_ref, value_ref, seg_pad, scratch, scratch_b, band, corr, dbl_ref, dctx_ref, dqm_ref, dkm_ref, stack_ref, dq_ref, dk_ref, dv_ref,
):
    width = wq_ref.shape[0]
    heads = head_count(width)
    half = SEQ_LEN // 2
    core = where_ref[1]
    other = 1 - core
    rows = 256

    grad_ref[0:HALF, :] = jnp.zeros((HALF, width), F32)
    grad_ref[SEQ_LEN + HALF :, :] = jnp.zeros((WINDOW - HALF, width), F32)
    value_ref[0:HALF, :] = jnp.zeros((HALF, width), BF16)
    value_ref[SEQ_LEN + HALF :, :] = jnp.zeros((WINDOW - HALF, width), BF16)
    value_ref[HALF : SEQ_LEN + HALF, :] = v_ref[...]
    for i in range(half // rows):
        at = pl.ds(i * rows, rows)
        to = pl.multiple_of(core * half + i * rows, rows)
        up_ref[pl.ds(to, rows), :] = mine_ref[at, :]
        grad_ref[pl.ds(to + HALF, rows), :] = mm(mine_ref[at, :], w_out_ref[...], NT)
        to = pl.multiple_of(other * half + i * rows, rows)
        up_ref[pl.ds(to, rows), :] = theirs_ref[at, :]
        grad_ref[pl.ds(to + HALF, rows), :] = mm(theirs_ref[at, :], w_out_ref[...], NT)
    attended_grad = mm(att_ref[...], up_ref[...], TN)
    weights_ref[3 * width : 4 * width, :] = prev_ref[3 * width : 4 * width, :] + attended_grad

    segment = seg_ref[0].astype(F32)
    masks = doc_masks(segment)
    pool = (mark_ref[0] == iota((LANDMARKS, SEQ_LEN), 0)).astype(BF16)
    first = [p1_ref[h * 8 : h * 8 + 8, :] for h in range(heads)]
    last = [p3_ref[h * 8 : h * 8 + 8, :] for h in range(heads)]
    gradient = split(grad_ref[HALF : SEQ_LEN + HALF, :])
    values = v_ref[...]
    queries = q_ref[...]
    keys = k_ref[...]

    first_wide = split(place(first, masks, heads))
    dbl = fold(mm3(first_wide, gradient), heads)
    dbl_ref[...] = dbl
    blended = split(block_diag(bl_ref[...], heads))
    dfirst = pick(mm3(blended, gradient, NT), masks, heads)
    dscore = [
        SCALE * first[h] * (dfirst[h] - jnp.sum(first[h] * dfirst[h], axis=0, keepdims=True)) for h in range(heads)
    ]
    dscore_one = split(place(dscore, masks, heads))
    dkm = fold(mm(dscore_one[0], queries) + mm(dscore_one[1], queries), heads)

    inverse = steps_ref[PINV_STEPS, 0]
    apply_blocks(lanes_to_rows(inverse, heads), dbl_ref, dctx_ref, heads, True)
    dctx = dctx_ref[...]
    context = unstack(ctx_ref[...], heads)
    grid = lax.dot_general(
        block_diag(dbl, heads), jnp.concatenate([context, context], axis=0), NT,
        precision=lax.Precision.HIGHEST, preferred_element_type=F32,
    )
    dinverse = rows_to_lanes(grid, scratch, heads)
    middle = mid_ref[...]
    eye = lane_eye()

    def step(n, carry):
        dz, dmid = carry
        n = PINV_STEPS - 1 - n
        z = steps_ref[n, 0]
        product = steps_ref[n, 1]
        second = steps_ref[n, 2]
        third = steps_ref[n, 3]
        dthird = 0.25 * bm_tn(z, dz)
        dz_next = 0.25 * bm(dz, flip(third, scratch_b.at[0]))
        dsecond = -bm_tn(product, dthird)
        dprod = -bm(dthird, flip(second, scratch_b.at[1])) - bm(dsecond, flip(7.0 * eye - product, scratch_b.at[2]))
        dprod = dprod + bm_tn(product, dsecond)
        dmid = dmid + bm(dprod, flip(z, scratch_b.at[3]))
        dz_next = dz_next + bm_tn(middle, dprod)
        return dz_next, dmid

    dz, dmid = lax.fori_loop(0, PINV_STEPS, step, (dinverse, jnp.zeros((64, 128), F32)))
    columns = column_sums(middle)
    across = row_sums(middle)
    column_most = head_most(columns, heads)
    row_most = head_most(across, heads)
    start = flip(middle, scratch) / (column_most * row_most)
    dmid = dmid + flip(dz, scratch) / (column_most * row_most)
    total = jnp.sum(dz * start, axis=0, keepdims=True)
    total = head_total(jnp.where(iota((8, 128), 0) == 0, jnp.broadcast_to(total, (8, 128)), 0.0), heads)
    hit = jnp.where(columns == column_most, 1.0, 0.0)
    dcolumns = -total / column_most * hit / jnp.maximum(head_total(hit, heads), 1.0)
    hit = jnp.where(across == row_most, 1.0, 0.0)
    drows = -total / row_most * hit / jnp.maximum(head_total(hit, heads), 1.0)
    dmid = dmid + jnp.concatenate([dcolumns + drows[i : i + 1] for i in range(8)], axis=0)
    dgrid = jnp.concatenate(
        [
            SCALE * middle[i * 8 : i * 8 + 8]
            * (dmid[i * 8 : i * 8 + 8] - jnp.sum(middle[i * 8 : i * 8 + 8] * dmid[i * 8 : i * 8 + 8], axis=0, keepdims=True))
            for i in range(8)
        ],
        axis=0,
    )
    coef = lanes_to_rows(dgrid, heads)
    q_stack = stack(qm_ref[...], heads)
    k_stack = stack(km_ref[...], heads)
    stack_ref[...] = k_stack
    apply_blocks(coef, stack_ref, dqm_ref, heads, False)
    stack_ref[...] = q_stack
    apply_blocks(coef, stack_ref, dkm_ref, heads, True)

    dctx_wide = split(block_diag(dctx, heads))
    dlast = pick(mm(dctx_wide[0], values, NT) + mm(dctx_wide[1], values, NT), masks, heads)
    inner = jnp.sum(dctx * ctx_ref[...], axis=1, keepdims=True)
    dscore = [
        SCALE * last[h] * (dlast[h] - per_doc(inner[h * 64 : (h + 1) * 64], masks)) for h in range(heads)
    ]
    dscore_last = split(place(dscore, masks, heads))
    dqm = fold(mm(dscore_last[0], keys) + mm(dscore_last[1], keys), heads) + dqm_ref[...]
    dkm = dkm + dkm_ref[...]
    counts = count_ref[:, 0:1]
    dqm = split(unstack(dqm, heads) / counts)
    dkm = split(unstack(dkm, heads) / counts)
    k_wide = split(spread(km_ref[...], heads))
    q_wide = split(spread(qm_ref[...], heads))

    def pulled(scores, wide, marks):
        left = jnp.concatenate([scores[0], pool], axis=0)
        return (
            mm(left, jnp.concatenate([wide[0], marks[0]], axis=0), TN)
            + mm(left, jnp.concatenate([wide[1], marks[1]], axis=0), TN)
            + mm(scores[1], wide[0], TN)
        )

    dq_ref[...] = pulled(dscore_one, k_wide, dqm).astype(BF16)
    dk_ref[...] = pulled(dscore_last, q_wide, dkm).astype(BF16)
    last_wide = split(place(last, masks, heads))
    dvalue = mm3(last_wide, dctx_wide, TN)

    for h in range(heads):
        tap = split(toeplitz(taps_ref[h : h + 1, :]))
        band[h, 0] = tap[0]
        band[h, 1] = tap[1]
        corr[h] = jnp.zeros((BLOCK, WINDOW), F32)
    seg_pad[:, 0:128] = jnp.zeros((8, 128), F32)
    seg_pad[:, 0:SEQ_LEN] = jnp.broadcast_to(pltpu.roll(segment, HALF, 1), (8, SEQ_LEN))
    seg_pad[:, SEQ_LEN:] = jnp.broadcast_to(segment[:, SEQ_LEN - 1 : SEQ_LEN], (8, WINDOW))
    lane_head = iota((BLOCK, width), 1) // HEAD_DIM
    for b in range(SEQ_LEN // BLOCK):
        begin = b * BLOCK
        same = same_document(segment, seg_pad, begin)
        window = split(grad_ref[begin : begin + WINDOW, :])
        near = value_ref[begin : begin + WINDOW, :]
        block = split(grad_ref[begin + HALF : begin + HALF + BLOCK, :])
        total = dvalue[begin : begin + BLOCK]
        for h in range(heads):
            taps = jnp.where(same, band[h, 0], 0)
            part = mm(taps, window[0]) + mm(taps, window[1]) + mm(jnp.where(same, band[h, 1], 0), window[0])
            total = total + jnp.where(lane_head == h, part, 0.0)
            mine = lane_head == h
            part = mm(jnp.where(mine, block[0], 0), near, NT) + mm(jnp.where(mine, block[1], 0), near, NT)
            corr[h] = corr[h] + jnp.where(same, part, 0.0)
        dv_ref[begin : begin + BLOCK, :] = total.astype(BF16)

    small_ref[...] = prev_small_ref[...]
    for h in range(heads):
        small_ref[h : h + 1, :] = prev_small_ref[h : h + 1, :] + diagonal_sums(corr[h])
    small_ref[heads : heads + 1, 0:width] = prev_small_ref[heads : heads + 1, 0:width] + jnp.sum(
        dq_ref[...].astype(F32), axis=0, keepdims=True
    )
    small_ref[heads + 1 : heads + 2, 0:width] = prev_small_ref[heads + 1 : heads + 2, 0:width] + jnp.sum(
        dv_ref[...].astype(F32), axis=0, keepdims=True
    )
    tokens = tokens_ref[0]
    for n, ref in enumerate((dq_ref, dk_ref, dv_ref)):
        at = pl.ds(n * width, width)
        weights_ref[at, :] = prev_ref[at, :] + mm(ref[...], tokens, TN)

    for i in range(half // rows):
        for base, out_ref in ((core, keep_ref), (other, send_ref)):
            at = pl.ds(pl.multiple_of(base * half + i * rows, rows), rows)
            out_ref[i * rows : (i + 1) * rows, :] = (
                mm(dq_ref[at, :], wq_ref[...]) + mm(dk_ref[at, :], wk_ref[...]) + mm(dv_ref[at, :], wv_ref[...])
            ).astype(BF16)


def attend_backward(where, mine, theirs, tokens, wq, wk, wv, taps, w_out, segments, marks, saved, prev, prev_small):
    dim = tokens.shape[2]
    width = wq.shape[0]
    heads = head_count(width)
    half = SEQ_LEN // 2

    def whole(*shape):
        return pl.BlockSpec(shape, lambda i, w: (0,) * len(shape))

    def one(*shape):
        return pl.BlockSpec((1,) + shape, lambda i, w: (w[0],) + (0,) * len(shape))

    outs = [((half, dim), BF16), ((half, dim), BF16), ((4 * width, dim), F32), ((8, WINDOW), F32)]
    return pl.pallas_call(
        attend_backward_kernel,
        out_shape=[jax.ShapeDtypeStruct(s, t) for s, t in outs],
        grid_spec=pltpu.PrefetchScalarGridSpec(
            num_scalar_prefetch=1,
            grid=(1,),
            in_specs=[
                whole(half, dim), whole(half, dim), one(SEQ_LEN, dim),
                whole(width, dim), whole(width, dim), whole(width, dim),
                whole(heads, WINDOW), whole(width, dim), one(1, SEQ_LEN), one(1, SEQ_LEN),
                *[whole(*s.shape) for s in saved], whole(4 * width, dim), whole(8, WINDOW),
            ],
            out_specs=[whole(*s) for s, t in outs],
            scratch_shapes=[
                pltpu.VMEM((SEQ_LEN + WINDOW, width), F32),
                pltpu.VMEM((SEQ_LEN, dim), BF16),
                pltpu.VMEM((SEQ_LEN + WINDOW, width), BF16),
                pltpu.VMEM((8, SEQ_LEN + WINDOW), F32),
                pltpu.VMEM((heads * LANDMARKS, 128), F32),
                pltpu.VMEM((4, 64, 128), F32),
                pltpu.VMEM((heads, 2, BLOCK, WINDOW), BF16),
                pltpu.VMEM((heads, BLOCK, WINDOW), F32),
                *[pltpu.VMEM((heads * LANDMARKS, HEAD_DIM), F32)] * 5,
                *[pltpu.VMEM((SEQ_LEN, width), BF16)] * 3,
            ],
        ),
        compiler_params=pltpu.CompilerParams(vmem_limit_bytes=60 << 20),
        cost_estimate=pl.CostEstimate(flops=12_000_000_000, bytes_accessed=14_000_000, transcendentals=100_000),
    )(where, mine, theirs, tokens, wq, wk, wv, taps, w_out, segments, marks, *saved, prev, prev_small)


ERFC = (
    0.12694266047513267, 0.12694157407364748, 0.11413597639508828, 0.08762459251766126, 0.05998263605520133,
    -0.01120062503236582, 0.07123816174906503, -0.1503297151041413, 0.09536518640917925, -0.020700440227622966,
)


def normal_cdf(value):
    size = jnp.abs(value)
    t = 1.0 / (1.0 + 0.31819805153394637 * size)
    poly = ERFC[-1]
    for coef in ERFC[-2::-1]:
        poly = poly * t + coef
    bell = jnp.exp(-0.5 * size * size)
    tail = bell * (t * poly)
    return jnp.where(value > 0.0, 1.0 - tail, tail), bell


def up_down_kernel(one_ref, two_ref, w_up_ref, b_up_ref, w_down_ref, *outs):
    for n, ref in enumerate((one_ref, two_ref)):
        act_ref, slope_ref, part_ref = outs[3 * n : 3 * n + 3]
        hidden = mm(ref[...], w_up_ref[...]) + b_up_ref[...]
        below, bell = normal_cdf(hidden)
        act = (hidden * below).astype(BF16)
        act_ref[...] = act
        slope_ref[...] = (below + hidden * (bell * 0.3989422804014327)).astype(BF16)
        part_ref[...] = mm(act, w_down_ref[...]).astype(BF16)


def up_down(one, two, w_up, b_up, w_down):
    rows, dim = one.shape
    units = w_up.shape[1]
    step = 128
    block = pl.BlockSpec((step, dim), lambda i: (i, 0))
    wide = pl.BlockSpec((step, units), lambda i: (i, 0))

    def fixed(*shape):
        return pl.BlockSpec(shape, lambda i: (0, 0), pipeline_mode=pl.Buffered(1))

    shapes = [(rows, units), (rows, units), (rows, dim)] * 2
    return pl.pallas_call(
        up_down_kernel,
        out_shape=[jax.ShapeDtypeStruct(s, BF16) for s in shapes],
        grid=(rows // step,),
        in_specs=[block, block, fixed(dim, units), fixed(1, units), fixed(units, dim)],
        out_specs=[wide, wide, block] * 2,
        compiler_params=pltpu.CompilerParams(vmem_limit_bytes=40 << 20),
        cost_estimate=pl.CostEstimate(flops=8 * rows * dim * units, bytes_accessed=8_000_000, transcendentals=2 * rows * units),
    )(one, two, w_up, b_up, w_down)


def up_down_back_kernel(*refs):
    ins, rest = refs[:8], refs[8:]
    w_up_ref, w_down_ref, prev_down_ref, prev_up_ref, prev_bias_ref = rest[:5]
    part_refs, down_ref, up_ref, bias_ref = rest[5:7], rest[7], rest[8], rest[9]

    @pl.when(pl.program_id(0) == 0)
    def _():
        down_ref[...] = prev_down_ref[...]
        up_ref[...] = prev_up_ref[...]
        bias_ref[...] = prev_bias_ref[...]

    for n in range(2):
        grad_ref, act_ref, slope_ref, low_ref = ins[4 * n : 4 * n + 4]
        grad = grad_ref[...]
        hidden = (mm(grad, w_down_ref[...], NT) * slope_ref[...].astype(F32)).astype(BF16)
        part_refs[n][...] = mm(hidden, w_up_ref[...], NT).astype(BF16)
        down_ref[...] += mm(act_ref[...], grad, TN)
        up_ref[...] += mm(low_ref[...], hidden, TN)
        bias_ref[0:1, :] += jnp.sum(hidden.astype(F32), axis=0, keepdims=True)


def up_down_back(one, two, w_up, w_down, prev):
    rows, dim = one[0].shape
    units = w_up.shape[1]
    step = 256
    block = pl.BlockSpec((step, dim), lambda i: (i, 0))
    wide = pl.BlockSpec((step, units), lambda i: (i, 0))

    def fixed(*shape):
        return pl.BlockSpec(shape, lambda i: (0, 0), pipeline_mode=pl.Buffered(1))

    return pl.pallas_call(
        up_down_back_kernel,
        out_shape=[
            jax.ShapeDtypeStruct((rows, dim), BF16), jax.ShapeDtypeStruct((rows, dim), BF16),
            jax.ShapeDtypeStruct((units, dim), F32), jax.ShapeDtypeStruct((dim, units), F32), jax.ShapeDtypeStruct((8, units), F32),
        ],
        grid=(rows // step,),
        in_specs=[block, wide, wide, block] * 2
        + [fixed(dim, units), fixed(units, dim), fixed(units, dim), fixed(dim, units), fixed(8, units)],
        out_specs=[block, block, fixed(units, dim), fixed(dim, units), fixed(8, units)],
        compiler_params=pltpu.CompilerParams(vmem_limit_bytes=56 << 20),
        cost_estimate=pl.CostEstimate(flops=16 * rows * dim * units, bytes_accessed=16_000_000, transcendentals=0),
    )(*one, *two, w_up, w_down, *prev)


def swap(value, mask, axis="tensor"):
    count = lax.axis_size(axis)
    return lax.ppermute(value, axis, [(i, i ^ mask) for i in range(count)])


def gather_blocks(mine):
    near = swap(mine, 1)
    far = swap(mine, 2)
    return mine, near, far, swap(far, 1)


def reduce_blocks(mine, near, far, cross):
    through = swap(far + swap(cross, 1), 2)
    return mine.astype(F32) + swap(near, 1).astype(F32) + through.astype(F32)


def normalize(value):
    centered = value - jnp.mean(value, axis=-1, keepdims=True)
    inv = lax.rsqrt(jnp.mean(centered * centered, axis=-1, keepdims=True) + EPSILON)
    return centered * inv, inv


def norm_back(grad, gain, unit, inv):
    r = grad * gain
    back = (r - jnp.mean(r, axis=-1, keepdims=True) - unit * jnp.mean(r * unit, axis=-1, keepdims=True)) * inv
    return back, jnp.sum(grad * unit, axis=0), jnp.sum(grad, axis=0)


def per_device(
    tokens, w_query, w_key, w_value, b_query, b_value, conv_taps, w_out, b_out, gain_one, shift_one, w_up, b_up, w_down,
    b_down, gain_two, shift_two, cotangent, segment_ids, landmark_ids,
):
    dim = tokens.shape[1]
    width = w_query.shape[1]
    heads = head_count(width)
    seqs = tokens.shape[0] // SEQ_LEN
    me = lax.axis_index("tensor")
    core, chip = me % 2, me // 2
    own_rows = cotangent.shape[0]
    sequences = tokens.reshape(seqs, SEQ_LEN, dim)
    segments = segment_ids.reshape(seqs, 1, SEQ_LEN)
    marks = landmark_ids.reshape(seqs, 1, SEQ_LEN)
    at_own = jnp.stack([chip, core]).astype(jnp.int32)
    at_far = jnp.stack([1 - chip, core]).astype(jnp.int32)
    taps = jnp.pad(conv_taps, ((0, 0), (0, WINDOW - CONV_TAPS)))
    taps_back = jnp.pad(conv_taps[:, ::-1], ((0, 0), (0, WINDOW - CONV_TAPS)))
    wq, wk, wv = w_query.T, w_key.T, w_value.T

    def forward(at):
        return attend_forward(
            at, sequences, wq, wk, wv, b_query[None], b_value[None], taps, w_out, segments, marks
        )

    far = forward(at_far)
    own = forward(at_own)
    summed = reduce_blocks(own[0], own[1], far[0], far[1])
    own_tokens = lax.dynamic_slice_in_dim(tokens, me * own_rows, own_rows, 0).astype(F32)
    unit_one, inv_one = normalize(own_tokens + summed + b_out)
    normed = unit_one * gain_one + shift_one
    low = gather_blocks(normed.astype(BF16))
    bias = b_up[None]
    fwd_own = up_down(low[0], low[1], w_up, bias, w_down)
    fwd_far = up_down(low[2], low[3], w_up, bias, w_down)
    branch = reduce_blocks(fwd_own[2], fwd_own[5], fwd_far[2], fwd_far[5])
    unit_two, inv_two = normalize(normed + branch + b_down)
    output = (unit_two * gain_two + shift_two).astype(BF16)
    grad_pre_out, grad_gain_two, grad_shift_two = norm_back(cotangent.astype(F32), gain_two, unit_two, inv_two)
    grad_b_down = jnp.sum(grad_pre_out, axis=0)
    grad = gather_blocks(grad_pre_out.astype(BF16))
    units = w_up.shape[1]
    zero = (jnp.zeros((units, dim), F32), jnp.zeros((dim, units), F32), jnp.zeros((8, units), F32))
    back_own = up_down_back(
        (grad[0], fwd_own[0], fwd_own[1], low[0]), (grad[1], fwd_own[3], fwd_own[4], low[1]), w_up, w_down, zero
    )
    back_far = up_down_back(
        (grad[2], fwd_far[0], fwd_far[1], low[2]), (grad[3], fwd_far[3], fwd_far[4], low[3]), w_up, w_down, back_own[2:]
    )
    back_normed = reduce_blocks(back_own[0], back_own[1], back_far[0], back_far[1])
    grad_pre_norm, grad_gain_one, grad_shift_one = norm_back(grad_pre_out + back_normed, gain_one, unit_one, inv_one)
    grad_b_out = jnp.sum(grad_pre_norm, axis=0)
    up = gather_blocks(grad_pre_norm.astype(BF16))
    ffn_sum = lax.psum(jnp.concatenate([back_far[2], back_far[3]], axis=0).astype(BF16), "dp")

    def backward(at, mine, theirs, saved, prev, prev_small):
        return attend_backward(
            at, mine, theirs, sequences, wq, wk, wv, taps_back, w_out, segments, marks, saved, prev, prev_small
        )

    none = (jnp.zeros((4 * width, dim), F32), jnp.zeros((8, WINDOW), F32))
    first = backward(at_own, up[0], up[1], own[2:], *none)
    second = backward(at_far, up[2], up[3], far[2:], first[2], first[3])
    input_grad = grad_pre_norm + reduce_blocks(first[0], first[1], second[0], second[1])
    attend_sum, ffn_sum = lax.optimization_barrier((second[2].astype(BF16), ffn_sum))
    attend_sum = lax.psum(attend_sum, "dp").astype(F32)
    ffn_sum = ffn_sum.astype(F32)

    norms = jnp.stack([grad_gain_one, grad_shift_one, grad_b_out, grad_gain_two, grad_shift_two, grad_b_down])
    for mask in (1, 2):
        norms = norms + swap(norms, mask)
    small = jnp.concatenate(
        [norms, back_far[4][0:1], jnp.pad(second[3][0 : heads + 2], ((0, 0), (0, dim - WINDOW)))], axis=0
    )
    mask = 1
    while mask < lax.axis_size("dp"):
        small = small + swap(small, mask, "dp")
        mask *= 2
    return (
        output,
        input_grad,
        attend_sum[0:width].T,
        attend_sum[width : 2 * width].T,
        attend_sum[2 * width : 3 * width].T,
        small[7 + heads, 0:width],
        small[8 + heads, 0:width],
        small[7 : 7 + heads, 0:CONV_TAPS],
        attend_sum[3 * width :],
        small[2],
        small[0],
        small[1],
        ffn_sum[units:],
        small[6, 0:units],
        ffn_sum[0:units],
        small[5],
        small[3],
        small[4],
    )


def solution(mesh):
    rows = P(("dp", "tensor"), None)
    columns = P(None, "tensor")
    split_rows = P("tensor", None)
    vector = P("tensor")
    return jax.shard_map(
        per_device,
        mesh=mesh,
        in_specs=(
            P("dp", None), columns, columns, columns, vector, vector, split_rows, split_rows, P(), P(), P(),
            columns, vector, split_rows, P(), P(), P(), rows, P("dp"), P("dp"),
        ),
        out_specs=(
            rows, rows, columns, columns, columns, vector, vector, split_rows, split_rows, P(), P(), P(),
            columns, vector, split_rows, P(), P(), P(),
        ),
        check_vma=False,
    )
```

```python
import functools

import jax
import jax.numpy as jnp
from jax import lax
from jax.experimental import pallas as pl
from jax.experimental.pallas import tpu as pltpu
from jax.sharding import PartitionSpec as P

HEAD_DIM = 64
LANDMARKS = 64
CONV_TAPS = 33
PINV_STEPS = 6
DOCS = 8
PER_DOC = LANDMARKS // DOCS
SEQ_LEN = 1024
EPSILON = 1e-05
SCALE = HEAD_DIM ** -0.5
HALF = CONV_TAPS // 2
BLOCK = 128
WINDOW = 256
CHUNK = 256
F32 = jnp.float32
BF16 = jnp.bfloat16
NN = (((1,), (0,)), ((), ()))
NT = (((1,), (1,)), ((), ()))
TN = (((0,), (0,)), ((), ()))


def takes(microseconds):
    return pl.CostEstimate(flops=int(microseconds * 1.1e9), bytes_accessed=1, transcendentals=0)


def mm(left, right, dims=NN):
    return lax.dot_general(left, right, dims, preferred_element_type=F32)


def split(value):
    high = value.astype(BF16)
    return high, (value - high.astype(F32)).astype(BF16)


def mm3(left, right, dims=NN):
    lh, ll = left
    rh, rl = right
    return mm(lh, rh, dims) + mm(ll, rh, dims) + mm(lh, rl, dims)


def iota(shape, dim):
    return lax.broadcasted_iota(jnp.int32, shape, dim)


def head_count(width):
    return width // HEAD_DIM


def block_mask(heads):
    shape = (heads * LANDMARKS, heads * HEAD_DIM)
    return iota(shape, 0) // LANDMARKS == iota(shape, 1) // HEAD_DIM


def spread(rows, heads):
    return jnp.where(block_mask(heads), jnp.concatenate([rows] * heads, axis=0), 0.0)


def fold(full, heads):
    return jnp.concatenate(
        [full[h * 64 : (h + 1) * 64, h * 64 : (h + 1) * 64] for h in range(heads)], axis=0
    )


def stack(rows, heads):
    return jnp.concatenate([rows[:, h * 64 : (h + 1) * 64] for h in range(heads)], axis=0)


def unstack(rows, heads):
    return jnp.concatenate([rows[h * 64 : (h + 1) * 64] for h in range(heads)], axis=1)


def block_diag(rows, heads):
    return jnp.where(block_mask(heads), jnp.concatenate([rows] * heads, axis=1), 0.0)


def doc_masks(segment):
    return [jnp.broadcast_to(segment == d, (PER_DOC, segment.shape[1])) for d in range(DOCS)]


def pick(full, masks, heads):
    out = []
    for h in range(heads):
        kept = jnp.zeros(masks[0].shape, F32)
        for d in range(DOCS):
            row = h * LANDMARKS + d * PER_DOC
            kept = jnp.where(masks[d], full[row : row + PER_DOC], kept)
        out.append(kept)
    return out


def place(compact, masks, heads):
    return jnp.concatenate(
        [jnp.where(masks[d], compact[h], 0.0) for h in range(heads) for d in range(DOCS)], axis=0
    )


def per_doc(rows, masks):
    out = jnp.zeros(masks[0].shape, F32)
    for d in range(DOCS):
        out = jnp.where(masks[d], rows[d * PER_DOC : (d + 1) * PER_DOC], out)
    return out


def rows_to_lanes(full, scratch, heads):
    rows = heads * LANDMARKS
    lane_doc = (iota((rows, 128), 1) // PER_DOC) % DOCS
    row_doc = (iota((rows, 128), 0) // PER_DOC) % DOCS
    kept = jnp.where(lane_doc == row_doc, full, 0.0)
    for shift in (8, 16, 32):
        kept = kept + pltpu.roll(kept, shift, 1)
    scratch[0:rows, :] = kept
    count = heads * DOCS
    group = iota((count, 128), 1) // PER_DOC
    out = jnp.zeros((count, 128), F32)
    for i in range(PER_DOC):
        out = jnp.where(group == i, scratch[pl.ds(i, count, stride=PER_DOC), :], out)
    return jnp.concatenate([out, jnp.zeros((128 - count, 128), F32)], axis=0).T[0:64]


def lanes_to_rows(blocks, heads):
    full = jnp.concatenate([blocks, jnp.zeros((64, 128), F32)], axis=0).T
    return full[0 : heads * DOCS]


def apply_blocks(coef, operand_ref, result_ref, heads, transposed):
    count = heads * DOCS
    pieces = [operand_ref[pl.ds(j, count, stride=PER_DOC), :] for j in range(PER_DOC)]
    for i in range(PER_DOC):
        total = jnp.zeros(pieces[0].shape, F32)
        for j in range(PER_DOC):
            k = j * PER_DOC + i if transposed else i * PER_DOC + j
            total = total + coef[:, k : k + 1] * pieces[j]
        result_ref[pl.ds(i, count, stride=PER_DOC), :] = total


def bm(left, right):
    a = left.reshape(8, 8, -1)
    b = right.reshape(8, 8, -1)
    total = a[:, 0:1] * b[0:1]
    for k in range(1, 8):
        total = total + a[:, k : k + 1] * b[k : k + 1]
    return total.reshape(64, -1)


def bm_tn(left, right):
    rows = []
    for i in range(8):
        total = left[i : i + 1] * right[0:8]
        for k in range(1, 8):
            total = total + left[k * 8 + i : k * 8 + i + 1] * right[k * 8 : k * 8 + 8]
        rows.append(total)
    return jnp.concatenate(rows, axis=0)


def flip(blocks, scratch):
    scratch[0:64, :] = blocks
    return jnp.concatenate([scratch[pl.ds(i, 8, stride=8), :] for i in range(8)], axis=0)


def lane_eye():
    row = iota((64, 128), 0)
    return jnp.where(row // 8 == row % 8, 1.0, 0.0)


def column_sums(blocks):
    total = blocks[0:8]
    for i in range(1, 8):
        total = total + blocks[i * 8 : i * 8 + 8]
    return total


def row_sums(blocks):
    return jnp.concatenate(
        [jnp.sum(blocks[i * 8 : i * 8 + 8], axis=0, keepdims=True) for i in range(8)], axis=0
    )


def head_lanes(h):
    return iota((8, 128), 1) // DOCS == h


def head_most(sums, heads):
    out = jnp.ones((1, 128), F32)
    for h in range(heads):
        mask = head_lanes(h)
        most = jnp.max(jnp.max(jnp.where(mask, sums, -1e30), axis=1, keepdims=True), axis=0, keepdims=True)
        out = jnp.where(mask[0:1], most, out)
    return out


def head_total(values, heads):
    out = jnp.zeros((1, 128), F32)
    for h in range(heads):
        mask = head_lanes(h)
        total = jnp.sum(jnp.sum(jnp.where(mask, values, 0.0), axis=1, keepdims=True), axis=0, keepdims=True)
        out = jnp.where(mask[0:1], total, out)
    return out


def same_document(segment, seg_pad, start):
    rows = jnp.broadcast_to(segment[:, start : start + BLOCK], (BLOCK, BLOCK)).T
    return jnp.concatenate([rows, rows], axis=1) == seg_pad[0:1, start : start + WINDOW]


def toeplitz(taps_row):
    return pltpu.roll(jnp.broadcast_to(taps_row, (BLOCK, WINDOW)), 0, 1, stride=1, stride_axis=0)


def pad_segment(seg_pad, segment):
    seg_pad[:, 0:128] = jnp.zeros((8, 128), F32)
    seg_pad[:, 0:SEQ_LEN] = jnp.broadcast_to(pltpu.roll(segment, HALF, 1), (8, SEQ_LEN))
    seg_pad[:, SEQ_LEN:] = jnp.broadcast_to(segment[:, SEQ_LEN - 1 : SEQ_LEN], (8, WINDOW))


def attend_forward_kernel(
    where_ref, tokens_ref, wq_ref, wk_ref, wv_ref, bq_ref, bv_ref, taps_ref, w_out_ref, seg_ref, mark_ref,
    keep_a_ref, keep_b_ref, send_a_ref, send_b_ref, q_ref, k_ref, v_ref, att_ref, p1_ref, p3_ref, qm_ref, km_ref, ctx_ref, bl_ref, count_ref, mid_ref, steps_ref,
    padded, seg_pad, scratch, band,
):
    width = wq_ref.shape[0]
    heads = head_count(width)
    tokens = tokens_ref.at[0]
    rows = 256

    def project(i, carry):
        at = pl.ds(pl.multiple_of(i * rows, rows), rows)
        x = tokens[at, :]
        q_ref[at, :] = (mm(x, wq_ref[...], NT) + bq_ref[...]).astype(BF16)
        k_ref[at, :] = mm(x, wk_ref[...], NT).astype(BF16)
        value = (mm(x, wv_ref[...], NT) + bv_ref[...]).astype(BF16)
        v_ref[at, :] = value
        padded[pl.ds(pl.multiple_of(i * rows + HALF, 16), rows), :] = value
        return carry

    padded[0:HALF, :] = jnp.zeros((HALF, width), BF16)
    padded[SEQ_LEN + HALF :, :] = jnp.zeros((WINDOW - HALF, width), BF16)
    lax.fori_loop(0, SEQ_LEN // rows, project, 0)

    segment = seg_ref[0].astype(F32)
    masks = doc_masks(segment)
    one_hot = mark_ref[0] == iota((LANDMARKS, SEQ_LEN), 0)
    counts = jnp.sum(one_hot.astype(F32), axis=1, keepdims=True)
    pool = one_hot.astype(BF16)
    q_marks = mm(pool, q_ref[...]) / counts
    k_marks = mm(pool, k_ref[...]) / counts
    count_ref[...] = jnp.broadcast_to(counts, (LANDMARKS, 128))
    qm_ref[...] = q_marks
    km_ref[...] = k_marks
    k_block = split(spread(k_marks, heads))
    q_wide = spread(q_marks, heads)
    q_block = split(q_wide)

    queries = q_ref[...]
    scores = pick(mm(k_block[0], queries, NT) + mm(k_block[1], queries, NT), masks, heads)
    first = []
    for h in range(heads):
        s = scores[h] * SCALE
        e = jnp.exp(s - jnp.max(s, axis=0, keepdims=True))
        first.append(e / jnp.sum(e, axis=0, keepdims=True))
    p1_ref[...] = jnp.concatenate(first, axis=0)

    keys = k_ref[...]
    scores = pick(mm(q_block[0], keys, NT) + mm(q_block[1], keys, NT), masks, heads)
    last = []
    for h in range(heads):
        s = scores[h] * SCALE
        most = jnp.concatenate(
            [jnp.max(jnp.where(masks[d], s, -1e30), axis=1, keepdims=True) for d in range(DOCS)], axis=0
        )
        e = jnp.exp(s - per_doc(most, masks))
        total = jnp.concatenate(
            [jnp.sum(jnp.where(masks[d], e, 0.0), axis=1, keepdims=True) for d in range(DOCS)], axis=0
        )
        last.append(e / per_doc(total, masks))
    p3_ref[...] = jnp.concatenate(last, axis=0)

    weights = split(place(last, masks, heads))
    values = v_ref[...]
    context = fold(mm(weights[0], values) + mm(weights[1], values), heads)
    ctx_ref[...] = context

    twice = jnp.concatenate([k_marks, k_marks], axis=0)
    grid = lax.dot_general(q_wide, twice, NT, precision=lax.Precision.HIGHEST, preferred_element_type=F32)
    scores = (rows_to_lanes(grid, scratch, heads) * SCALE).reshape(8, 8, 128)
    e = jnp.exp(scores - jnp.max(scores, axis=1, keepdims=True))
    middle = (e / jnp.sum(e, axis=1, keepdims=True)).reshape(64, 128)
    used = iota((64, 128), 1) < heads * DOCS
    middle = jnp.where(used, middle, 0.0)
    mid_ref[...] = middle
    norm = head_most(column_sums(middle), heads) * head_most(row_sums(middle), heads)
    eye = lane_eye()

    def step(n, inverse):
        product = bm(middle, inverse)
        second = 15.0 * eye - bm(product, 7.0 * eye - product)
        third = 13.0 * eye - bm(product, second)
        steps_ref[n, 0] = inverse
        steps_ref[n, 1] = product
        steps_ref[n, 2] = second
        steps_ref[n, 3] = third
        return 0.25 * bm(inverse, third)

    inverse = lax.fori_loop(0, PINV_STEPS, step, flip(middle, scratch) / norm)
    steps_ref[PINV_STEPS, 0] = inverse
    coef = lanes_to_rows(inverse, heads)
    apply_blocks(coef, ctx_ref, bl_ref, heads, False)
    blended = split(block_diag(bl_ref[...], heads))
    weights = split(place(first, masks, heads))
    attended = mm3(weights, blended, TN)

    for h in range(heads):
        tap = split(toeplitz(taps_ref[h : h + 1, :]))
        band[h, 0] = tap[0]
        band[h, 1] = tap[1]
    pad_segment(seg_pad, segment)
    att_ref[...] = attended.astype(BF16)
    lane_head = iota((BLOCK, width), 1) // HEAD_DIM
    scratch_f = attended

    for b in range(SEQ_LEN // BLOCK):
        start = b * BLOCK
        rows_at = pl.ds(start, BLOCK)
        same = same_document(segment, seg_pad, start)
        window = padded[pl.ds(start, WINDOW), :]
        total = scratch_f[start : start + BLOCK]
        for h in range(heads):
            part = mm(jnp.where(same, band[h, 0], 0), window) + mm(jnp.where(same, band[h, 1], 0), window)
            total = total + jnp.where(lane_head == h, part, 0.0)
        att_ref[rows_at, :] = total.astype(BF16)

    half = SEQ_LEN // 2
    core = where_ref[1]
    weight = w_out_ref[...]
    for base, refs in ((core, (keep_a_ref, keep_b_ref)), (1 - core, (send_a_ref, send_b_ref))):
        for i, ref in enumerate(refs):
            at = pl.ds(pl.multiple_of(base * half + i * CHUNK, CHUNK), CHUNK)
            ref[...] = mm(att_ref[at, :], weight).astype(BF16)


def attend_forward(where, tokens, wq, wk, wv, bq, bv, taps, w_out, segments, marks):
    dim = tokens.shape[2]
    width = wq.shape[0]
    heads = head_count(width)

    def whole(*shape):
        return pl.BlockSpec(shape, lambda i, w: (0,) * len(shape))

    def one(*shape):
        return pl.BlockSpec((1,) + shape, lambda i, w: (w[0],) + (0,) * len(shape))

    outs = [
        *[((CHUNK, dim), BF16)] * 4,
        ((SEQ_LEN, width), BF16), ((SEQ_LEN, width), BF16), ((SEQ_LEN, width), BF16), ((SEQ_LEN, width), BF16),
        ((heads * 8, SEQ_LEN), F32), ((heads * 8, SEQ_LEN), F32),
        ((LANDMARKS, width), F32), ((LANDMARKS, width), F32),
        ((heads * LANDMARKS, HEAD_DIM), F32), ((heads * LANDMARKS, HEAD_DIM), F32),
        ((LANDMARKS, 128), F32), ((64, 128), F32), ((PINV_STEPS + 1, 4, 64, 128), F32),
    ]
    return pl.pallas_call(
        attend_forward_kernel,
        out_shape=[jax.ShapeDtypeStruct(s, t) for s, t in outs],
        grid_spec=pltpu.PrefetchScalarGridSpec(
            num_scalar_prefetch=1,
            grid=(1,),
            in_specs=[
                one(SEQ_LEN, dim), whole(width, dim), whole(width, dim), whole(width, dim), whole(1, width), whole(1, width),
                whole(heads, WINDOW), whole(width, dim), one(1, SEQ_LEN), one(1, SEQ_LEN),
            ],
            out_specs=[whole(*s) for s, t in outs],
            scratch_shapes=[
                pltpu.VMEM((SEQ_LEN + WINDOW, width), BF16),
                pltpu.VMEM((8, SEQ_LEN + WINDOW), F32),
                pltpu.VMEM((heads * LANDMARKS, 128), F32),
                pltpu.VMEM((heads, 2, BLOCK, WINDOW), BF16),
            ],
        ),
        compiler_params=pltpu.CompilerParams(vmem_limit_bytes=56 << 20),
        cost_estimate=takes(12),
    )(where, tokens, wq, wk, wv, bq, bv, taps, w_out, segments, marks)


def diagonal_sums(band):
    row = iota(band.shape, 0)
    for bit in range(7):
        shift = 1 << bit
        moved = pltpu.roll(band, WINDOW - shift, 1)
        band = jnp.where((row // shift) % 2 == 1, moved, band)
    return jnp.sum(band, axis=0, keepdims=True)


def plus(ref, at, value):
    return value if ref is None else ref[at] + value


def sums_refs(final, where_ref, refs, turn):
    if not final:
        weights_ref, *refs = refs
        return None, None, weights_ref, refs, lambda: None
    prev_ref, prev_small_ref, kept_ref, sent_ref, *refs = refs
    *refs, weights_ref = refs

    def finish():
        half = kept_ref.shape[0]
        bit = where_ref[2 + turn]
        kept_ref[...] = weights_ref[pl.ds(pl.multiple_of(bit * half, half), half), :]
        sent_ref[...] = weights_ref[pl.ds(pl.multiple_of((1 - bit) * half, half), half), :].astype(BF16)

    return prev_ref, prev_small_ref, weights_ref, refs, finish


def attend_back_values_kernel(
    final, where_ref, mine_ref, theirs_ref, tokens_ref, taps_ref, w_out_ref, seg_ref,
    v_ref, att_ref, p1_ref, p3_ref, ctx_ref, bl_ref, steps_ref, *refs
):
    prev_ref, prev_small_ref, weights_ref, refs, finish = sums_refs(final, where_ref, refs, 0)
    small_ref, dv_ref, ds1_ref, ds3_ref, dbl_ref, dctx_ref, grad_ref, up_ref, value_ref, seg_pad, band, corr = refs
    width = v_ref.shape[1]
    heads = head_count(width)
    half = SEQ_LEN // 2
    core = where_ref[1]

    grad_ref[0:HALF, :] = jnp.zeros((HALF, width), F32)
    grad_ref[SEQ_LEN + HALF :, :] = jnp.zeros((WINDOW - HALF, width), F32)
    value_ref[0:HALF, :] = jnp.zeros((HALF, width), BF16)
    value_ref[SEQ_LEN + HALF :, :] = jnp.zeros((WINDOW - HALF, width), BF16)
    value_ref[HALF : SEQ_LEN + HALF, :] = v_ref[...]
    for base, ref in ((core, mine_ref), (1 - core, theirs_ref)):
        for i in range(half // CHUNK):
            at = pl.ds(i * CHUNK, CHUNK)
            to = pl.multiple_of(base * half + i * CHUNK, CHUNK)
            up_ref[pl.ds(to, CHUNK), :] = ref[at, :]
            grad_ref[pl.ds(to + HALF, CHUNK), :] = mm(ref[at, :], w_out_ref[...], NT)
    at = (slice(width, 2 * width), slice(None))
    weights_ref[at] = plus(prev_ref, at, mm(att_ref[...], up_ref[...], TN))

    segment = seg_ref[0].astype(F32)
    masks = doc_masks(segment)
    first = [p1_ref[h * 8 : h * 8 + 8, :] for h in range(heads)]
    last = [p3_ref[h * 8 : h * 8 + 8, :] for h in range(heads)]
    gradient = split(grad_ref[HALF : SEQ_LEN + HALF, :])
    values = v_ref[...]

    first_wide = split(place(first, masks, heads))
    dbl = fold(mm3(first_wide, gradient), heads)
    dbl_ref[...] = dbl
    blended = split(block_diag(bl_ref[...], heads))
    dfirst = pick(mm3(blended, gradient, NT), masks, heads)
    for h in range(heads):
        ds1_ref[h * 8 : h * 8 + 8, :] = (
            SCALE * first[h] * (dfirst[h] - jnp.sum(first[h] * dfirst[h], axis=0, keepdims=True))
        )

    apply_blocks(lanes_to_rows(steps_ref[PINV_STEPS, 0], heads), dbl_ref, dctx_ref, heads, True)
    dctx = dctx_ref[...]
    dctx_wide = split(block_diag(dctx, heads))
    dlast = pick(mm(dctx_wide[0], values, NT) + mm(dctx_wide[1], values, NT), masks, heads)
    inner = jnp.sum(dctx * ctx_ref[...], axis=1, keepdims=True)
    for h in range(heads):
        ds3_ref[h * 8 : h * 8 + 8, :] = (
            SCALE * last[h] * (dlast[h] - per_doc(inner[h * 64 : (h + 1) * 64], masks))
        )
    last_wide = split(place(last, masks, heads))
    dvalue = mm3(last_wide, dctx_wide, TN)

    for h in range(heads):
        tap = split(toeplitz(taps_ref[h : h + 1, :]))
        band[h, 0] = tap[0]
        band[h, 1] = tap[1]
        corr[h] = jnp.zeros((BLOCK, WINDOW), F32)
    pad_segment(seg_pad, segment)
    lane_head = iota((BLOCK, width), 1) // HEAD_DIM
    for b in range(SEQ_LEN // BLOCK):
        begin = b * BLOCK
        same = same_document(segment, seg_pad, begin)
        window = split(grad_ref[begin : begin + WINDOW, :])
        near = value_ref[begin : begin + WINDOW, :]
        block = split(grad_ref[begin + HALF : begin + HALF + BLOCK, :])
        total = dvalue[begin : begin + BLOCK]
        for h in range(heads):
            taps = jnp.where(same, band[h, 0], 0)
            part = mm(taps, window[0]) + mm(taps, window[1]) + mm(jnp.where(same, band[h, 1], 0), window[0])
            total = total + jnp.where(lane_head == h, part, 0.0)
            mine = lane_head == h
            part = mm(jnp.where(mine, block[0], 0), near, NT) + mm(jnp.where(mine, block[1], 0), near, NT)
            corr[h] = corr[h] + jnp.where(same, part, 0.0)
        dv_ref[begin : begin + BLOCK, :] = total.astype(BF16)

    small_ref[...] = jnp.zeros(small_ref.shape, F32)
    for h in range(heads):
        at = (slice(h, h + 1), slice(None))
        small_ref[at] = plus(prev_small_ref, at, diagonal_sums(corr[h]))
    at = (slice(heads + 1, heads + 2), slice(0, width))
    small_ref[at] = plus(prev_small_ref, at, jnp.sum(dv_ref[...].astype(F32), axis=0, keepdims=True))
    at = (slice(0, width), slice(None))
    weights_ref[at] = plus(prev_ref, at, mm(dv_ref[...], tokens_ref[0], TN))
    finish()


def attend_back_queries_kernel(
    final, where_ref, tokens_ref, wq_ref, wk_ref, wv_ref, seg_ref, mark_ref,
    q_ref, k_ref, p1_ref, p3_ref, qm_ref, km_ref, ctx_ref, count_ref, mid_ref, steps_ref, dv_ref, ds1_ref, ds3_ref, dbl_ref, *refs
):
    prev_ref, prev_small_ref, weights_ref, refs, finish = sums_refs(final, where_ref, refs, 1)
    small_ref, keep_ref, send_ref, scratch, scratch_b, dqm_ref, dkm_ref, stack_ref, dq_ref, dk_ref = refs
    width = wq_ref.shape[0]
    heads = head_count(width)
    half = SEQ_LEN // 2
    core = where_ref[1]
    masks = doc_masks(seg_ref[0].astype(F32))
    pool = (mark_ref[0] == iota((LANDMARKS, SEQ_LEN), 0)).astype(BF16)
    queries = q_ref[...]
    keys = k_ref[...]
    dscore_one = split(place([ds1_ref[h * 8 : h * 8 + 8, :] for h in range(heads)], masks, heads))
    dscore_last = split(place([ds3_ref[h * 8 : h * 8 + 8, :] for h in range(heads)], masks, heads))
    dkm = fold(mm(dscore_one[0], queries) + mm(dscore_one[1], queries), heads)
    dqm = fold(mm(dscore_last[0], keys) + mm(dscore_last[1], keys), heads)

    context = unstack(ctx_ref[...], heads)
    grid = lax.dot_general(
        block_diag(dbl_ref[...], heads), jnp.concatenate([context, context], axis=0), NT,
        precision=lax.Precision.HIGHEST, preferred_element_type=F32,
    )
    dinverse = rows_to_lanes(grid, scratch, heads)
    middle = mid_ref[...]
    eye = lane_eye()

    def step(n, carry):
        dz, dmid = carry
        n = PINV_STEPS - 1 - n
        z = steps_ref[n, 0]
        product = steps_ref[n, 1]
        second = steps_ref[n, 2]
        third = steps_ref[n, 3]
        dthird = 0.25 * bm_tn(z, dz)
        dz_next = 0.25 * bm(dz, flip(third, scratch_b.at[0]))
        dsecond = -bm_tn(product, dthird)
        dprod = -bm(dthird, flip(second, scratch_b.at[1])) - bm(dsecond, flip(7.0 * eye - product, scratch_b.at[2]))
        dprod = dprod + bm_tn(product, dsecond)
        dmid = dmid + bm(dprod, flip(z, scratch_b.at[3]))
        dz_next = dz_next + bm_tn(middle, dprod)
        return dz_next, dmid

    dz, dmid = lax.fori_loop(0, PINV_STEPS, step, (dinverse, jnp.zeros((64, 128), F32)))
    columns = column_sums(middle)
    across = row_sums(middle)
    column_most = head_most(columns, heads)
    row_most = head_most(across, heads)
    start = flip(middle, scratch) / (column_most * row_most)
    dmid = dmid + flip(dz, scratch) / (column_most * row_most)
    total = jnp.sum(dz * start, axis=0, keepdims=True)
    total = head_total(jnp.where(iota((8, 128), 0) == 0, jnp.broadcast_to(total, (8, 128)), 0.0), heads)
    hit = jnp.where(columns == column_most, 1.0, 0.0)
    dcolumns = -total / column_most * hit / jnp.maximum(head_total(hit, heads), 1.0)
    hit = jnp.where(across == row_most, 1.0, 0.0)
    drows = -total / row_most * hit / jnp.maximum(head_total(hit, heads), 1.0)
    dmid = dmid + jnp.concatenate([dcolumns + drows[i : i + 1] for i in range(8)], axis=0)
    dgrid = jnp.concatenate(
        [
            SCALE * middle[i * 8 : i * 8 + 8]
            * (dmid[i * 8 : i * 8 + 8] - jnp.sum(middle[i * 8 : i * 8 + 8] * dmid[i * 8 : i * 8 + 8], axis=0, keepdims=True))
            for i in range(8)
        ],
        axis=0,
    )
    coef = lanes_to_rows(dgrid, heads)
    q_stack = stack(qm_ref[...], heads)
    k_stack = stack(km_ref[...], heads)
    stack_ref[...] = k_stack
    apply_blocks(coef, stack_ref, dqm_ref, heads, False)
    stack_ref[...] = q_stack
    apply_blocks(coef, stack_ref, dkm_ref, heads, True)

    dqm = dqm + dqm_ref[...]
    dkm = dkm + dkm_ref[...]
    counts = count_ref[:, 0:1]
    dqm = split(unstack(dqm, heads) / counts)
    dkm = split(unstack(dkm, heads) / counts)
    k_wide = split(spread(km_ref[...], heads))
    q_wide = split(spread(qm_ref[...], heads))

    def pulled(scores, wide, marks):
        left = jnp.concatenate([scores[0], pool], axis=0)
        return (
            mm(left, jnp.concatenate([wide[0], marks[0]], axis=0), TN)
            + mm(left, jnp.concatenate([wide[1], marks[1]], axis=0), TN)
            + mm(scores[1], wide[0], TN)
        )

    dq_ref[...] = pulled(dscore_one, k_wide, dqm).astype(BF16)
    dk_ref[...] = pulled(dscore_last, q_wide, dkm).astype(BF16)

    small_ref[...] = jnp.zeros(small_ref.shape, F32)
    at = (slice(heads, heads + 1), slice(0, width))
    small_ref[...] = plus(prev_small_ref, (slice(None), slice(None)), small_ref[...])
    small_ref[at] = plus(prev_small_ref, at, jnp.sum(dq_ref[...].astype(F32), axis=0, keepdims=True))
    tokens = tokens_ref[0]
    for n, ref in enumerate((dq_ref, dk_ref)):
        at = (slice(n * width, (n + 1) * width), slice(None))
        weights_ref[at] = plus(prev_ref, at, mm(ref[...], tokens, TN))
    finish()
    for base, ref in ((core, keep_ref), (1 - core, send_ref)):
        for i in range(half // CHUNK):
            at = pl.ds(pl.multiple_of(base * half + i * CHUNK, CHUNK), CHUNK)
            ref[i * CHUNK : (i + 1) * CHUNK, :] = (
                mm(dq_ref[at, :], wq_ref[...]) + mm(dk_ref[at, :], wk_ref[...]) + mm(dv_ref[at, :], wv_ref[...])
            ).astype(BF16)


def whole(shape):
    return pl.BlockSpec(shape, lambda i, w: (0,) * len(shape))


def chosen(shape):
    return pl.BlockSpec((1,) + shape, lambda i, w: (w[0],) + (0,) * len(shape))


def sums_outs(width, dim, final):
    return [((width, dim), F32), ((width, dim), BF16)] if final else [((2 * width, dim), F32)]


def back_call(kernel, where, ins, specs, outs, scratch):
    return pl.pallas_call(
        kernel,
        out_shape=[jax.ShapeDtypeStruct(s, t) for s, t in outs],
        grid_spec=pltpu.PrefetchScalarGridSpec(
            num_scalar_prefetch=1, grid=(1,), in_specs=specs, out_specs=[whole(s) for s, t in outs], scratch_shapes=scratch
        ),
        compiler_params=pltpu.CompilerParams(vmem_limit_bytes=56 << 20),
        cost_estimate=takes(0.1),
    )(where, *ins)


def attend_back_values(where, mine, theirs, tokens, taps, w_out, segments, saved, prev=()):
    dim = tokens.shape[2]
    q, k, v, att, p1, p3, qm, km, ctx, bl, count, mid, steps = saved
    width = v.shape[1]
    heads = head_count(width)
    final = len(prev) > 0
    rest = (v, att, p1, p3, ctx, bl, steps, *prev)
    specs = [
        whole(mine.shape), whole(theirs.shape), chosen((SEQ_LEN, dim)), whole(taps.shape), whole(w_out.shape), chosen((1, SEQ_LEN)),
        *[whole(x.shape) for x in rest],
    ]
    outs = [
        *sums_outs(width, dim, final), ((8, WINDOW), F32), ((SEQ_LEN, width), BF16), (p1.shape, F32), (p3.shape, F32),
        (bl.shape, F32), (ctx.shape, F32),
    ]
    scratch = [
        pltpu.VMEM((SEQ_LEN + WINDOW, width), F32),
        pltpu.VMEM((SEQ_LEN, dim), BF16),
        pltpu.VMEM((SEQ_LEN + WINDOW, width), BF16),
        pltpu.VMEM((8, SEQ_LEN + WINDOW), F32),
        pltpu.VMEM((heads, 2, BLOCK, WINDOW), BF16),
        pltpu.VMEM((heads, BLOCK, WINDOW), F32),
        *([pltpu.VMEM((2 * width, dim), F32)] if final else []),
    ]
    kernel = functools.partial(attend_back_values_kernel, final)
    return back_call(kernel, where, (mine, theirs, tokens, taps, w_out, segments, *rest), specs, outs, scratch)


def attend_back_queries(where, tokens, wq, wk, wv, segments, marks, saved, part, prev=()):
    dim = tokens.shape[2]
    q, k, v, att, p1, p3, qm, km, ctx, bl, count, mid, steps = saved
    dv, ds1, ds3, dbl = part
    width = q.shape[1]
    heads = head_count(width)
    half = SEQ_LEN // 2
    final = len(prev) > 0
    rest = (q, k, p1, p3, qm, km, ctx, count, mid, steps, dv, ds1, ds3, dbl, *prev)
    specs = [
        chosen((SEQ_LEN, dim)), *[whole(wq.shape)] * 3, chosen((1, SEQ_LEN)), chosen((1, SEQ_LEN)), *[whole(x.shape) for x in rest]
    ]
    outs = [*sums_outs(width, dim, final), ((8, WINDOW), F32), ((half, dim), BF16), ((half, dim), BF16)]
    scratch = [
        pltpu.VMEM((heads * LANDMARKS, 128), F32),
        pltpu.VMEM((4, 64, 128), F32),
        *[pltpu.VMEM((heads * LANDMARKS, HEAD_DIM), F32)] * 3,
        *[pltpu.VMEM((SEQ_LEN, width), BF16)] * 2,
        *([pltpu.VMEM((2 * width, dim), F32)] if final else []),
    ]
    kernel = functools.partial(attend_back_queries_kernel, final)
    return back_call(kernel, where, (tokens, wq, wk, wv, segments, marks, *rest), specs, outs, scratch)


ERFC = (
    0.12694266047513267, 0.12694157407364748, 0.11413597639508828, 0.08762459251766126, 0.05998263605520133,
    -0.01120062503236582, 0.07123816174906503, -0.1503297151041413, 0.09536518640917925, -0.020700440227622966,
)


def normal_cdf(value):
    size = jnp.abs(value)
    t = 1.0 / (1.0 + 0.31819805153394637 * size)
    poly = ERFC[-1]
    for coef in ERFC[-2::-1]:
        poly = poly * t + coef
    bell = jnp.exp(-0.5 * size * size)
    tail = bell * (t * poly)
    return jnp.where(value > 0.0, 1.0 - tail, tail), bell


def up_down_kernel(*refs):
    count = (len(refs) - 3) // 4
    w_up_ref, b_up_ref, w_down_ref = refs[count : count + 3]
    outs = refs[count + 3 :]
    for n in range(count):
        act_ref, slope_ref, part_ref = outs[3 * n : 3 * n + 3]
        hidden = mm(refs[n][...], w_up_ref[...]) + b_up_ref[...]
        below, bell = normal_cdf(hidden)
        act = (hidden * below).astype(BF16)
        act_ref[...] = act
        slope_ref[...] = (below + hidden * (bell * 0.3989422804014327)).astype(BF16)
        part_ref[...] = mm(act, w_down_ref[...]).astype(BF16)


def fixed(*shape):
    return pl.BlockSpec(shape, lambda i: (0,) * len(shape), pipeline_mode=pl.Buffered(1))


def strip(rows, width):
    return pl.BlockSpec((rows, width), lambda i: (i, 0))


def up_down(blocks, w_up, b_up, w_down):
    rows, dim = blocks[0].shape
    units = w_up.shape[1]
    step = 128
    total = rows * len(blocks)
    out = pl.pallas_call(
        up_down_kernel,
        out_shape=[jax.ShapeDtypeStruct((rows, w), BF16) for w in (units, units, dim)] * len(blocks),
        grid=(rows // step,),
        in_specs=[strip(step, dim)] * len(blocks) + [fixed(dim, units), fixed(1, units), fixed(units, dim)],
        out_specs=[strip(step, units), strip(step, units), strip(step, dim)] * len(blocks),
        compiler_params=pltpu.CompilerParams(vmem_limit_bytes=40 << 20),
        cost_estimate=takes(total * 0.007),
    )(*blocks, w_up, b_up, w_down)
    return [out[3 * n : 3 * n + 3] for n in range(len(blocks))]


def up_down_back_kernel(*refs):
    count = (len(refs) - 2) // 4
    w_up_ref, w_down_ref = refs[2 * count : 2 * count + 2]
    outs = refs[2 * count + 2 :]
    for n in range(count):
        grad_ref, slope_ref = refs[2 * n : 2 * n + 2]
        hidden = (mm(grad_ref[...], w_down_ref[...], NT) * slope_ref[...].astype(F32)).astype(BF16)
        outs[2 * n][...] = hidden
        outs[2 * n + 1][...] = mm(hidden, w_up_ref[...], NT).astype(BF16)


def up_down_back(pairs, w_up, w_down):
    rows, dim = pairs[0][0].shape
    units = w_up.shape[1]
    step = 128
    total = rows * len(pairs)
    out = pl.pallas_call(
        up_down_back_kernel,
        out_shape=[jax.ShapeDtypeStruct((rows, w), BF16) for w in (units, dim)] * len(pairs),
        grid=(rows // step,),
        in_specs=[strip(step, dim), strip(step, units)] * len(pairs) + [fixed(dim, units), fixed(units, dim)],
        out_specs=[strip(step, units), strip(step, dim)] * len(pairs),
        compiler_params=pltpu.CompilerParams(vmem_limit_bytes=40 << 20),
        cost_estimate=takes(total * 0.007),
    )(*[x for pair in pairs for x in pair], w_up, w_down)
    return [out[2 * n : 2 * n + 2] for n in range(len(pairs))]


def up_down_weights_kernel(final, bits_ref, *refs):
    outs = refs[-7:] if final else refs[-3:]
    ins = refs[: len(refs) - len(outs)]
    prev, ins = (ins[-3:], ins[:-3]) if final else ((), ins)
    down_ref, up_ref = outs[-2:] if final else outs[:2]
    bias_ref = outs[4] if final else outs[2]

    @pl.when(pl.program_id(0) == 0)
    def _():
        for n, ref in enumerate((down_ref, up_ref, bias_ref)):
            ref[...] = prev[n][...] if final else jnp.zeros(ref.shape, F32)

    for n in range(len(ins) // 4):
        act_ref, grad_ref, low_ref, hidden_ref = ins[4 * n : 4 * n + 4]
        hidden = hidden_ref[...]
        down_ref[...] += mm(act_ref[...], grad_ref[...], TN)
        up_ref[...] += mm(low_ref[...], hidden, TN)
        bias_ref[0:1, :] += jnp.sum(hidden.astype(F32), axis=0, keepdims=True)

    if final:

        @pl.when(pl.program_id(0) == pl.num_programs(0) - 1)
        def _():
            for n, ref in enumerate((down_ref, up_ref)):
                half = ref.shape[0] // 2
                bit = bits_ref[2 + n]
                outs[2 * n][...] = ref[pl.ds(pl.multiple_of(bit * half, half), half), :]
                outs[2 * n + 1][...] = ref[pl.ds(pl.multiple_of((1 - bit) * half, half), half), :].astype(BF16)


def up_down_weights(bits, blocks, prev=()):
    rows, units = blocks[0][0].shape
    dim = blocks[0][1].shape[1]
    step = 256
    final = len(prev) > 0
    sums = [((units, dim), F32), ((dim, units), F32)]
    outs = sums
    if final:
        outs = [o for (r, c), t in sums for o in (((r // 2, c), F32), ((r // 2, c), BF16))]
    outs = [*outs, ((8, units), F32)]

    def strips(width):
        return pl.BlockSpec((step, width), lambda i, w: (i, 0))

    def once(shape):
        return pl.BlockSpec(shape, lambda i, w: (0, 0), pipeline_mode=pl.Buffered(1))

    return pl.pallas_call(
        functools.partial(up_down_weights_kernel, final),
        out_shape=[jax.ShapeDtypeStruct(s, t) for s, t in outs],
        grid_spec=pltpu.PrefetchScalarGridSpec(
            num_scalar_prefetch=1,
            grid=(rows // step,),
            in_specs=[strips(units), strips(dim), strips(dim), strips(units)] * len(blocks) + [once(p.shape) for p in prev],
            out_specs=[once(s) for s, t in outs],
            scratch_shapes=[pltpu.VMEM(s, t) for s, t in sums] if final else [],
        ),
        compiler_params=pltpu.CompilerParams(vmem_limit_bytes=40 << 20),
        cost_estimate=takes(5),
    )(bits, *[x for block in blocks for x in block], *prev)


def swap(value, mask, axis="tensor"):
    count = lax.axis_size(axis)
    return lax.ppermute(value, axis, [(i, i ^ mask) for i in range(count)])


class Total:
    def __init__(self, kept, sent, first, axis):
        masks = [1 << n for n in range(lax.axis_size(axis).bit_length() - 1)]
        masks.insert(0, masks.pop(first))
        self.order = masks + masks[-2::-1]
        self.count = len(masks)
        self.axis = axis
        self.index = lax.axis_index(axis)
        self.kept = kept
        self.level = 0
        self.begin(sent)

    def bit(self, n):
        return ((self.index & self.order[n]) != 0).astype(jnp.int32)

    def begin(self, sent):
        self.sent = sent
        self.got = swap(sent, self.order[self.level], self.axis)
        self.level += 1

    def step(self, *others):
        got = after(self.got, *others)
        if self.level < self.count - 1:
            half = got.shape[0] // 2
            bit = self.bit(self.level)

            def rows(which):
                at = which * half
                kept = lax.dynamic_slice_in_dim(self.kept, at, half, 0)
                return kept + lax.dynamic_slice_in_dim(got, at, half, 0).astype(F32)

            sent = rows(1 - bit).astype(BF16)
            self.kept = rows(bit)
        elif self.level == self.count - 1:
            sent = self.kept = (self.kept + got.astype(F32)).astype(BF16)
        elif self.level == self.count:
            sent = self.kept = (self.kept.astype(F32) + got.astype(F32)).astype(BF16)
        else:
            bit = self.bit(self.level - 1) > 0
            sent = self.kept = jnp.concatenate([jnp.where(bit, got, self.kept), jnp.where(bit, self.kept, got)], axis=0)
        if self.level < len(self.order):
            self.begin(sent)
        return sent

    def finish(self):
        while self.level < len(self.order):
            self.step()
        return self.step()


def after(value, *others):
    return lax.optimization_barrier((value,) + others)[0]


def normalize(value):
    centered = value - jnp.mean(value, axis=-1, keepdims=True)
    inv = lax.rsqrt(jnp.mean(centered * centered, axis=-1, keepdims=True) + EPSILON)
    return centered * inv, inv


def norm_back(grad, gain, unit, inv):
    r = grad * gain
    back = (r - jnp.mean(r, axis=-1, keepdims=True) - unit * jnp.mean(r * unit, axis=-1, keepdims=True)) * inv
    return back, jnp.sum(grad * unit, axis=0), jnp.sum(grad, axis=0)


def per_device(
    tokens, w_query, w_key, w_value, b_query, b_value, conv_taps, w_out, b_out, gain_one, shift_one, w_up, b_up, w_down,
    b_down, gain_two, shift_two, cotangent, segment_ids, landmark_ids,
):
    dim = tokens.shape[1]
    width = w_query.shape[1]
    units = w_up.shape[1]
    heads = head_count(width)
    seqs = tokens.shape[0] // SEQ_LEN
    me = lax.axis_index("tensor")
    core, chip = me % 2, me // 2
    own_rows = cotangent.shape[0]
    sequences = tokens.reshape(seqs, SEQ_LEN, dim)
    segments = segment_ids.reshape(seqs, 1, SEQ_LEN)
    marks = landmark_ids.reshape(seqs, 1, SEQ_LEN)
    place_dp = lax.axis_index("dp")
    bits = [place_dp % 2, place_dp // 2 % 2]
    at_own = jnp.stack([chip, core, *bits]).astype(jnp.int32)
    at_far = jnp.stack([1 - chip, core, *bits]).astype(jnp.int32)
    taps = jnp.pad(conv_taps, ((0, 0), (0, WINDOW - CONV_TAPS)))
    taps_back = jnp.pad(conv_taps[:, ::-1], ((0, 0), (0, WINDOW - CONV_TAPS)))
    wq, wk, wv = w_query.T, w_key.T, w_value.T
    bias = b_up[None]

    def forward(at):
        return attend_forward(
            at, sequences, wq, wk, wv, b_query[None], b_value[None], taps, w_out, segments, marks
        )

    def halves(first, second):
        return jnp.concatenate([first, second], axis=0)

    far = forward(at_far)
    owed = halves(far[0] + swap(far[2], 1), far[1] + swap(far[3], 1))
    own = forward(after(at_own, owed))
    through = swap(owed, 2)
    near = halves(swap(own[2], 1), swap(own[3], 1))
    summed = halves(own[0], own[1]).astype(F32) + near.astype(F32) + through.astype(F32)
    own_tokens = lax.dynamic_slice_in_dim(tokens, me * own_rows, own_rows, 0).astype(F32)
    unit_one, inv_one = normalize(own_tokens + summed + b_out)
    normed = unit_one * gain_one + shift_one

    def feed(mine, run, meanwhile=None):
        near = swap(mine, 1)
        got = swap(mine, 2)
        here = run([mine, near], 0)
        ready = here[0][-1] if meanwhile is None else meanwhile([mine, near], here)
        got = after(got, ready)
        cross = swap(got, 1)
        there = run([got], 2)
        cross = after(cross, there[0][-1])
        there = there + run([cross], 3)
        owed = there[0][-1] + swap(there[1][-1], 1)
        blocks = [mine, near, got, cross]
        through = swap(owed, 2)
        total = here[0][-1].astype(F32) + swap(here[1][-1], 1).astype(F32) + through.astype(F32)
        return blocks, here + there, total, owed

    lows, acts, branch, _ = feed(normed.astype(BF16), lambda blocks, n: up_down(blocks, w_up, bias, w_down))
    unit_two, inv_two = normalize(normed + branch + b_down)
    output = (unit_two * gain_two + shift_two).astype(BF16)
    grad_pre_out, grad_gain_two, grad_shift_two = norm_back(cotangent.astype(F32), gain_two, unit_two, inv_two)
    grad_b_down = jnp.sum(grad_pre_out, axis=0)

    sums = []

    def weigh_own(grads, backs):
        blocks = [(acts[n][0], grads[n], lows[n], backs[n][0]) for n in range(2)]
        sums.extend(up_down_weights(at_own, blocks))
        return sums[0]

    grads, backs, back_normed, owed = feed(
        grad_pre_out.astype(BF16),
        lambda blocks, n: up_down_back([(b, acts[n + i][1]) for i, b in enumerate(blocks)], w_up, w_down),
        weigh_own,
    )
    blocks = [(acts[n][0], grads[n], lows[n], backs[n][0]) for n in (2, 3)]
    blocks[0] = (after(blocks[0][0], owed), *blocks[0][1:])
    down_kept, down_sent, up_kept, up_sent, d_bias = up_down_weights(at_own, blocks, sums)
    back_normed = after(back_normed, down_sent, up_sent)
    down = Total(down_kept, down_sent, 0, "dp")
    up = Total(up_kept, up_sent, 1, "dp")
    grad_pre_norm, grad_gain_one, grad_shift_one = norm_back(grad_pre_out + back_normed, gain_one, unit_one, inv_one)
    grad_b_out = jnp.sum(grad_pre_norm, axis=0)
    top = grad_pre_norm.astype(BF16)
    near = swap(top, 1)
    over = swap(top, 2)

    def values(at, mine, theirs, saved, prev=()):
        return attend_back_values(at, mine, theirs, sequences, taps_back, w_out, segments, saved, prev)

    def queries(at, saved, part, prev=()):
        return attend_back_queries(at, sequences, wq, wk, wv, segments, marks, saved, part, prev)

    def both(*others):
        return down.step(*others), up.step(*others)

    norms = jnp.stack([grad_gain_one, grad_shift_one, grad_b_out, grad_gain_two, grad_shift_two, grad_b_down])
    own_v = values(after(at_own, *both(top)), top, near, own[4:])
    over = after(over, own_v[0])
    own_q = queries(after(at_own, *both(own_v[0])), own[4:], own_v[2:6])
    norms = norms + after(swap(norms, 1), own_q[0])
    far_v = values(after(at_far, own_q[0]), over, swap(over, 1), far[4:], own_v[0:2])
    norms = norms + after(swap(norms, 2), far_v[0])
    one = Total(far_v[0], far_v[1], 0, "dp")
    far_q = queries(after(at_far, *both(far_v[0])), far[4:], far_v[3:7], own_q[0:2])
    two = Total(far_q[0], far_q[1], 1, "dp")
    owed = far_q[3] + swap(far_q[4], 1)
    through = swap(owed, 2)
    near = swap(own_q[3], 1)
    small = jnp.concatenate(
        [norms, d_bias[0:1], jnp.pad((far_v[2] + far_q[2])[0 : heads + 2], ((0, 0), (0, dim - WINDOW)))], axis=0
    )
    one.step(far_q[0])
    down.got, up.got, one.got, two.got = lax.optimization_barrier((down.got, up.got, one.got, two.got))
    for part in (two, one, up, down):
        part.step()
    mask = 1
    while mask < lax.axis_size("dp"):
        got = swap(small, mask, "dp")
        if mask < 8:
            got, one.got, two.got = lax.optimization_barrier((got, one.got, two.got))
            two.step()
            if mask < 4:
                one.step()
        small = small + got
        mask *= 2
    one.got, two.got, through = lax.optimization_barrier((one.got, two.got, through))
    input_grad = grad_pre_norm + own_q[2].astype(F32) + near.astype(F32) + through.astype(F32)
    value_out = one.finish().astype(F32)
    query_key = two.finish().astype(F32)
    down_sum = down.finish().astype(F32)
    up_sum = up.finish().astype(F32)

    return (
        output,
        input_grad,
        query_key[0:width].T,
        query_key[width:].T,
        value_out[0:width].T,
        small[7 + heads, 0:width],
        small[8 + heads, 0:width],
        small[7 : 7 + heads, 0:CONV_TAPS],
        value_out[width:],
        small[2],
        small[0],
        small[1],
        up_sum,
        small[6, 0:units],
        down_sum,
        small[5],
        small[3],
        small[4],
    )


def solution(mesh):
    rows = P(("dp", "tensor"), None)
    columns = P(None, "tensor")
    split_rows = P("tensor", None)
    vector = P("tensor")
    return jax.shard_map(
        per_device,
        mesh=mesh,
        in_specs=(
            P("dp", None), columns, columns, columns, vector, vector, split_rows, split_rows, P(), P(), P(),
            columns, vector, split_rows, P(), P(), P(), rows, P("dp"), P("dp"),
        ),
        out_specs=(
            rows, rows, columns, columns, columns, vector, vector, split_rows, split_rows, P(), P(), P(),
            columns, vector, split_rows, P(), P(), P(),
        ),
        check_vma=False,
    )
```

```python
import functools

import jax
import jax.numpy as jnp
from jax import lax
from jax.experimental import pallas as pl
from jax.experimental.pallas import tpu as pltpu
from jax.sharding import PartitionSpec as P

HEAD_DIM = 64
LANDMARKS = 64
CONV_TAPS = 33
PINV_STEPS = 6
DOCS = 8
PER_DOC = LANDMARKS // DOCS
SEQ_LEN = 1024
EPSILON = 1e-05
SCALE = HEAD_DIM ** -0.5
HALF = CONV_TAPS // 2
BLOCK = 128
WINDOW = 256
CHUNK = 256
F32 = jnp.float32
BF16 = jnp.bfloat16
NN = (((1,), (0,)), ((), ()))
NT = (((1,), (1,)), ((), ()))
TN = (((0,), (0,)), ((), ()))


def takes(microseconds):
    return pl.CostEstimate(flops=int(microseconds * 1.1e9), bytes_accessed=1, transcendentals=0)


def mm(left, right, dims=NN):
    return lax.dot_general(left, right, dims, preferred_element_type=F32)


def split(value):
    high = value.astype(BF16)
    return high, (value - high.astype(F32)).astype(BF16)


def mm3(left, right, dims=NN):
    lh, ll = left
    rh, rl = right
    return mm(lh, rh, dims) + mm(ll, rh, dims) + mm(lh, rl, dims)


def iota(shape, dim):
    return lax.broadcasted_iota(jnp.int32, shape, dim)


def head_count(width):
    return width // HEAD_DIM


def block_mask(heads):
    shape = (heads * LANDMARKS, heads * HEAD_DIM)
    return iota(shape, 0) // LANDMARKS == iota(shape, 1) // HEAD_DIM


def spread(rows, heads):
    return jnp.where(block_mask(heads), jnp.concatenate([rows] * heads, axis=0), 0.0)


def fold(full, heads):
    return jnp.concatenate(
        [full[h * 64 : (h + 1) * 64, h * 64 : (h + 1) * 64] for h in range(heads)], axis=0
    )


def stack(rows, heads):
    return jnp.concatenate([rows[:, h * 64 : (h + 1) * 64] for h in range(heads)], axis=0)


def unstack(rows, heads):
    return jnp.concatenate([rows[h * 64 : (h + 1) * 64] for h in range(heads)], axis=1)


def block_diag(rows, heads):
    return jnp.where(block_mask(heads), jnp.concatenate([rows] * heads, axis=1), 0.0)


def doc_masks(segment):
    return [jnp.broadcast_to(segment == d, (PER_DOC, segment.shape[1])) for d in range(DOCS)]


def pick(full, masks, heads):
    out = []
    for h in range(heads):
        kept = jnp.zeros(masks[0].shape, F32)
        for d in range(DOCS):
            row = h * LANDMARKS + d * PER_DOC
            kept = jnp.where(masks[d], full[row : row + PER_DOC], kept)
        out.append(kept)
    return out


def place(compact, masks, heads):
    return jnp.concatenate(
        [jnp.where(masks[d], compact[h], 0.0) for h in range(heads) for d in range(DOCS)], axis=0
    )


def per_doc(rows, masks):
    out = jnp.zeros(masks[0].shape, F32)
    for d in range(DOCS):
        out = jnp.where(masks[d], rows[d * PER_DOC : (d + 1) * PER_DOC], out)
    return out


def rows_to_lanes(full, scratch, heads):
    rows = heads * LANDMARKS
    lane_doc = (iota((rows, 128), 1) // PER_DOC) % DOCS
    row_doc = (iota((rows, 128), 0) // PER_DOC) % DOCS
    kept = jnp.where(lane_doc == row_doc, full, 0.0)
    for shift in (8, 16, 32):
        kept = kept + pltpu.roll(kept, shift, 1)
    scratch[0:rows, :] = kept
    count = heads * DOCS
    group = iota((count, 128), 1) // PER_DOC
    out = jnp.zeros((count, 128), F32)
    for i in range(PER_DOC):
        out = jnp.where(group == i, scratch[pl.ds(i, count, stride=PER_DOC), :], out)
    return jnp.concatenate([out, jnp.zeros((128 - count, 128), F32)], axis=0).T[0:64]


def lanes_to_rows(blocks, heads):
    full = jnp.concatenate([blocks, jnp.zeros((64, 128), F32)], axis=0).T
    return full[0 : heads * DOCS]


def apply_blocks(coef, operand_ref, result_ref, heads, transposed):
    count = heads * DOCS
    pieces = [operand_ref[pl.ds(j, count, stride=PER_DOC), :] for j in range(PER_DOC)]
    for i in range(PER_DOC):
        total = jnp.zeros(pieces[0].shape, F32)
        for j in range(PER_DOC):
            k = j * PER_DOC + i if transposed else i * PER_DOC + j
            total = total + coef[:, k : k + 1] * pieces[j]
        result_ref[pl.ds(i, count, stride=PER_DOC), :] = total


def bm(left, right):
    a = left.reshape(8, 8, -1)
    b = right.reshape(8, 8, -1)
    total = a[:, 0:1] * b[0:1]
    for k in range(1, 8):
        total = total + a[:, k : k + 1] * b[k : k + 1]
    return total.reshape(64, -1)


def bm_tn(left, right):
    rows = []
    for i in range(8):
        total = left[i : i + 1] * right[0:8]
        for k in range(1, 8):
            total = total + left[k * 8 + i : k * 8 + i + 1] * right[k * 8 : k * 8 + 8]
        rows.append(total)
    return jnp.concatenate(rows, axis=0)


def flip(blocks, scratch):
    scratch[0:64, :] = blocks
    return jnp.concatenate([scratch[pl.ds(i, 8, stride=8), :] for i in range(8)], axis=0)


def lane_eye():
    row = iota((64, 128), 0)
    return jnp.where(row // 8 == row % 8, 1.0, 0.0)


def column_sums(blocks):
    total = blocks[0:8]
    for i in range(1, 8):
        total = total + blocks[i * 8 : i * 8 + 8]
    return total


def row_sums(blocks):
    return jnp.concatenate(
        [jnp.sum(blocks[i * 8 : i * 8 + 8], axis=0, keepdims=True) for i in range(8)], axis=0
    )


def head_lanes(h):
    return iota((8, 128), 1) // DOCS == h


def head_most(sums, heads):
    out = jnp.ones((1, 128), F32)
    for h in range(heads):
        mask = head_lanes(h)
        most = jnp.max(jnp.max(jnp.where(mask, sums, -1e30), axis=1, keepdims=True), axis=0, keepdims=True)
        out = jnp.where(mask[0:1], most, out)
    return out


def head_total(values, heads):
    out = jnp.zeros((1, 128), F32)
    for h in range(heads):
        mask = head_lanes(h)
        total = jnp.sum(jnp.sum(jnp.where(mask, values, 0.0), axis=1, keepdims=True), axis=0, keepdims=True)
        out = jnp.where(mask[0:1], total, out)
    return out


def same_document(segment, seg_pad, start):
    rows = jnp.broadcast_to(segment[:, start : start + BLOCK], (BLOCK, BLOCK)).T
    return jnp.concatenate([rows, rows], axis=1) == seg_pad[0:1, start : start + WINDOW]


def toeplitz(taps_row):
    return pltpu.roll(jnp.broadcast_to(taps_row, (BLOCK, WINDOW)), 0, 1, stride=1, stride_axis=0)


def pad_segment(seg_pad, segment):
    seg_pad[:, 0:128] = jnp.zeros((8, 128), F32)
    seg_pad[:, 0:SEQ_LEN] = jnp.broadcast_to(pltpu.roll(segment, HALF, 1), (8, SEQ_LEN))
    seg_pad[:, SEQ_LEN:] = jnp.broadcast_to(segment[:, SEQ_LEN - 1 : SEQ_LEN], (8, WINDOW))


def attend_forward_kernel(
    where_ref, tokens_ref, wq_ref, wk_ref, wv_ref, bq_ref, bv_ref, taps_ref, w_out_ref, seg_ref, mark_ref,
    keep_a_ref, keep_b_ref, send_a_ref, send_b_ref, q_ref, k_ref, v_ref, att_ref, p1_ref, p3_ref, qm_ref, km_ref, ctx_ref, bl_ref, count_ref, mid_ref, steps_ref, inverse_ref,
    padded, seg_pad, scratch, band,
):
    width = wq_ref.shape[0]
    heads = head_count(width)
    tokens = tokens_ref.at[0]
    rows = 256

    def project(i, carry):
        at = pl.ds(pl.multiple_of(i * rows, rows), rows)
        x = tokens[at, :]
        q_ref[at, :] = (mm(x, wq_ref[...], NT) + bq_ref[...]).astype(BF16)
        k_ref[at, :] = mm(x, wk_ref[...], NT).astype(BF16)
        value = (mm(x, wv_ref[...], NT) + bv_ref[...]).astype(BF16)
        v_ref[at, :] = value
        padded[pl.ds(pl.multiple_of(i * rows + HALF, 16), rows), :] = value
        return carry

    padded[0:HALF, :] = jnp.zeros((HALF, width), BF16)
    padded[SEQ_LEN + HALF :, :] = jnp.zeros((WINDOW - HALF, width), BF16)
    lax.fori_loop(0, SEQ_LEN // rows, project, 0)

    segment = seg_ref[0].astype(F32)
    masks = doc_masks(segment)
    one_hot = mark_ref[0] == iota((LANDMARKS, SEQ_LEN), 0)
    counts = jnp.sum(one_hot.astype(F32), axis=1, keepdims=True)
    pool = one_hot.astype(BF16)
    q_marks = mm(pool, q_ref[...]) / counts
    k_marks = mm(pool, k_ref[...]) / counts
    count_ref[...] = jnp.broadcast_to(counts, (LANDMARKS, 128))
    qm_ref[...] = q_marks
    km_ref[...] = k_marks
    k_block = split(spread(k_marks, heads))
    q_wide = spread(q_marks, heads)
    q_block = split(q_wide)

    queries = q_ref[...]
    scores = pick(mm(k_block[0], queries, NT) + mm(k_block[1], queries, NT), masks, heads)
    first = []
    for h in range(heads):
        s = scores[h] * SCALE
        e = jnp.exp(s - jnp.max(s, axis=0, keepdims=True))
        first.append(e / jnp.sum(e, axis=0, keepdims=True))
    p1_ref[...] = jnp.concatenate(first, axis=0)

    keys = k_ref[...]
    scores = pick(mm(q_block[0], keys, NT) + mm(q_block[1], keys, NT), masks, heads)
    last = []
    for h in range(heads):
        s = scores[h] * SCALE
        most = jnp.concatenate(
            [jnp.max(jnp.where(masks[d], s, -1e30), axis=1, keepdims=True) for d in range(DOCS)], axis=0
        )
        e = jnp.exp(s - per_doc(most, masks))
        total = jnp.concatenate(
            [jnp.sum(jnp.where(masks[d], e, 0.0), axis=1, keepdims=True) for d in range(DOCS)], axis=0
        )
        last.append(e / per_doc(total, masks))
    p3_ref[...] = jnp.concatenate(last, axis=0)

    weights = split(place(last, masks, heads))
    values = v_ref[...]
    context = fold(mm(weights[0], values) + mm(weights[1], values), heads)
    ctx_ref[...] = context

    twice = jnp.concatenate([k_marks, k_marks], axis=0)
    grid = lax.dot_general(q_wide, twice, NT, precision=lax.Precision.HIGHEST, preferred_element_type=F32)
    scores = (rows_to_lanes(grid, scratch, heads) * SCALE).reshape(8, 8, 128)
    e = jnp.exp(scores - jnp.max(scores, axis=1, keepdims=True))
    middle = (e / jnp.sum(e, axis=1, keepdims=True)).reshape(64, 128)
    used = iota((64, 128), 1) < heads * DOCS
    middle = jnp.where(used, middle, 0.0)
    mid_ref[...] = middle
    norm = head_most(column_sums(middle), heads) * head_most(row_sums(middle), heads)
    eye = lane_eye()

    def step(n, inverse):
        product = bm(middle, inverse)
        second = 15.0 * eye - bm(product, 7.0 * eye - product)
        third = 13.0 * eye - bm(product, second)
        steps_ref[n, 0] = inverse
        steps_ref[n, 1] = product
        steps_ref[n, 2] = second
        steps_ref[n, 3] = third
        return 0.25 * bm(inverse, third)

    inverse = lax.fori_loop(0, PINV_STEPS, step, flip(middle, scratch) / norm)
    inverse_ref[...] = inverse
    coef = lanes_to_rows(inverse, heads)
    apply_blocks(coef, ctx_ref, bl_ref, heads, False)
    blended = split(block_diag(bl_ref[...], heads))
    weights = split(place(first, masks, heads))
    attended = mm3(weights, blended, TN)

    for h in range(heads):
        tap = split(toeplitz(taps_ref[h : h + 1, :]))
        band[h, 0] = tap[0]
        band[h, 1] = tap[1]
    pad_segment(seg_pad, segment)
    att_ref[...] = attended.astype(BF16)
    lane_head = iota((BLOCK, width), 1) // HEAD_DIM
    scratch_f = attended

    for b in range(SEQ_LEN // BLOCK):
        start = b * BLOCK
        rows_at = pl.ds(start, BLOCK)
        same = same_document(segment, seg_pad, start)
        window = padded[pl.ds(start, WINDOW), :]
        total = scratch_f[start : start + BLOCK]
        for h in range(heads):
            part = mm(jnp.where(same, band[h, 0], 0), window) + mm(jnp.where(same, band[h, 1], 0), window)
            total = total + jnp.where(lane_head == h, part, 0.0)
        att_ref[rows_at, :] = total.astype(BF16)

    half = SEQ_LEN // 2
    core = where_ref[1]
    weight = w_out_ref[...]
    for base, refs in ((core, (keep_a_ref, keep_b_ref)), (1 - core, (send_a_ref, send_b_ref))):
        for i, ref in enumerate(refs):
            at = pl.ds(pl.multiple_of(base * half + i * CHUNK, CHUNK), CHUNK)
            ref[...] = mm(att_ref[at, :], weight).astype(BF16)


def attend_forward(where, tokens, wq, wk, wv, bq, bv, taps, w_out, segments, marks):
    dim = tokens.shape[2]
    width = wq.shape[0]
    heads = head_count(width)

    def whole(*shape):
        return pl.BlockSpec(shape, lambda i, w: (0,) * len(shape))

    def one(*shape):
        return pl.BlockSpec((1,) + shape, lambda i, w: (w[0],) + (0,) * len(shape))

    outs = [
        *[((CHUNK, dim), BF16)] * 4,
        ((SEQ_LEN, width), BF16), ((SEQ_LEN, width), BF16), ((SEQ_LEN, width), BF16), ((SEQ_LEN, width), BF16),
        ((heads * 8, SEQ_LEN), F32), ((heads * 8, SEQ_LEN), F32),
        ((LANDMARKS, width), F32), ((LANDMARKS, width), F32),
        ((heads * LANDMARKS, HEAD_DIM), F32), ((heads * LANDMARKS, HEAD_DIM), F32),
        ((LANDMARKS, 128), F32), ((64, 128), F32), ((PINV_STEPS, 4, 64, 128), F32), ((64, 128), F32),
    ]
    return pl.pallas_call(
        attend_forward_kernel,
        out_shape=[jax.ShapeDtypeStruct(s, t) for s, t in outs],
        grid_spec=pltpu.PrefetchScalarGridSpec(
            num_scalar_prefetch=1,
            grid=(1,),
            in_specs=[
                one(SEQ_LEN, dim), whole(width, dim), whole(width, dim), whole(width, dim), whole(1, width), whole(1, width),
                whole(heads, WINDOW), whole(width, dim), one(1, SEQ_LEN), one(1, SEQ_LEN),
            ],
            out_specs=[whole(*s) for s, t in outs],
            scratch_shapes=[
                pltpu.VMEM((SEQ_LEN + WINDOW, width), BF16),
                pltpu.VMEM((8, SEQ_LEN + WINDOW), F32),
                pltpu.VMEM((heads * LANDMARKS, 128), F32),
                pltpu.VMEM((heads, 2, BLOCK, WINDOW), BF16),
            ],
        ),
        compiler_params=pltpu.CompilerParams(vmem_limit_bytes=56 << 20),
        cost_estimate=takes(12),
    )(where, tokens, wq, wk, wv, bq, bv, taps, w_out, segments, marks)


def diagonal_sums(band):
    row = iota(band.shape, 0)
    for bit in range(7):
        shift = 1 << bit
        moved = pltpu.roll(band, WINDOW - shift, 1)
        band = jnp.where((row // shift) % 2 == 1, moved, band)
    return jnp.sum(band, axis=0, keepdims=True)


def plus(ref, at, value):
    return value if ref is None else ref[at] + value


def sums_refs(final, where_ref, refs, turn):
    if not final:
        weights_ref, *refs = refs
        return None, None, weights_ref, refs, lambda: None
    prev_ref, prev_small_ref, kept_ref, sent_ref, *refs = refs
    *refs, weights_ref = refs

    def finish():
        half = kept_ref.shape[0]
        bit = where_ref[2 + turn]
        kept_ref[...] = weights_ref[pl.ds(pl.multiple_of(bit * half, half), half), :]
        sent_ref[...] = weights_ref[pl.ds(pl.multiple_of((1 - bit) * half, half), half), :].astype(BF16)

    return prev_ref, prev_small_ref, weights_ref, refs, finish


def attend_back_values_kernel(
    final, where_ref, mine_ref, theirs_ref, tokens_ref, taps_ref, w_out_ref, seg_ref,
    v_ref, att_ref, p1_ref, p3_ref, ctx_ref, bl_ref, inverse_ref, *refs
):
    prev_ref, prev_small_ref, weights_ref, refs, finish = sums_refs(final, where_ref, refs, 0)
    small_ref, dv_ref, ds1_ref, ds3_ref, dbl_ref, dctx_ref, grad_ref, up_ref, value_ref, seg_pad, band, corr = refs
    width = v_ref.shape[1]
    heads = head_count(width)
    half = SEQ_LEN // 2
    core = where_ref[1]

    grad_ref[0:HALF, :] = jnp.zeros((HALF, width), F32)
    grad_ref[SEQ_LEN + HALF :, :] = jnp.zeros((WINDOW - HALF, width), F32)
    value_ref[0:HALF, :] = jnp.zeros((HALF, width), BF16)
    value_ref[SEQ_LEN + HALF :, :] = jnp.zeros((WINDOW - HALF, width), BF16)
    value_ref[HALF : SEQ_LEN + HALF, :] = v_ref[...]
    for base, ref in ((core, mine_ref), (1 - core, theirs_ref)):
        for i in range(half // CHUNK):
            at = pl.ds(i * CHUNK, CHUNK)
            to = pl.multiple_of(base * half + i * CHUNK, CHUNK)
            up_ref[pl.ds(to, CHUNK), :] = ref[at, :]
            grad_ref[pl.ds(to + HALF, CHUNK), :] = mm(ref[at, :], w_out_ref[...], NT)
    at = (slice(width, 2 * width), slice(None))
    weights_ref[at] = plus(prev_ref, at, mm(att_ref[...], up_ref[...], TN))

    segment = seg_ref[0].astype(F32)
    masks = doc_masks(segment)
    first = [p1_ref[h * 8 : h * 8 + 8, :] for h in range(heads)]
    last = [p3_ref[h * 8 : h * 8 + 8, :] for h in range(heads)]
    gradient = split(grad_ref[HALF : SEQ_LEN + HALF, :])
    values = v_ref[...]

    first_wide = split(place(first, masks, heads))
    dbl = fold(mm3(first_wide, gradient), heads)
    dbl_ref[...] = dbl
    blended = split(block_diag(bl_ref[...], heads))
    dfirst = pick(mm3(blended, gradient, NT), masks, heads)
    for h in range(heads):
        ds1_ref[h * 8 : h * 8 + 8, :] = (
            SCALE * first[h] * (dfirst[h] - jnp.sum(first[h] * dfirst[h], axis=0, keepdims=True))
        )

    apply_blocks(lanes_to_rows(inverse_ref[...], heads), dbl_ref, dctx_ref, heads, True)
    dctx = dctx_ref[...]
    dctx_wide = split(block_diag(dctx, heads))
    dlast = pick(mm(dctx_wide[0], values, NT) + mm(dctx_wide[1], values, NT), masks, heads)
    inner = jnp.sum(dctx * ctx_ref[...], axis=1, keepdims=True)
    for h in range(heads):
        ds3_ref[h * 8 : h * 8 + 8, :] = (
            SCALE * last[h] * (dlast[h] - per_doc(inner[h * 64 : (h + 1) * 64], masks))
        )
    last_wide = split(place(last, masks, heads))
    dvalue = mm3(last_wide, dctx_wide, TN)

    for h in range(heads):
        tap = split(toeplitz(taps_ref[h : h + 1, :]))
        band[h, 0] = tap[0]
        band[h, 1] = tap[1]
        corr[h] = jnp.zeros((BLOCK, WINDOW), F32)
    pad_segment(seg_pad, segment)
    lane_head = iota((BLOCK, width), 1) // HEAD_DIM
    for b in range(SEQ_LEN // BLOCK):
        begin = b * BLOCK
        same = same_document(segment, seg_pad, begin)
        window = split(grad_ref[begin : begin + WINDOW, :])
        near = value_ref[begin : begin + WINDOW, :]
        block = split(grad_ref[begin + HALF : begin + HALF + BLOCK, :])
        total = dvalue[begin : begin + BLOCK]
        for h in range(heads):
            taps = jnp.where(same, band[h, 0], 0)
            part = mm(taps, window[0]) + mm(taps, window[1]) + mm(jnp.where(same, band[h, 1], 0), window[0])
            total = total + jnp.where(lane_head == h, part, 0.0)
            mine = lane_head == h
            part = mm(jnp.where(mine, block[0], 0), near, NT) + mm(jnp.where(mine, block[1], 0), near, NT)
            corr[h] = corr[h] + jnp.where(same, part, 0.0)
        dv_ref[begin : begin + BLOCK, :] = total.astype(BF16)

    small_ref[...] = jnp.zeros(small_ref.shape, F32)
    for h in range(heads):
        at = (slice(h, h + 1), slice(None))
        small_ref[at] = plus(prev_small_ref, at, diagonal_sums(corr[h]))
    at = (slice(heads + 1, heads + 2), slice(0, width))
    small_ref[at] = plus(prev_small_ref, at, jnp.sum(dv_ref[...].astype(F32), axis=0, keepdims=True))
    at = (slice(0, width), slice(None))
    weights_ref[at] = plus(prev_ref, at, mm(dv_ref[...], tokens_ref[0], TN))
    finish()


def attend_back_queries_kernel(
    final, where_ref, tokens_ref, seg_ref, mark_ref,
    q_ref, k_ref, qm_ref, km_ref, ctx_ref, count_ref, mid_ref, steps_ref, ds1_ref, ds3_ref, dbl_ref, *refs
):
    prev_ref, prev_small_ref, weights_ref, refs, finish = sums_refs(final, where_ref, refs, 1)
    small_ref, dq_ref, dk_ref, scratch, scratch_b, dqm_ref, dkm_ref, stack_ref = refs
    width = q_ref.shape[1]
    heads = head_count(width)
    masks = doc_masks(seg_ref[0].astype(F32))
    pool = (mark_ref[0] == iota((LANDMARKS, SEQ_LEN), 0)).astype(BF16)
    queries = q_ref[...]
    keys = k_ref[...]
    dscore_one = split(place([ds1_ref[h * 8 : h * 8 + 8, :] for h in range(heads)], masks, heads))
    dscore_last = split(place([ds3_ref[h * 8 : h * 8 + 8, :] for h in range(heads)], masks, heads))
    dkm = fold(mm(dscore_one[0], queries) + mm(dscore_one[1], queries), heads)
    dqm = fold(mm(dscore_last[0], keys) + mm(dscore_last[1], keys), heads)

    context = unstack(ctx_ref[...], heads)
    grid = lax.dot_general(
        block_diag(dbl_ref[...], heads), jnp.concatenate([context, context], axis=0), NT,
        precision=lax.Precision.HIGHEST, preferred_element_type=F32,
    )
    dinverse = rows_to_lanes(grid, scratch, heads)
    middle = mid_ref[...]
    eye = lane_eye()

    def step(n, carry):
        dz, dmid = carry
        n = PINV_STEPS - 1 - n
        z = steps_ref[n, 0]
        product = steps_ref[n, 1]
        second = steps_ref[n, 2]
        third = steps_ref[n, 3]
        dthird = 0.25 * bm_tn(z, dz)
        dz_next = 0.25 * bm(dz, flip(third, scratch_b.at[0]))
        dsecond = -bm_tn(product, dthird)
        dprod = -bm(dthird, flip(second, scratch_b.at[1])) - bm(dsecond, flip(7.0 * eye - product, scratch_b.at[2]))
        dprod = dprod + bm_tn(product, dsecond)
        dmid = dmid + bm(dprod, flip(z, scratch_b.at[3]))
        dz_next = dz_next + bm_tn(middle, dprod)
        return dz_next, dmid

    dz, dmid = lax.fori_loop(0, PINV_STEPS, step, (dinverse, jnp.zeros((64, 128), F32)))
    columns = column_sums(middle)
    across = row_sums(middle)
    column_most = head_most(columns, heads)
    row_most = head_most(across, heads)
    start = flip(middle, scratch) / (column_most * row_most)
    dmid = dmid + flip(dz, scratch) / (column_most * row_most)
    total = jnp.sum(dz * start, axis=0, keepdims=True)
    total = head_total(jnp.where(iota((8, 128), 0) == 0, jnp.broadcast_to(total, (8, 128)), 0.0), heads)
    hit = jnp.where(columns == column_most, 1.0, 0.0)
    dcolumns = -total / column_most * hit / jnp.maximum(head_total(hit, heads), 1.0)
    hit = jnp.where(across == row_most, 1.0, 0.0)
    drows = -total / row_most * hit / jnp.maximum(head_total(hit, heads), 1.0)
    dmid = dmid + jnp.concatenate([dcolumns + drows[i : i + 1] for i in range(8)], axis=0)
    dgrid = jnp.concatenate(
        [
            SCALE * middle[i * 8 : i * 8 + 8]
            * (dmid[i * 8 : i * 8 + 8] - jnp.sum(middle[i * 8 : i * 8 + 8] * dmid[i * 8 : i * 8 + 8], axis=0, keepdims=True))
            for i in range(8)
        ],
        axis=0,
    )
    coef = lanes_to_rows(dgrid, heads)
    q_stack = stack(qm_ref[...], heads)
    k_stack = stack(km_ref[...], heads)
    stack_ref[...] = k_stack
    apply_blocks(coef, stack_ref, dqm_ref, heads, False)
    stack_ref[...] = q_stack
    apply_blocks(coef, stack_ref, dkm_ref, heads, True)

    dqm = dqm + dqm_ref[...]
    dkm = dkm + dkm_ref[...]
    counts = count_ref[:, 0:1]
    dqm = split(unstack(dqm, heads) / counts)
    dkm = split(unstack(dkm, heads) / counts)
    k_wide = split(spread(km_ref[...], heads))
    q_wide = split(spread(qm_ref[...], heads))

    def pulled(scores, wide, marks):
        left = jnp.concatenate([scores[0], pool], axis=0)
        return (
            mm(left, jnp.concatenate([wide[0], marks[0]], axis=0), TN)
            + mm(left, jnp.concatenate([wide[1], marks[1]], axis=0), TN)
            + mm(scores[1], wide[0], TN)
        )

    dq_ref[...] = pulled(dscore_one, k_wide, dqm).astype(BF16)
    dk_ref[...] = pulled(dscore_last, q_wide, dkm).astype(BF16)

    small_ref[...] = jnp.zeros(small_ref.shape, F32)
    at = (slice(heads, heads + 1), slice(0, width))
    small_ref[...] = plus(prev_small_ref, (slice(None), slice(None)), small_ref[...])
    small_ref[at] = plus(prev_small_ref, at, jnp.sum(dq_ref[...].astype(F32), axis=0, keepdims=True))
    tokens = tokens_ref[0]
    for n, ref in enumerate((dq_ref, dk_ref)):
        at = (slice(n * width, (n + 1) * width), slice(None))
        weights_ref[at] = plus(prev_ref, at, mm(ref[...], tokens, TN))
    finish()


def attend_back_tokens_kernel(where_ref, *refs):
    ins, weights, outs = refs[:6], [ref[...] for ref in refs[6:9]], refs[9:]
    for n in range(2):
        outs[n][...] = sum(mm(ref[...], w) for ref, w in zip(ins[3 * n : 3 * n + 3], weights)).astype(BF16)


def attend_back_tokens(where, parts, weights):
    width, dim = weights[0].shape
    step = 256
    count = SEQ_LEN // 2 // step

    def rows(near):
        def at(i, w):
            return ((w[1] if near else 1 - w[1]) * count + i, 0)

        return pl.BlockSpec((step, width), at)

    return pl.pallas_call(
        attend_back_tokens_kernel,
        out_shape=[jax.ShapeDtypeStruct((SEQ_LEN // 2, dim), BF16)] * 2,
        grid_spec=pltpu.PrefetchScalarGridSpec(
            num_scalar_prefetch=1,
            grid=(count,),
            in_specs=[rows(True)] * 3 + [rows(False)] * 3 + [pl.BlockSpec((width, dim), lambda i, w: (0, 0))] * 3,
            out_specs=[pl.BlockSpec((step, dim), lambda i, w: (i, 0))] * 2,
        ),
        compiler_params=pltpu.CompilerParams(vmem_limit_bytes=40 << 20),
        cost_estimate=takes(3),
    )(where, *parts, *parts, *weights)


def whole(shape):
    return pl.BlockSpec(shape, lambda i, w: (0,) * len(shape))


def chosen(shape):
    return pl.BlockSpec((1,) + shape, lambda i, w: (w[0],) + (0,) * len(shape))


def sums_outs(width, dim, final):
    return [((width, dim), F32), ((width, dim), BF16)] if final else [((2 * width, dim), F32)]


def back_call(kernel, where, ins, specs, outs, scratch, final):
    return pl.pallas_call(
        kernel,
        out_shape=[jax.ShapeDtypeStruct(s, t) for s, t in outs],
        grid_spec=pltpu.PrefetchScalarGridSpec(
            num_scalar_prefetch=1, grid=(1,), in_specs=specs, out_specs=[whole(s) for s, t in outs], scratch_shapes=scratch
        ),
        compiler_params=pltpu.CompilerParams(vmem_limit_bytes=56 << 20),
        cost_estimate=takes(0.1 if final else 11),
    )(where, *ins)


def attend_back_values(where, mine, theirs, tokens, taps, w_out, segments, saved, prev=()):
    dim = tokens.shape[2]
    q, k, v, att, p1, p3, qm, km, ctx, bl, count, mid, steps, inverse = saved
    width = v.shape[1]
    heads = head_count(width)
    final = len(prev) > 0
    rest = (v, att, p1, p3, ctx, bl, inverse, *prev)
    specs = [
        whole(mine.shape), whole(theirs.shape), chosen((SEQ_LEN, dim)), whole(taps.shape), whole(w_out.shape), chosen((1, SEQ_LEN)),
        *[whole(x.shape) for x in rest],
    ]
    outs = [
        *sums_outs(width, dim, final), ((8, WINDOW), F32), ((SEQ_LEN, width), BF16), (p1.shape, F32), (p3.shape, F32),
        (bl.shape, F32), (ctx.shape, F32),
    ]
    scratch = [
        pltpu.VMEM((SEQ_LEN + WINDOW, width), F32),
        pltpu.VMEM((SEQ_LEN, dim), BF16),
        pltpu.VMEM((SEQ_LEN + WINDOW, width), BF16),
        pltpu.VMEM((8, SEQ_LEN + WINDOW), F32),
        pltpu.VMEM((heads, 2, BLOCK, WINDOW), BF16),
        pltpu.VMEM((heads, BLOCK, WINDOW), F32),
        *([pltpu.VMEM((2 * width, dim), F32)] if final else []),
    ]
    kernel = functools.partial(attend_back_values_kernel, final)
    return back_call(kernel, where, (mine, theirs, tokens, taps, w_out, segments, *rest), specs, outs, scratch, final)


def attend_back_queries(where, tokens, segments, marks, saved, part, prev=()):
    dim = tokens.shape[2]
    q, k, v, att, p1, p3, qm, km, ctx, bl, count, mid, steps, inverse = saved
    ds1, ds3, dbl = part
    width = q.shape[1]
    heads = head_count(width)
    final = len(prev) > 0
    rest = (q, k, qm, km, ctx, count, mid, steps, ds1, ds3, dbl, *prev)
    specs = [chosen((SEQ_LEN, dim)), chosen((1, SEQ_LEN)), chosen((1, SEQ_LEN)), *[whole(x.shape) for x in rest]]
    outs = [*sums_outs(width, dim, final), ((8, WINDOW), F32), ((SEQ_LEN, width), BF16), ((SEQ_LEN, width), BF16)]
    scratch = [
        pltpu.VMEM((heads * LANDMARKS, 128), F32),
        pltpu.VMEM((4, 64, 128), F32),
        *[pltpu.VMEM((heads * LANDMARKS, HEAD_DIM), F32)] * 3,
        *([pltpu.VMEM((2 * width, dim), F32)] if final else []),
    ]
    kernel = functools.partial(attend_back_queries_kernel, final)
    return back_call(kernel, where, (tokens, segments, marks, *rest), specs, outs, scratch, final)


ERFC = (
    0.12694266047513267, 0.12694157407364748, 0.11413597639508828, 0.08762459251766126, 0.05998263605520133,
    -0.01120062503236582, 0.07123816174906503, -0.1503297151041413, 0.09536518640917925, -0.020700440227622966,
)


def normal_cdf(value):
    size = jnp.abs(value)
    t = 1.0 / (1.0 + 0.31819805153394637 * size)
    poly = ERFC[-1]
    for coef in ERFC[-2::-1]:
        poly = poly * t + coef
    bell = jnp.exp(-0.5 * size * size)
    tail = bell * (t * poly)
    return jnp.where(value > 0.0, 1.0 - tail, tail), bell


def up_down_kernel(*refs):
    count = (len(refs) - 3) // 4
    w_up_ref, b_up_ref, w_down_ref = refs[count : count + 3]
    outs = refs[count + 3 :]
    for n in range(count):
        act_ref, slope_ref, part_ref = outs[3 * n : 3 * n + 3]
        hidden = mm(refs[n][...], w_up_ref[...]) + b_up_ref[...]
        below, bell = normal_cdf(hidden)
        act = (hidden * below).astype(BF16)
        act_ref[...] = act
        slope_ref[...] = (below + hidden * (bell * 0.3989422804014327)).astype(BF16)
        part_ref[...] = mm(act, w_down_ref[...]).astype(BF16)


def fixed(*shape):
    return pl.BlockSpec(shape, lambda i: (0,) * len(shape), pipeline_mode=pl.Buffered(1))


def strip(rows, width):
    return pl.BlockSpec((rows, width), lambda i: (i, 0))


def up_down(blocks, w_up, b_up, w_down):
    rows, dim = blocks[0].shape
    units = w_up.shape[1]
    step = 128
    total = rows * len(blocks)
    out = pl.pallas_call(
        up_down_kernel,
        out_shape=[jax.ShapeDtypeStruct((rows, w), BF16) for w in (units, units, dim)] * len(blocks),
        grid=(rows // step,),
        in_specs=[strip(step, dim)] * len(blocks) + [fixed(dim, units), fixed(1, units), fixed(units, dim)],
        out_specs=[strip(step, units), strip(step, units), strip(step, dim)] * len(blocks),
        compiler_params=pltpu.CompilerParams(vmem_limit_bytes=40 << 20),
        cost_estimate=takes(total * 0.007),
    )(*blocks, w_up, b_up, w_down)
    return [out[3 * n : 3 * n + 3] for n in range(len(blocks))]


def up_down_back_kernel(*refs):
    count = (len(refs) - 2) // 4
    w_up_ref, w_down_ref = refs[2 * count : 2 * count + 2]
    outs = refs[2 * count + 2 :]
    for n in range(count):
        grad_ref, slope_ref = refs[2 * n : 2 * n + 2]
        hidden = (mm(grad_ref[...], w_down_ref[...], NT) * slope_ref[...].astype(F32)).astype(BF16)
        outs[2 * n][...] = hidden
        outs[2 * n + 1][...] = mm(hidden, w_up_ref[...], NT).astype(BF16)


def up_down_back(pairs, w_up, w_down):
    rows, dim = pairs[0][0].shape
    units = w_up.shape[1]
    step = 128
    total = rows * len(pairs)
    out = pl.pallas_call(
        up_down_back_kernel,
        out_shape=[jax.ShapeDtypeStruct((rows, w), BF16) for w in (units, dim)] * len(pairs),
        grid=(rows // step,),
        in_specs=[strip(step, dim), strip(step, units)] * len(pairs) + [fixed(dim, units), fixed(units, dim)],
        out_specs=[strip(step, units), strip(step, dim)] * len(pairs),
        compiler_params=pltpu.CompilerParams(vmem_limit_bytes=40 << 20),
        cost_estimate=takes(total * 0.007),
    )(*[x for pair in pairs for x in pair], w_up, w_down)
    return [out[2 * n : 2 * n + 2] for n in range(len(pairs))]


def up_down_weights_kernel(final, bits_ref, *refs):
    outs = refs[-7:] if final else refs[-3:]
    ins = refs[: len(refs) - len(outs)]
    prev, ins = (ins[-3:], ins[:-3]) if final else ((), ins)
    down_ref, up_ref = outs[-2:] if final else outs[:2]
    bias_ref = outs[4] if final else outs[2]

    @pl.when(pl.program_id(0) == 0)
    def _():
        for n, ref in enumerate((down_ref, up_ref, bias_ref)):
            ref[...] = prev[n][...] if final else jnp.zeros(ref.shape, F32)

    for n in range(len(ins) // 4):
        act_ref, grad_ref, low_ref, hidden_ref = ins[4 * n : 4 * n + 4]
        hidden = hidden_ref[...]
        down_ref[...] += mm(act_ref[...], grad_ref[...], TN)
        up_ref[...] += mm(low_ref[...], hidden, TN)
        bias_ref[0:1, :] += jnp.sum(hidden.astype(F32), axis=0, keepdims=True)

    if final:

        @pl.when(pl.program_id(0) == pl.num_programs(0) - 1)
        def _():
            for n, ref in enumerate((down_ref, up_ref)):
                half = ref.shape[0] // 2
                bit = bits_ref[2 + n]
                outs[2 * n][...] = ref[pl.ds(pl.multiple_of(bit * half, half), half), :]
                outs[2 * n + 1][...] = ref[pl.ds(pl.multiple_of((1 - bit) * half, half), half), :].astype(BF16)


def up_down_weights(bits, blocks, prev=()):
    rows, units = blocks[0][0].shape
    dim = blocks[0][1].shape[1]
    step = 256
    final = len(prev) > 0
    sums = [((units, dim), F32), ((dim, units), F32)]
    outs = sums
    if final:
        outs = [o for (r, c), t in sums for o in (((r // 2, c), F32), ((r // 2, c), BF16))]
    outs = [*outs, ((8, units), F32)]

    def strips(width):
        return pl.BlockSpec((step, width), lambda i, w: (i, 0))

    def once(shape):
        return pl.BlockSpec(shape, lambda i, w: (0, 0), pipeline_mode=pl.Buffered(1))

    return pl.pallas_call(
        functools.partial(up_down_weights_kernel, final),
        out_shape=[jax.ShapeDtypeStruct(s, t) for s, t in outs],
        grid_spec=pltpu.PrefetchScalarGridSpec(
            num_scalar_prefetch=1,
            grid=(rows // step,),
            in_specs=[strips(units), strips(dim), strips(dim), strips(units)] * len(blocks) + [once(p.shape) for p in prev],
            out_specs=[once(s) for s, t in outs],
            scratch_shapes=[pltpu.VMEM(s, t) for s, t in sums] if final else [],
        ),
        compiler_params=pltpu.CompilerParams(vmem_limit_bytes=40 << 20),
        cost_estimate=takes(5),
    )(bits, *[x for block in blocks for x in block], *prev)


def swap(value, mask, axis="tensor"):
    count = lax.axis_size(axis)
    return lax.ppermute(value, axis, [(i, i ^ mask) for i in range(count)])


class Total:
    def __init__(self, kept, sent, first, axis):
        masks = [1 << n for n in range(lax.axis_size(axis).bit_length() - 1)]
        masks.insert(0, masks.pop(first))
        self.order = masks + masks[-2::-1]
        self.count = len(masks)
        self.axis = axis
        self.index = lax.axis_index(axis)
        self.kept = kept
        self.level = 0
        self.begin(sent)

    def bit(self, n):
        return ((self.index & self.order[n]) != 0).astype(jnp.int32)

    def begin(self, sent):
        self.sent = sent
        self.got = swap(sent, self.order[self.level], self.axis)
        self.level += 1

    def step(self, *others):
        got = after(self.got, *others)
        if self.level < self.count - 1:
            half = got.shape[0] // 2
            bit = self.bit(self.level)

            def rows(which):
                at = which * half
                kept = lax.dynamic_slice_in_dim(self.kept, at, half, 0)
                return kept + lax.dynamic_slice_in_dim(got, at, half, 0).astype(F32)

            sent = rows(1 - bit).astype(BF16)
            self.kept = rows(bit)
        elif self.level == self.count - 1:
            sent = self.kept = (self.kept + got.astype(F32)).astype(BF16)
        elif self.level == self.count:
            sent = self.kept = (self.kept.astype(F32) + got.astype(F32)).astype(BF16)
        else:
            bit = self.bit(self.level - 1) > 0
            sent = self.kept = jnp.concatenate([jnp.where(bit, got, self.kept), jnp.where(bit, self.kept, got)], axis=0)
        if self.level < len(self.order):
            self.begin(sent)
        return sent

    def finish(self):
        while self.level < len(self.order):
            self.step()
        return self.step()


def after(value, *others):
    return lax.optimization_barrier((value,) + others)[0]


def normalize(value):
    centered = value - jnp.mean(value, axis=-1, keepdims=True)
    inv = lax.rsqrt(jnp.mean(centered * centered, axis=-1, keepdims=True) + EPSILON)
    return centered * inv, inv


def norm_back(grad, gain, unit, inv):
    r = grad * gain
    back = (r - jnp.mean(r, axis=-1, keepdims=True) - unit * jnp.mean(r * unit, axis=-1, keepdims=True)) * inv
    return back, jnp.sum(grad * unit, axis=0), jnp.sum(grad, axis=0)


def per_device(
    tokens, w_query, w_key, w_value, b_query, b_value, conv_taps, w_out, b_out, gain_one, shift_one, w_up, b_up, w_down,
    b_down, gain_two, shift_two, cotangent, segment_ids, landmark_ids,
):
    dim = tokens.shape[1]
    width = w_query.shape[1]
    units = w_up.shape[1]
    heads = head_count(width)
    seqs = tokens.shape[0] // SEQ_LEN
    me = lax.axis_index("tensor")
    core, chip = me % 2, me // 2
    own_rows = cotangent.shape[0]
    sequences = tokens.reshape(seqs, SEQ_LEN, dim)
    segments = segment_ids.reshape(seqs, 1, SEQ_LEN)
    marks = landmark_ids.reshape(seqs, 1, SEQ_LEN)
    place_dp = lax.axis_index("dp")
    bits = [place_dp % 2, place_dp // 2 % 2]
    at_own = jnp.stack([chip, core, *bits]).astype(jnp.int32)
    at_far = jnp.stack([1 - chip, core, *bits]).astype(jnp.int32)
    taps = jnp.pad(conv_taps, ((0, 0), (0, WINDOW - CONV_TAPS)))
    taps_back = jnp.pad(conv_taps[:, ::-1], ((0, 0), (0, WINDOW - CONV_TAPS)))
    wq, wk, wv = w_query.T, w_key.T, w_value.T
    bias = b_up[None]

    def forward(at):
        return attend_forward(
            at, sequences, wq, wk, wv, b_query[None], b_value[None], taps, w_out, segments, marks
        )

    def halves(first, second):
        return jnp.concatenate([first, second], axis=0)

    far = forward(at_far)
    owed = halves(far[0] + swap(far[2], 1), far[1] + swap(far[3], 1))
    own = forward(after(at_own, owed))
    through = swap(owed, 2)
    near = halves(swap(own[2], 1), swap(own[3], 1))
    summed = halves(own[0], own[1]).astype(F32) + near.astype(F32) + through.astype(F32)
    own_tokens = lax.dynamic_slice_in_dim(tokens, me * own_rows, own_rows, 0).astype(F32)
    unit_one, inv_one = normalize(own_tokens + summed + b_out)
    normed = unit_one * gain_one + shift_one

    def feed(mine, run, meanwhile=None):
        near = swap(mine, 1)
        got = swap(mine, 2)
        here = run([mine, near], 0)
        ready = here[0][-1] if meanwhile is None else meanwhile([mine, near], here)
        got = after(got, ready)
        cross = swap(got, 1)
        there = run([got], 2)
        cross = after(cross, there[0][-1])
        there = there + run([cross], 3)
        owed = there[0][-1] + swap(there[1][-1], 1)
        blocks = [mine, near, got, cross]
        through = swap(owed, 2)
        total = here[0][-1].astype(F32) + swap(here[1][-1], 1).astype(F32) + through.astype(F32)
        return blocks, here + there, total, owed

    lows, acts, branch, _ = feed(normed.astype(BF16), lambda blocks, n: up_down(blocks, w_up, bias, w_down))
    unit_two, inv_two = normalize(normed + branch + b_down)
    output = (unit_two * gain_two + shift_two).astype(BF16)
    grad_pre_out, grad_gain_two, grad_shift_two = norm_back(cotangent.astype(F32), gain_two, unit_two, inv_two)
    grad_b_down = jnp.sum(grad_pre_out, axis=0)

    sums = []

    def weigh_own(grads, backs):
        blocks = [(acts[n][0], grads[n], lows[n], backs[n][0]) for n in range(2)]
        sums.extend(up_down_weights(at_own, blocks))
        return sums[0]

    grads, backs, back_normed, owed = feed(
        grad_pre_out.astype(BF16),
        lambda blocks, n: up_down_back([(b, acts[n + i][1]) for i, b in enumerate(blocks)], w_up, w_down),
        weigh_own,
    )
    blocks = [(acts[n][0], grads[n], lows[n], backs[n][0]) for n in (2, 3)]
    blocks[0] = (after(blocks[0][0], owed), *blocks[0][1:])
    down_kept, down_sent, up_kept, up_sent, d_bias = up_down_weights(at_own, blocks, sums)
    back_normed = after(back_normed, down_sent, up_sent)
    down = Total(down_kept, down_sent, 0, "dp")
    up = Total(up_kept, up_sent, 1, "dp")
    grad_pre_norm, grad_gain_one, grad_shift_one = norm_back(grad_pre_out + back_normed, gain_one, unit_one, inv_one)
    grad_b_out = jnp.sum(grad_pre_norm, axis=0)
    top = grad_pre_norm.astype(BF16)
    near = swap(top, 1)
    over = swap(top, 2)

    def values(at, mine, theirs, saved, prev=()):
        return attend_back_values(at, mine, theirs, sequences, taps_back, w_out, segments, saved, prev)

    def queries(at, saved, part, prev=()):
        return attend_back_queries(at, sequences, segments, marks, saved, part, prev)

    def both(*others):
        return down.step(*others), up.step(*others)

    norms = jnp.stack([grad_gain_one, grad_shift_one, grad_b_out, grad_gain_two, grad_shift_two, grad_b_down])
    own_v = values(after(at_own, *both(top)), top, near, own[4:])
    own_q = queries(after(at_own, *both(own_v[0])), own[4:], own_v[3:6])
    norms = norms + after(swap(norms, 1), own_q[0])
    far_v = values(after(at_far, own_q[0]), over, swap(over, 1), far[4:], own_v[0:2])
    norms = norms + after(swap(norms, 2), far_v[0])
    one = Total(far_v[0], far_v[1], 0, "dp")
    far_q = queries(after(at_far, *both(far_v[0])), far[4:], far_v[4:7], own_q[0:2])
    two = Total(far_q[0], far_q[1], 1, "dp")
    far_x = attend_back_tokens(at_far, (far_q[3], far_q[4], far_v[3]), (wq, wk, wv))
    owed = far_x[0] + swap(far_x[1], 1)
    through = swap(owed, 2)
    own_x = attend_back_tokens(at_own, (after(own_q[2], owed), own_q[3], own_v[2]), (wq, wk, wv))
    near = swap(own_x[1], 1)
    small = jnp.concatenate(
        [norms, d_bias[0:1], jnp.pad((far_v[2] + far_q[2])[0 : heads + 2], ((0, 0), (0, dim - WINDOW)))], axis=0
    )
    one.step(far_q[0])
    down.got, up.got, one.got, two.got = lax.optimization_barrier((down.got, up.got, one.got, two.got))
    for part in (two, one, up, down):
        part.step()
    mask = 1
    while mask < lax.axis_size("dp"):
        got = swap(small, mask, "dp")
        if mask == 1:
            got, one.got, two.got = lax.optimization_barrier((got, one.got, two.got))
            two.step()
            one.step()
            down.got, up.got, two.got = lax.optimization_barrier((down.got, up.got, two.got))
        elif mask == 2:
            got, one.got, two.got = lax.optimization_barrier((got, one.got, two.got))
            two.step()
            one.step()
        elif mask == 4:
            got, one.got, two.got, through = lax.optimization_barrier((got, one.got, two.got, through))
            two.step()
        small = small + got
        mask *= 2
    input_grad = grad_pre_norm + own_x[0].astype(F32) + near.astype(F32) + through.astype(F32)
    value_out = one.finish().astype(F32)
    query_key = two.finish().astype(F32)
    down_sum = down.finish().astype(F32)
    up_sum = up.finish().astype(F32)

    return (
        output,
        input_grad,
        query_key[0:width].T,
        query_key[width:].T,
        value_out[0:width].T,
        small[7 + heads, 0:width],
        small[8 + heads, 0:width],
        small[7 : 7 + heads, 0:CONV_TAPS],
        value_out[width:],
        small[2],
        small[0],
        small[1],
        up_sum,
        small[6, 0:units],
        down_sum,
        small[5],
        small[3],
        small[4],
    )


def solution(mesh):
    rows = P(("dp", "tensor"), None)
    columns = P(None, "tensor")
    split_rows = P("tensor", None)
    vector = P("tensor")
    return jax.shard_map(
        per_device,
        mesh=mesh,
        in_specs=(
            P("dp", None), columns, columns, columns, vector, vector, split_rows, split_rows, P(), P(), P(),
            columns, vector, split_rows, P(), P(), P(), rows, P("dp"), P("dp"),
        ),
        out_specs=(
            rows, rows, columns, columns, columns, vector, vector, split_rows, split_rows, P(), P(), P(),
            columns, vector, split_rows, P(), P(), P(),
        ),
        check_vma=False,
    )
```

```python
import functools

import jax
import jax.numpy as jnp
from jax import lax
from jax.experimental import pallas as pl
from jax.experimental.pallas import tpu as pltpu
from jax.sharding import PartitionSpec as P

HEAD_DIM = 64
LANDMARKS = 64
CONV_TAPS = 33
PINV_STEPS = 6
DOCS = 8
PER_DOC = LANDMARKS // DOCS
SEQ_LEN = 1024
EPSILON = 1e-05
SCALE = HEAD_DIM ** -0.5
HALF = CONV_TAPS // 2
BLOCK = 128
WINDOW = 256
CHUNK = 256
F32 = jnp.float32
BF16 = jnp.bfloat16
NN = (((1,), (0,)), ((), ()))
NT = (((1,), (1,)), ((), ()))
TN = (((0,), (0,)), ((), ()))


def takes(microseconds):
    return pl.CostEstimate(flops=int(microseconds * 1.1e9), bytes_accessed=1, transcendentals=0)


def mm(left, right, dims=NN):
    return lax.dot_general(left, right, dims, preferred_element_type=F32)


def split(value):
    high = value.astype(BF16)
    return high, (value - high.astype(F32)).astype(BF16)


def mm3(left, right, dims=NN):
    lh, ll = left
    rh, rl = right
    return mm(lh, rh, dims) + mm(ll, rh, dims) + mm(lh, rl, dims)


def iota(shape, dim):
    return lax.broadcasted_iota(jnp.int32, shape, dim)


def head_count(width):
    return width // HEAD_DIM


def block_mask(heads):
    shape = (heads * LANDMARKS, heads * HEAD_DIM)
    return iota(shape, 0) // LANDMARKS == iota(shape, 1) // HEAD_DIM


def spread(rows, heads):
    return jnp.where(block_mask(heads), jnp.concatenate([rows] * heads, axis=0), 0.0)


def fold(full, heads):
    return jnp.concatenate(
        [full[h * 64 : (h + 1) * 64, h * 64 : (h + 1) * 64] for h in range(heads)], axis=0
    )


def stack(rows, heads):
    return jnp.concatenate([rows[:, h * 64 : (h + 1) * 64] for h in range(heads)], axis=0)


def unstack(rows, heads):
    return jnp.concatenate([rows[h * 64 : (h + 1) * 64] for h in range(heads)], axis=1)


def block_diag(rows, heads):
    return jnp.where(block_mask(heads), jnp.concatenate([rows] * heads, axis=1), 0.0)


def doc_masks(segment):
    return [jnp.broadcast_to(segment == d, (PER_DOC, segment.shape[1])) for d in range(DOCS)]


def pick(full, masks, heads):
    out = []
    for h in range(heads):
        kept = jnp.zeros(masks[0].shape, F32)
        for d in range(DOCS):
            row = h * LANDMARKS + d * PER_DOC
            kept = jnp.where(masks[d], full[row : row + PER_DOC], kept)
        out.append(kept)
    return out


def place(compact, masks, heads):
    return jnp.concatenate(
        [jnp.where(masks[d], compact[h], 0.0) for h in range(heads) for d in range(DOCS)], axis=0
    )


def per_doc(rows, masks):
    out = jnp.zeros(masks[0].shape, F32)
    for d in range(DOCS):
        out = jnp.where(masks[d], rows[d * PER_DOC : (d + 1) * PER_DOC], out)
    return out


def rows_to_lanes(full, scratch, heads):
    rows = heads * LANDMARKS
    lane_doc = (iota((rows, 128), 1) // PER_DOC) % DOCS
    row_doc = (iota((rows, 128), 0) // PER_DOC) % DOCS
    kept = jnp.where(lane_doc == row_doc, full, 0.0)
    for shift in (8, 16, 32):
        kept = kept + pltpu.roll(kept, shift, 1)
    scratch[0:rows, :] = kept
    count = heads * DOCS
    group = iota((count, 128), 1) // PER_DOC
    out = jnp.zeros((count, 128), F32)
    for i in range(PER_DOC):
        out = jnp.where(group == i, scratch[pl.ds(i, count, stride=PER_DOC), :], out)
    return jnp.concatenate([out, jnp.zeros((128 - count, 128), F32)], axis=0).T[0:64]


def lanes_to_rows(blocks, heads):
    full = jnp.concatenate([blocks, jnp.zeros((64, 128), F32)], axis=0).T
    return full[0 : heads * DOCS]


def apply_blocks(coef, operand_ref, result_ref, heads, transposed):
    count = heads * DOCS
    pieces = [operand_ref[pl.ds(j, count, stride=PER_DOC), :] for j in range(PER_DOC)]
    for i in range(PER_DOC):
        total = jnp.zeros(pieces[0].shape, F32)
        for j in range(PER_DOC):
            k = j * PER_DOC + i if transposed else i * PER_DOC + j
            total = total + coef[:, k : k + 1] * pieces[j]
        result_ref[pl.ds(i, count, stride=PER_DOC), :] = total


def bm(left, right):
    a = left.reshape(8, 8, -1)
    b = right.reshape(8, 8, -1)
    total = a[:, 0:1] * b[0:1]
    for k in range(1, 8):
        total = total + a[:, k : k + 1] * b[k : k + 1]
    return total.reshape(64, -1)


def bm_tn(left, right):
    rows = []
    for i in range(8):
        total = left[i : i + 1] * right[0:8]
        for k in range(1, 8):
            total = total + left[k * 8 + i : k * 8 + i + 1] * right[k * 8 : k * 8 + 8]
        rows.append(total)
    return jnp.concatenate(rows, axis=0)


def flip(blocks, scratch):
    scratch[0:64, :] = blocks
    return jnp.concatenate([scratch[pl.ds(i, 8, stride=8), :] for i in range(8)], axis=0)


def lane_eye():
    row = iota((64, 128), 0)
    return jnp.where(row // 8 == row % 8, 1.0, 0.0)


def column_sums(blocks):
    total = blocks[0:8]
    for i in range(1, 8):
        total = total + blocks[i * 8 : i * 8 + 8]
    return total


def row_sums(blocks):
    return jnp.concatenate(
        [jnp.sum(blocks[i * 8 : i * 8 + 8], axis=0, keepdims=True) for i in range(8)], axis=0
    )


def head_lanes(h):
    return iota((8, 128), 1) // DOCS == h


def head_most(sums, heads):
    out = jnp.ones((1, 128), F32)
    for h in range(heads):
        mask = head_lanes(h)
        most = jnp.max(jnp.max(jnp.where(mask, sums, -1e30), axis=1, keepdims=True), axis=0, keepdims=True)
        out = jnp.where(mask[0:1], most, out)
    return out


def head_total(values, heads):
    out = jnp.zeros((1, 128), F32)
    for h in range(heads):
        mask = head_lanes(h)
        total = jnp.sum(jnp.sum(jnp.where(mask, values, 0.0), axis=1, keepdims=True), axis=0, keepdims=True)
        out = jnp.where(mask[0:1], total, out)
    return out


def same_document(segment, seg_pad, start):
    rows = jnp.broadcast_to(segment[:, start : start + BLOCK], (BLOCK, BLOCK)).T
    return jnp.concatenate([rows, rows], axis=1) == seg_pad[0:1, start : start + WINDOW]


def toeplitz(taps_row):
    return pltpu.roll(jnp.broadcast_to(taps_row, (BLOCK, WINDOW)), 0, 1, stride=1, stride_axis=0)


def pad_segment(seg_pad, segment):
    seg_pad[:, 0:128] = jnp.zeros((8, 128), F32)
    seg_pad[:, 0:SEQ_LEN] = jnp.broadcast_to(pltpu.roll(segment, HALF, 1), (8, SEQ_LEN))
    seg_pad[:, SEQ_LEN:] = jnp.broadcast_to(segment[:, SEQ_LEN - 1 : SEQ_LEN], (8, WINDOW))


def attend_forward_kernel(
    where_ref, tokens_ref, wq_ref, wk_ref, wv_ref, bq_ref, bv_ref, taps_ref, w_out_ref, seg_ref, mark_ref,
    keep_a_ref, keep_b_ref, send_a_ref, send_b_ref, q_ref, k_ref, v_ref, att_ref, p1_ref, p3_ref, qm_ref, km_ref, ctx_ref, bl_ref, count_ref, mid_ref, steps_ref, inverse_ref,
    padded, seg_pad, scratch, band,
):
    width = wq_ref.shape[0]
    heads = head_count(width)
    tokens = tokens_ref.at[0]
    rows = 256

    def project(i, carry):
        at = pl.ds(pl.multiple_of(i * rows, rows), rows)
        x = tokens[at, :]
        q_ref[at, :] = (mm(x, wq_ref[...], NT) + bq_ref[...]).astype(BF16)
        k_ref[at, :] = mm(x, wk_ref[...], NT).astype(BF16)
        value = (mm(x, wv_ref[...], NT) + bv_ref[...]).astype(BF16)
        v_ref[at, :] = value
        padded[pl.ds(pl.multiple_of(i * rows + HALF, 16), rows), :] = value
        return carry

    padded[0:HALF, :] = jnp.zeros((HALF, width), BF16)
    padded[SEQ_LEN + HALF :, :] = jnp.zeros((WINDOW - HALF, width), BF16)
    lax.fori_loop(0, SEQ_LEN // rows, project, 0)

    segment = seg_ref[0].astype(F32)
    masks = doc_masks(segment)
    one_hot = mark_ref[0] == iota((LANDMARKS, SEQ_LEN), 0)
    counts = jnp.sum(one_hot.astype(F32), axis=1, keepdims=True)
    pool = one_hot.astype(BF16)
    q_marks = mm(pool, q_ref[...]) / counts
    k_marks = mm(pool, k_ref[...]) / counts
    count_ref[...] = jnp.broadcast_to(counts, (LANDMARKS, 128))
    qm_ref[...] = q_marks
    km_ref[...] = k_marks
    k_block = split(spread(k_marks, heads))
    q_wide = spread(q_marks, heads)
    q_block = split(q_wide)

    queries = q_ref[...]
    scores = pick(mm(k_block[0], queries, NT) + mm(k_block[1], queries, NT), masks, heads)
    first = []
    for h in range(heads):
        s = scores[h] * SCALE
        e = jnp.exp(s - jnp.max(s, axis=0, keepdims=True))
        first.append(e / jnp.sum(e, axis=0, keepdims=True))
    p1_ref[...] = jnp.concatenate(first, axis=0)

    keys = k_ref[...]
    scores = pick(mm(q_block[0], keys, NT) + mm(q_block[1], keys, NT), masks, heads)
    last = []
    for h in range(heads):
        s = scores[h] * SCALE
        most = jnp.concatenate(
            [jnp.max(jnp.where(masks[d], s, -1e30), axis=1, keepdims=True) for d in range(DOCS)], axis=0
        )
        e = jnp.exp(s - per_doc(most, masks))
        total = jnp.concatenate(
            [jnp.sum(jnp.where(masks[d], e, 0.0), axis=1, keepdims=True) for d in range(DOCS)], axis=0
        )
        last.append(e / per_doc(total, masks))
    p3_ref[...] = jnp.concatenate(last, axis=0)

    weights = split(place(last, masks, heads))
    values = v_ref[...]
    context = fold(mm(weights[0], values) + mm(weights[1], values), heads)
    ctx_ref[...] = context

    twice = jnp.concatenate([k_marks, k_marks], axis=0)
    grid = lax.dot_general(q_wide, twice, NT, precision=lax.Precision.HIGHEST, preferred_element_type=F32)
    scores = (rows_to_lanes(grid, scratch, heads) * SCALE).reshape(8, 8, 128)
    e = jnp.exp(scores - jnp.max(scores, axis=1, keepdims=True))
    middle = (e / jnp.sum(e, axis=1, keepdims=True)).reshape(64, 128)
    used = iota((64, 128), 1) < heads * DOCS
    middle = jnp.where(used, middle, 0.0)
    mid_ref[...] = middle
    norm = head_most(column_sums(middle), heads) * head_most(row_sums(middle), heads)
    eye = lane_eye()

    def step(n, inverse):
        product = bm(middle, inverse)
        second = 15.0 * eye - bm(product, 7.0 * eye - product)
        third = 13.0 * eye - bm(product, second)
        steps_ref[n, 0] = inverse
        steps_ref[n, 1] = product
        steps_ref[n, 2] = second
        steps_ref[n, 3] = third
        return 0.25 * bm(inverse, third)

    inverse = lax.fori_loop(0, PINV_STEPS, step, flip(middle, scratch) / norm)
    inverse_ref[...] = inverse
    coef = lanes_to_rows(inverse, heads)
    apply_blocks(coef, ctx_ref, bl_ref, heads, False)
    blended = split(block_diag(bl_ref[...], heads))
    weights = split(place(first, masks, heads))
    attended = mm3(weights, blended, TN)

    for h in range(heads):
        band[h] = toeplitz(taps_ref[h : h + 1, :]).astype(BF16)
    pad_segment(seg_pad, segment)
    att_ref[...] = attended.astype(BF16)
    lane_head = iota((BLOCK, width), 1) // HEAD_DIM
    scratch_f = attended

    for b in range(SEQ_LEN // BLOCK):
        start = b * BLOCK
        rows_at = pl.ds(start, BLOCK)
        same = same_document(segment, seg_pad, start)
        window = padded[pl.ds(start, WINDOW), :]
        total = scratch_f[start : start + BLOCK]
        for h in range(heads):
            part = mm(jnp.where(same, band[h], 0), window)
            total = total + jnp.where(lane_head == h, part, 0.0)
        att_ref[rows_at, :] = total.astype(BF16)

    half = SEQ_LEN // 2
    core = where_ref[1]
    weight = w_out_ref[...]
    for base, refs in ((core, (keep_a_ref, keep_b_ref)), (1 - core, (send_a_ref, send_b_ref))):
        for i, ref in enumerate(refs):
            at = pl.ds(pl.multiple_of(base * half + i * CHUNK, CHUNK), CHUNK)
            ref[...] = mm(att_ref[at, :], weight).astype(BF16)


def attend_forward(where, tokens, wq, wk, wv, bq, bv, taps, w_out, segments, marks):
    dim = tokens.shape[2]
    width = wq.shape[0]
    heads = head_count(width)

    def whole(*shape):
        return pl.BlockSpec(shape, lambda i, w: (0,) * len(shape))

    def one(*shape):
        return pl.BlockSpec((1,) + shape, lambda i, w: (w[0],) + (0,) * len(shape))

    outs = [
        *[((CHUNK, dim), BF16)] * 4,
        ((SEQ_LEN, width), BF16), ((SEQ_LEN, width), BF16), ((SEQ_LEN, width), BF16), ((SEQ_LEN, width), BF16),
        ((heads * 8, SEQ_LEN), F32), ((heads * 8, SEQ_LEN), F32),
        ((LANDMARKS, width), F32), ((LANDMARKS, width), F32),
        ((heads * LANDMARKS, HEAD_DIM), F32), ((heads * LANDMARKS, HEAD_DIM), F32),
        ((LANDMARKS, 128), F32), ((64, 128), F32), ((PINV_STEPS, 4, 64, 128), F32), ((64, 128), F32),
    ]
    return pl.pallas_call(
        attend_forward_kernel,
        out_shape=[jax.ShapeDtypeStruct(s, t) for s, t in outs],
        grid_spec=pltpu.PrefetchScalarGridSpec(
            num_scalar_prefetch=1,
            grid=(1,),
            in_specs=[
                one(SEQ_LEN, dim), whole(width, dim), whole(width, dim), whole(width, dim), whole(1, width), whole(1, width),
                whole(heads, WINDOW), whole(width, dim), one(1, SEQ_LEN), one(1, SEQ_LEN),
            ],
            out_specs=[whole(*s) for s, t in outs],
            scratch_shapes=[
                pltpu.VMEM((SEQ_LEN + WINDOW, width), BF16),
                pltpu.VMEM((8, SEQ_LEN + WINDOW), F32),
                pltpu.VMEM((heads * LANDMARKS, 128), F32),
                pltpu.VMEM((heads, BLOCK, WINDOW), BF16),
            ],
        ),
        compiler_params=pltpu.CompilerParams(vmem_limit_bytes=56 << 20),
        cost_estimate=takes(12),
    )(where, tokens, wq, wk, wv, bq, bv, taps, w_out, segments, marks)


def diagonal_sums(band):
    row = iota(band.shape, 0)
    for bit in range(7):
        shift = 1 << bit
        moved = pltpu.roll(band, WINDOW - shift, 1)
        band = jnp.where((row // shift) % 2 == 1, moved, band)
    return jnp.sum(band, axis=0, keepdims=True)


def plus(ref, at, value):
    return value if ref is None else ref[at] + value


def sums_refs(final, where_ref, refs, turn):
    if not final:
        weights_ref, *refs = refs
        return None, None, weights_ref, refs, lambda: None
    prev_ref, prev_small_ref, kept_ref, sent_ref, *refs = refs
    *refs, weights_ref = refs

    def finish():
        half = kept_ref.shape[0]
        bit = where_ref[2 + turn]
        kept_ref[...] = weights_ref[pl.ds(pl.multiple_of(bit * half, half), half), :]
        sent_ref[...] = weights_ref[pl.ds(pl.multiple_of((1 - bit) * half, half), half), :].astype(BF16)

    return prev_ref, prev_small_ref, weights_ref, refs, finish


def attend_back_values_kernel(
    final, where_ref, mine_ref, theirs_ref, tokens_ref, taps_ref, w_out_ref, seg_ref,
    v_ref, att_ref, p1_ref, p3_ref, ctx_ref, bl_ref, inverse_ref, *refs
):
    prev_ref, prev_small_ref, weights_ref, refs, finish = sums_refs(final, where_ref, refs, 0)
    small_ref, dv_ref, ds1_ref, ds3_ref, dbl_ref, dctx_ref, grad_ref, up_ref, value_ref, seg_pad, band, corr = refs
    width = v_ref.shape[1]
    heads = head_count(width)
    half = SEQ_LEN // 2
    core = where_ref[1]

    grad_ref[0:HALF, :] = jnp.zeros((HALF, width), BF16)
    grad_ref[SEQ_LEN + HALF :, :] = jnp.zeros((WINDOW - HALF, width), BF16)
    value_ref[0:HALF, :] = jnp.zeros((HALF, width), BF16)
    value_ref[SEQ_LEN + HALF :, :] = jnp.zeros((WINDOW - HALF, width), BF16)
    value_ref[HALF : SEQ_LEN + HALF, :] = v_ref[...]
    for base, ref in ((core, mine_ref), (1 - core, theirs_ref)):
        for i in range(half // CHUNK):
            at = pl.ds(i * CHUNK, CHUNK)
            to = pl.multiple_of(base * half + i * CHUNK, CHUNK)
            up_ref[pl.ds(to, CHUNK), :] = ref[at, :]
            grad_ref[pl.ds(pl.multiple_of(to + HALF, HALF), CHUNK), :] = mm(ref[at, :], w_out_ref[...], NT).astype(BF16)
    at = (slice(width, 2 * width), slice(None))
    weights_ref[at] = plus(prev_ref, at, mm(att_ref[...], up_ref[...], TN))

    segment = seg_ref[0].astype(F32)
    masks = doc_masks(segment)
    first = [p1_ref[h * 8 : h * 8 + 8, :] for h in range(heads)]
    last = [p3_ref[h * 8 : h * 8 + 8, :] for h in range(heads)]
    gradient = grad_ref[HALF : SEQ_LEN + HALF, :]
    values = v_ref[...]

    first_wide = split(place(first, masks, heads))
    dbl = fold(mm(first_wide[0], gradient) + mm(first_wide[1], gradient), heads)
    dbl_ref[...] = dbl
    blended = split(block_diag(bl_ref[...], heads))
    dfirst = pick(mm(blended[0], gradient, NT) + mm(blended[1], gradient, NT), masks, heads)
    for h in range(heads):
        ds1_ref[h * 8 : h * 8 + 8, :] = (
            SCALE * first[h] * (dfirst[h] - jnp.sum(first[h] * dfirst[h], axis=0, keepdims=True))
        )

    apply_blocks(lanes_to_rows(inverse_ref[...], heads), dbl_ref, dctx_ref, heads, True)
    dctx = dctx_ref[...]
    dctx_wide = split(block_diag(dctx, heads))
    dlast = pick(mm(dctx_wide[0], values, NT) + mm(dctx_wide[1], values, NT), masks, heads)
    inner = jnp.sum(dctx * ctx_ref[...], axis=1, keepdims=True)
    for h in range(heads):
        ds3_ref[h * 8 : h * 8 + 8, :] = (
            SCALE * last[h] * (dlast[h] - per_doc(inner[h * 64 : (h + 1) * 64], masks))
        )
    last_wide = place(last, masks, heads).astype(BF16)
    dvalue = mm(last_wide, dctx_wide[0], TN) + mm(last_wide, dctx_wide[1], TN)

    for h in range(heads):
        band[h] = toeplitz(taps_ref[h : h + 1, :]).astype(BF16)
        corr[h] = jnp.zeros((BLOCK, WINDOW), F32)
    pad_segment(seg_pad, segment)
    lane_head = iota((BLOCK, width), 1) // HEAD_DIM
    for b in range(SEQ_LEN // BLOCK):
        begin = b * BLOCK
        same = same_document(segment, seg_pad, begin)
        window = grad_ref[begin : begin + WINDOW, :]
        near = value_ref[begin : begin + WINDOW, :]
        block = grad_ref[begin + HALF : begin + HALF + BLOCK, :]
        total = dvalue[begin : begin + BLOCK]
        for h in range(heads):
            taps = jnp.where(same, band[h], 0)
            part = mm(taps, window)
            total = total + jnp.where(lane_head == h, part, 0.0)
            mine = lane_head == h
            part = mm(jnp.where(mine, block, 0), near, NT)
            corr[h] = corr[h] + jnp.where(same, part, 0.0)
        dv_ref[begin : begin + BLOCK, :] = total.astype(BF16)

    small_ref[...] = jnp.zeros(small_ref.shape, F32)
    for h in range(heads):
        at = (slice(h, h + 1), slice(None))
        small_ref[at] = plus(prev_small_ref, at, diagonal_sums(corr[h]))
    at = (slice(heads + 1, heads + 2), slice(0, width))
    small_ref[at] = plus(prev_small_ref, at, jnp.sum(dv_ref[...].astype(F32), axis=0, keepdims=True))
    at = (slice(0, width), slice(None))
    weights_ref[at] = plus(prev_ref, at, mm(dv_ref[...], tokens_ref[0], TN))
    finish()


def attend_back_queries_kernel(
    final, where_ref, tokens_ref, seg_ref, mark_ref,
    q_ref, k_ref, qm_ref, km_ref, ctx_ref, count_ref, mid_ref, steps_ref, ds1_ref, ds3_ref, dbl_ref, *refs
):
    prev_ref, prev_small_ref, weights_ref, refs, finish = sums_refs(final, where_ref, refs, 1)
    small_ref, dq_ref, dk_ref, scratch, scratch_b, dqm_ref, dkm_ref, stack_ref = refs
    width = q_ref.shape[1]
    heads = head_count(width)
    masks = doc_masks(seg_ref[0].astype(F32))
    pool = (mark_ref[0] == iota((LANDMARKS, SEQ_LEN), 0)).astype(BF16)
    queries = q_ref[...]
    keys = k_ref[...]
    dscore_one = split(place([ds1_ref[h * 8 : h * 8 + 8, :] for h in range(heads)], masks, heads))
    dscore_last = split(place([ds3_ref[h * 8 : h * 8 + 8, :] for h in range(heads)], masks, heads))
    dkm = fold(mm(dscore_one[0], queries) + mm(dscore_one[1], queries), heads)
    dqm = fold(mm(dscore_last[0], keys) + mm(dscore_last[1], keys), heads)

    context = unstack(ctx_ref[...], heads)
    grid = lax.dot_general(
        block_diag(dbl_ref[...], heads), jnp.concatenate([context, context], axis=0), NT,
        precision=lax.Precision.HIGHEST, preferred_element_type=F32,
    )
    dinverse = rows_to_lanes(grid, scratch, heads)
    middle = mid_ref[...]
    eye = lane_eye()

    def step(n, carry):
        dz, dmid = carry
        n = PINV_STEPS - 1 - n
        z = steps_ref[n, 0]
        product = steps_ref[n, 1]
        second = steps_ref[n, 2]
        third = steps_ref[n, 3]
        dthird = 0.25 * bm_tn(z, dz)
        dz_next = 0.25 * bm(dz, flip(third, scratch_b.at[0]))
        dsecond = -bm_tn(product, dthird)
        dprod = -bm(dthird, flip(second, scratch_b.at[1])) - bm(dsecond, flip(7.0 * eye - product, scratch_b.at[2]))
        dprod = dprod + bm_tn(product, dsecond)
        dmid = dmid + bm(dprod, flip(z, scratch_b.at[3]))
        dz_next = dz_next + bm_tn(middle, dprod)
        return dz_next, dmid

    dz, dmid = lax.fori_loop(0, PINV_STEPS, step, (dinverse, jnp.zeros((64, 128), F32)))
    columns = column_sums(middle)
    across = row_sums(middle)
    column_most = head_most(columns, heads)
    row_most = head_most(across, heads)
    start = flip(middle, scratch) / (column_most * row_most)
    dmid = dmid + flip(dz, scratch) / (column_most * row_most)
    total = jnp.sum(dz * start, axis=0, keepdims=True)
    total = head_total(jnp.where(iota((8, 128), 0) == 0, jnp.broadcast_to(total, (8, 128)), 0.0), heads)
    hit = jnp.where(columns == column_most, 1.0, 0.0)
    dcolumns = -total / column_most * hit / jnp.maximum(head_total(hit, heads), 1.0)
    hit = jnp.where(across == row_most, 1.0, 0.0)
    drows = -total / row_most * hit / jnp.maximum(head_total(hit, heads), 1.0)
    dmid = dmid + jnp.concatenate([dcolumns + drows[i : i + 1] for i in range(8)], axis=0)
    dgrid = jnp.concatenate(
        [
            SCALE * middle[i * 8 : i * 8 + 8]
            * (dmid[i * 8 : i * 8 + 8] - jnp.sum(middle[i * 8 : i * 8 + 8] * dmid[i * 8 : i * 8 + 8], axis=0, keepdims=True))
            for i in range(8)
        ],
        axis=0,
    )
    coef = lanes_to_rows(dgrid, heads)
    q_stack = stack(qm_ref[...], heads)
    k_stack = stack(km_ref[...], heads)
    stack_ref[...] = k_stack
    apply_blocks(coef, stack_ref, dqm_ref, heads, False)
    stack_ref[...] = q_stack
    apply_blocks(coef, stack_ref, dkm_ref, heads, True)

    dqm = dqm + dqm_ref[...]
    dkm = dkm + dkm_ref[...]
    counts = count_ref[:, 0:1]
    dqm = split(unstack(dqm, heads) / counts)
    dkm = split(unstack(dkm, heads) / counts)
    k_wide = split(spread(km_ref[...], heads))
    q_wide = split(spread(qm_ref[...], heads))

    def pulled(scores, wide, marks):
        left = jnp.concatenate([scores[0], pool], axis=0)
        return mm(left, jnp.concatenate([wide[0], marks[0]], axis=0), TN) + mm(
            left, jnp.concatenate([wide[1], marks[1]], axis=0), TN
        )

    dq_ref[...] = pulled(dscore_one, k_wide, dqm).astype(BF16)
    dk_ref[...] = pulled(dscore_last, q_wide, dkm).astype(BF16)

    small_ref[...] = jnp.zeros(small_ref.shape, F32)
    at = (slice(heads, heads + 1), slice(0, width))
    small_ref[...] = plus(prev_small_ref, (slice(None), slice(None)), small_ref[...])
    small_ref[at] = plus(prev_small_ref, at, jnp.sum(dq_ref[...].astype(F32), axis=0, keepdims=True))
    tokens = tokens_ref[0]
    for n, ref in enumerate((dq_ref, dk_ref)):
        at = (slice(n * width, (n + 1) * width), slice(None))
        weights_ref[at] = plus(prev_ref, at, mm(ref[...], tokens, TN))
    finish()


def attend_back_tokens_kernel(where_ref, *refs):
    ins, weights, outs = refs[:6], [ref[...] for ref in refs[6:9]], refs[9:]
    for n in range(2):
        outs[n][...] = sum(mm(ref[...], w) for ref, w in zip(ins[3 * n : 3 * n + 3], weights)).astype(BF16)


def attend_back_tokens(where, parts, weights):
    width, dim = weights[0].shape
    step = 256
    count = SEQ_LEN // 2 // step

    def rows(near):
        def at(i, w):
            return ((w[1] if near else 1 - w[1]) * count + i, 0)

        return pl.BlockSpec((step, width), at)

    return pl.pallas_call(
        attend_back_tokens_kernel,
        out_shape=[jax.ShapeDtypeStruct((SEQ_LEN // 2, dim), BF16)] * 2,
        grid_spec=pltpu.PrefetchScalarGridSpec(
            num_scalar_prefetch=1,
            grid=(count,),
            in_specs=[rows(True)] * 3 + [rows(False)] * 3 + [pl.BlockSpec((width, dim), lambda i, w: (0, 0))] * 3,
            out_specs=[pl.BlockSpec((step, dim), lambda i, w: (i, 0))] * 2,
        ),
        compiler_params=pltpu.CompilerParams(vmem_limit_bytes=40 << 20),
        cost_estimate=takes(3),
    )(where, *parts, *parts, *weights)


def whole(shape):
    return pl.BlockSpec(shape, lambda i, w: (0,) * len(shape))


def chosen(shape):
    return pl.BlockSpec((1,) + shape, lambda i, w: (w[0],) + (0,) * len(shape))


def sums_outs(width, dim, final):
    return [((width, dim), F32), ((width, dim), BF16)] if final else [((2 * width, dim), F32)]


def back_call(kernel, where, ins, specs, outs, scratch, final):
    return pl.pallas_call(
        kernel,
        out_shape=[jax.ShapeDtypeStruct(s, t) for s, t in outs],
        grid_spec=pltpu.PrefetchScalarGridSpec(
            num_scalar_prefetch=1, grid=(1,), in_specs=specs, out_specs=[whole(s) for s, t in outs], scratch_shapes=scratch
        ),
        compiler_params=pltpu.CompilerParams(vmem_limit_bytes=56 << 20),
        cost_estimate=takes(0.1 if final else 11),
    )(where, *ins)


def attend_back_values(where, mine, theirs, tokens, taps, w_out, segments, saved, prev=()):
    dim = tokens.shape[2]
    q, k, v, att, p1, p3, qm, km, ctx, bl, count, mid, steps, inverse = saved
    width = v.shape[1]
    heads = head_count(width)
    final = len(prev) > 0
    rest = (v, att, p1, p3, ctx, bl, inverse, *prev)
    specs = [
        whole(mine.shape), whole(theirs.shape), chosen((SEQ_LEN, dim)), whole(taps.shape), whole(w_out.shape), chosen((1, SEQ_LEN)),
        *[whole(x.shape) for x in rest],
    ]
    outs = [
        *sums_outs(width, dim, final), ((8, WINDOW), F32), ((SEQ_LEN, width), BF16), (p1.shape, F32), (p3.shape, F32),
        (bl.shape, F32), (ctx.shape, F32),
    ]
    scratch = [
        pltpu.VMEM((SEQ_LEN + WINDOW, width), BF16),
        pltpu.VMEM((SEQ_LEN, dim), BF16),
        pltpu.VMEM((SEQ_LEN + WINDOW, width), BF16),
        pltpu.VMEM((8, SEQ_LEN + WINDOW), F32),
        pltpu.VMEM((heads, BLOCK, WINDOW), BF16),
        pltpu.VMEM((heads, BLOCK, WINDOW), F32),
        *([pltpu.VMEM((2 * width, dim), F32)] if final else []),
    ]
    kernel = functools.partial(attend_back_values_kernel, final)
    return back_call(kernel, where, (mine, theirs, tokens, taps, w_out, segments, *rest), specs, outs, scratch, final)


def attend_back_queries(where, tokens, segments, marks, saved, part, prev=()):
    dim = tokens.shape[2]
    q, k, v, att, p1, p3, qm, km, ctx, bl, count, mid, steps, inverse = saved
    ds1, ds3, dbl = part
    width = q.shape[1]
    heads = head_count(width)
    final = len(prev) > 0
    rest = (q, k, qm, km, ctx, count, mid, steps, ds1, ds3, dbl, *prev)
    specs = [chosen((SEQ_LEN, dim)), chosen((1, SEQ_LEN)), chosen((1, SEQ_LEN)), *[whole(x.shape) for x in rest]]
    outs = [*sums_outs(width, dim, final), ((8, WINDOW), F32), ((SEQ_LEN, width), BF16), ((SEQ_LEN, width), BF16)]
    scratch = [
        pltpu.VMEM((heads * LANDMARKS, 128), F32),
        pltpu.VMEM((4, 64, 128), F32),
        *[pltpu.VMEM((heads * LANDMARKS, HEAD_DIM), F32)] * 3,
        *([pltpu.VMEM((2 * width, dim), F32)] if final else []),
    ]
    kernel = functools.partial(attend_back_queries_kernel, final)
    return back_call(kernel, where, (tokens, segments, marks, *rest), specs, outs, scratch, final)


ERFC = (
    0.12694266047513267, 0.12694157407364748, 0.11413597639508828, 0.08762459251766126, 0.05998263605520133,
    -0.01120062503236582, 0.07123816174906503, -0.1503297151041413, 0.09536518640917925, -0.020700440227622966,
)


def normal_cdf(value):
    size = jnp.abs(value)
    t = 1.0 / (1.0 + 0.31819805153394637 * size)
    poly = ERFC[-1]
    for coef in ERFC[-2::-1]:
        poly = poly * t + coef
    bell = jnp.exp(-0.5 * size * size)
    tail = bell * (t * poly)
    return jnp.where(value > 0.0, 1.0 - tail, tail), bell


def up_down_kernel(*refs):
    count = (len(refs) - 3) // 4
    w_up_ref, b_up_ref, w_down_ref = refs[count : count + 3]
    outs = refs[count + 3 :]
    for n in range(count):
        act_ref, slope_ref, part_ref = outs[3 * n : 3 * n + 3]
        hidden = mm(refs[n][...], w_up_ref[...]) + b_up_ref[...]
        below, bell = normal_cdf(hidden)
        act = (hidden * below).astype(BF16)
        act_ref[...] = act
        slope_ref[...] = (below + hidden * (bell * 0.3989422804014327)).astype(BF16)
        part_ref[...] = mm(act, w_down_ref[...]).astype(BF16)


def fixed(*shape):
    return pl.BlockSpec(shape, lambda i: (0,) * len(shape), pipeline_mode=pl.Buffered(1))


def strip(rows, width):
    return pl.BlockSpec((rows, width), lambda i: (i, 0))


def up_down(blocks, w_up, b_up, w_down):
    rows, dim = blocks[0].shape
    units = w_up.shape[1]
    step = 128
    total = rows * len(blocks)
    out = pl.pallas_call(
        up_down_kernel,
        out_shape=[jax.ShapeDtypeStruct((rows, w), BF16) for w in (units, units, dim)] * len(blocks),
        grid=(rows // step,),
        in_specs=[strip(step, dim)] * len(blocks) + [fixed(dim, units), fixed(1, units), fixed(units, dim)],
        out_specs=[strip(step, units), strip(step, units), strip(step, dim)] * len(blocks),
        compiler_params=pltpu.CompilerParams(vmem_limit_bytes=40 << 20),
        cost_estimate=takes(total * 0.007),
    )(*blocks, w_up, b_up, w_down)
    return [out[3 * n : 3 * n + 3] for n in range(len(blocks))]


def up_down_back_kernel(*refs):
    count = (len(refs) - 2) // 4
    w_up_ref, w_down_ref = refs[2 * count : 2 * count + 2]
    outs = refs[2 * count + 2 :]
    for n in range(count):
        grad_ref, slope_ref = refs[2 * n : 2 * n + 2]
        hidden = (mm(grad_ref[...], w_down_ref[...], NT) * slope_ref[...].astype(F32)).astype(BF16)
        outs[2 * n][...] = hidden
        outs[2 * n + 1][...] = mm(hidden, w_up_ref[...], NT).astype(BF16)


def up_down_back(pairs, w_up, w_down):
    rows, dim = pairs[0][0].shape
    units = w_up.shape[1]
    step = 128
    total = rows * len(pairs)
    out = pl.pallas_call(
        up_down_back_kernel,
        out_shape=[jax.ShapeDtypeStruct((rows, w), BF16) for w in (units, dim)] * len(pairs),
        grid=(rows // step,),
        in_specs=[strip(step, dim), strip(step, units)] * len(pairs) + [fixed(dim, units), fixed(units, dim)],
        out_specs=[strip(step, units), strip(step, dim)] * len(pairs),
        compiler_params=pltpu.CompilerParams(vmem_limit_bytes=40 << 20),
        cost_estimate=takes(total * 0.007),
    )(*[x for pair in pairs for x in pair], w_up, w_down)
    return [out[2 * n : 2 * n + 2] for n in range(len(pairs))]


def up_down_weights_kernel(final, bits_ref, *refs):
    outs = refs[-7:] if final else refs[-3:]
    ins = refs[: len(refs) - len(outs)]
    prev, ins = (ins[-3:], ins[:-3]) if final else ((), ins)
    down_ref, up_ref = outs[-2:] if final else outs[:2]
    bias_ref = outs[4] if final else outs[2]

    @pl.when(pl.program_id(0) == 0)
    def _():
        for n, ref in enumerate((down_ref, up_ref, bias_ref)):
            ref[...] = prev[n][...] if final else jnp.zeros(ref.shape, F32)

    for n in range(len(ins) // 4):
        act_ref, grad_ref, low_ref, hidden_ref = ins[4 * n : 4 * n + 4]
        hidden = hidden_ref[...]
        down_ref[...] += mm(act_ref[...], grad_ref[...], TN)
        up_ref[...] += mm(low_ref[...], hidden, TN)
        bias_ref[0:1, :] += jnp.sum(hidden.astype(F32), axis=0, keepdims=True)

    if final:

        @pl.when(pl.program_id(0) == pl.num_programs(0) - 1)
        def _():
            for n, ref in enumerate((down_ref, up_ref)):
                half = ref.shape[0] // 2
                bit = bits_ref[2 + n]
                outs[2 * n][...] = ref[pl.ds(pl.multiple_of(bit * half, half), half), :]
                outs[2 * n + 1][...] = ref[pl.ds(pl.multiple_of((1 - bit) * half, half), half), :].astype(BF16)


def up_down_weights(bits, blocks, prev=()):
    rows, units = blocks[0][0].shape
    dim = blocks[0][1].shape[1]
    step = 256
    final = len(prev) > 0
    sums = [((units, dim), F32), ((dim, units), F32)]
    outs = sums
    if final:
        outs = [o for (r, c), t in sums for o in (((r // 2, c), F32), ((r // 2, c), BF16))]
    outs = [*outs, ((8, units), F32)]

    def strips(width):
        return pl.BlockSpec((step, width), lambda i, w: (i, 0))

    def once(shape):
        return pl.BlockSpec(shape, lambda i, w: (0, 0), pipeline_mode=pl.Buffered(1))

    return pl.pallas_call(
        functools.partial(up_down_weights_kernel, final),
        out_shape=[jax.ShapeDtypeStruct(s, t) for s, t in outs],
        grid_spec=pltpu.PrefetchScalarGridSpec(
            num_scalar_prefetch=1,
            grid=(rows // step,),
            in_specs=[strips(units), strips(dim), strips(dim), strips(units)] * len(blocks) + [once(p.shape) for p in prev],
            out_specs=[once(s) for s, t in outs],
            scratch_shapes=[pltpu.VMEM(s, t) for s, t in sums] if final else [],
        ),
        compiler_params=pltpu.CompilerParams(vmem_limit_bytes=40 << 20),
        cost_estimate=takes(5),
    )(bits, *[x for block in blocks for x in block], *prev)


def swap(value, mask, axis="tensor"):
    count = lax.axis_size(axis)
    return lax.ppermute(value, axis, [(i, i ^ mask) for i in range(count)])


class Total:
    def __init__(self, kept, sent, first, axis):
        masks = [1 << n for n in range(lax.axis_size(axis).bit_length() - 1)]
        masks.insert(0, masks.pop(first))
        self.order = masks + masks[-2::-1]
        self.count = len(masks)
        self.axis = axis
        self.index = lax.axis_index(axis)
        self.kept = kept
        self.level = 0
        self.begin(sent)

    def bit(self, n):
        return ((self.index & self.order[n]) != 0).astype(jnp.int32)

    def begin(self, sent):
        self.sent = sent
        self.got = swap(sent, self.order[self.level], self.axis)
        self.level += 1

    def step(self, *others):
        got = after(self.got, *others)
        if self.level < self.count - 1:
            half = got.shape[0] // 2
            bit = self.bit(self.level)

            def rows(which):
                at = which * half
                kept = lax.dynamic_slice_in_dim(self.kept, at, half, 0)
                return kept + lax.dynamic_slice_in_dim(got, at, half, 0).astype(F32)

            sent = rows(1 - bit).astype(BF16)
            self.kept = rows(bit)
        elif self.level == self.count - 1:
            sent = self.kept = (self.kept + got.astype(F32)).astype(BF16)
        elif self.level == self.count:
            sent = self.kept = (self.kept.astype(F32) + got.astype(F32)).astype(BF16)
        else:
            bit = self.bit(self.level - 1) > 0
            sent = self.kept = jnp.concatenate([jnp.where(bit, got, self.kept), jnp.where(bit, self.kept, got)], axis=0)
        if self.level < len(self.order):
            self.begin(sent)
        return sent

    def finish(self):
        while self.level < len(self.order):
            self.step()
        return self.step()


def after(value, *others):
    return lax.optimization_barrier((value,) + others)[0]


def normalize(value):
    centered = value - jnp.mean(value, axis=-1, keepdims=True)
    inv = lax.rsqrt(jnp.mean(centered * centered, axis=-1, keepdims=True) + EPSILON)
    return centered * inv, inv


def norm_back(grad, gain, unit, inv):
    r = grad * gain
    back = (r - jnp.mean(r, axis=-1, keepdims=True) - unit * jnp.mean(r * unit, axis=-1, keepdims=True)) * inv
    return back, jnp.sum(grad * unit, axis=0), jnp.sum(grad, axis=0)


def per_device(
    tokens, w_query, w_key, w_value, b_query, b_value, conv_taps, w_out, b_out, gain_one, shift_one, w_up, b_up, w_down,
    b_down, gain_two, shift_two, cotangent, segment_ids, landmark_ids,
):
    dim = tokens.shape[1]
    width = w_query.shape[1]
    units = w_up.shape[1]
    heads = head_count(width)
    seqs = tokens.shape[0] // SEQ_LEN
    me = lax.axis_index("tensor")
    core, chip = me % 2, me // 2
    own_rows = cotangent.shape[0]
    sequences = tokens.reshape(seqs, SEQ_LEN, dim)
    segments = segment_ids.reshape(seqs, 1, SEQ_LEN)
    marks = landmark_ids.reshape(seqs, 1, SEQ_LEN)
    place_dp = lax.axis_index("dp")
    bits = [place_dp % 2, place_dp // 2 % 2]
    at_own = jnp.stack([chip, core, *bits]).astype(jnp.int32)
    at_far = jnp.stack([1 - chip, core, *bits]).astype(jnp.int32)
    taps = jnp.pad(conv_taps, ((0, 0), (0, WINDOW - CONV_TAPS)))
    taps_back = jnp.pad(conv_taps[:, ::-1], ((0, 0), (0, WINDOW - CONV_TAPS)))
    wq, wk, wv = w_query.T, w_key.T, w_value.T
    bias = b_up[None]

    def forward(at):
        return attend_forward(
            at, sequences, wq, wk, wv, b_query[None], b_value[None], taps, w_out, segments, marks
        )

    def halves(first, second):
        return jnp.concatenate([first, second], axis=0)

    far = forward(at_far)
    owed = halves(far[0] + swap(far[2], 1), far[1] + swap(far[3], 1))
    own = forward(after(at_own, owed))
    through = swap(owed, 2)
    near = halves(swap(own[2], 1), swap(own[3], 1))
    summed = halves(own[0], own[1]).astype(F32) + near.astype(F32) + through.astype(F32)
    own_tokens = lax.dynamic_slice_in_dim(tokens, me * own_rows, own_rows, 0).astype(F32)
    unit_one, inv_one = normalize(own_tokens + summed + b_out)
    normed = unit_one * gain_one + shift_one

    def feed(mine, run, meanwhile=None):
        near = swap(mine, 1)
        got = swap(mine, 2)
        here = run([mine, near], 0)
        ready = here[0][-1] if meanwhile is None else meanwhile([mine, near], here)
        got = after(got, ready)
        cross = swap(got, 1)
        there = run([got], 2)
        cross = after(cross, there[0][-1])
        there = there + run([cross], 3)
        owed = there[0][-1] + swap(there[1][-1], 1)
        blocks = [mine, near, got, cross]
        through = swap(owed, 2)
        total = here[0][-1].astype(F32) + swap(here[1][-1], 1).astype(F32) + through.astype(F32)
        return blocks, here + there, total, owed

    lows, acts, branch, _ = feed(normed.astype(BF16), lambda blocks, n: up_down(blocks, w_up, bias, w_down))
    unit_two, inv_two = normalize(normed + branch + b_down)
    output = (unit_two * gain_two + shift_two).astype(BF16)
    grad_pre_out, grad_gain_two, grad_shift_two = norm_back(cotangent.astype(F32), gain_two, unit_two, inv_two)
    grad_b_down = jnp.sum(grad_pre_out, axis=0)
    grad_low = lax.optimization_barrier(grad_pre_out.astype(BF16))
    unit_low = lax.optimization_barrier(unit_one.astype(BF16))

    sums = []

    def weigh_own(grads, backs):
        blocks = [(acts[n][0], grads[n], lows[n], backs[n][0]) for n in range(2)]
        sums.extend(up_down_weights(at_own, blocks))
        return sums[0]

    grads, backs, back_normed, owed = feed(
        grad_low,
        lambda blocks, n: up_down_back([(b, acts[n + i][1]) for i, b in enumerate(blocks)], w_up, w_down),
        weigh_own,
    )
    blocks = [(acts[n][0], grads[n], lows[n], backs[n][0]) for n in (2, 3)]
    blocks[0] = (after(blocks[0][0], owed), *blocks[0][1:])
    down_kept, down_sent, up_kept, up_sent, d_bias = up_down_weights(at_own, blocks, sums)
    back_normed = after(back_normed, down_sent, up_sent)
    down = Total(down_kept, down_sent, 0, "dp")
    up = Total(up_kept, up_sent, 1, "dp")
    grad_pre_norm, grad_gain_one, grad_shift_one = norm_back(
        grad_low.astype(F32) + back_normed, gain_one, unit_low.astype(F32), inv_one
    )
    grad_b_out = jnp.sum(grad_pre_norm, axis=0)
    top = lax.optimization_barrier(grad_pre_norm.astype(BF16))
    near = swap(top, 1)
    over = swap(top, 2)

    def values(at, mine, theirs, saved, prev=()):
        return attend_back_values(at, mine, theirs, sequences, taps_back, w_out, segments, saved, prev)

    def queries(at, saved, part, prev=()):
        return attend_back_queries(at, sequences, segments, marks, saved, part, prev)

    def both(*others):
        return down.step(*others), up.step(*others)

    norms = jnp.stack([grad_gain_one, grad_shift_one, grad_b_out, grad_gain_two, grad_shift_two, grad_b_down])
    own_v = values(after(at_own, *both(top)), top, near, own[4:])
    own_q = queries(after(at_own, *both(own_v[0])), own[4:], own_v[3:6])
    norms = norms + after(swap(norms, 1), own_q[0])
    far_v = values(after(at_far, own_q[0]), over, swap(over, 1), far[4:], own_v[0:2])
    norms = norms + after(swap(norms, 2), far_v[0])
    one = Total(far_v[0], far_v[1], 0, "dp")
    far_q = queries(after(at_far, *both(far_v[0])), far[4:], far_v[4:7], own_q[0:2])
    two = Total(far_q[0], far_q[1], 1, "dp")
    far_x = attend_back_tokens(at_far, (far_q[3], far_q[4], far_v[3]), (wq, wk, wv))
    owed = far_x[0] + swap(far_x[1], 1)
    through = swap(owed, 2)
    own_x = attend_back_tokens(at_own, (after(own_q[2], owed), own_q[3], own_v[2]), (wq, wk, wv))
    near = swap(own_x[1], 1)
    small = jnp.concatenate(
        [norms, d_bias[0:1], jnp.pad((far_v[2] + far_q[2])[0 : heads + 2], ((0, 0), (0, dim - WINDOW)))], axis=0
    )
    one.step(far_q[0])
    down.got, up.got, one.got, two.got = lax.optimization_barrier((down.got, up.got, one.got, two.got))
    for part in (two, one, up, down):
        part.step()
    mask = 1
    while mask < lax.axis_size("dp"):
        got = swap(small, mask, "dp")
        if mask == 1:
            got, one.got, two.got = lax.optimization_barrier((got, one.got, two.got))
            two.step()
            one.step()
            down.got, up.got, two.got = lax.optimization_barrier((down.got, up.got, two.got))
        elif mask == 2:
            got, one.got, two.got = lax.optimization_barrier((got, one.got, two.got))
            two.step()
            one.step()
        elif mask == 4:
            got, one.got, two.got, through = lax.optimization_barrier((got, one.got, two.got, through))
            two.step()
        small = small + got
        mask *= 2
    input_grad = top.astype(F32) + own_x[0].astype(F32) + near.astype(F32) + through.astype(F32)
    value_out = one.finish().astype(F32)
    query_key = two.finish().astype(F32)
    down_sum = down.finish().astype(F32)
    up_sum = up.finish().astype(F32)

    return (
        output,
        input_grad,
        query_key[0:width].T,
        query_key[width:].T,
        value_out[0:width].T,
        small[7 + heads, 0:width],
        small[8 + heads, 0:width],
        small[7 : 7 + heads, 0:CONV_TAPS],
        value_out[width:],
        small[2],
        small[0],
        small[1],
        up_sum,
        small[6, 0:units],
        down_sum,
        small[5],
        small[3],
        small[4],
    )


def solution(mesh):
    rows = P(("dp", "tensor"), None)
    columns = P(None, "tensor")
    split_rows = P("tensor", None)
    vector = P("tensor")
    return jax.shard_map(
        per_device,
        mesh=mesh,
        in_specs=(
            P("dp", None), columns, columns, columns, vector, vector, split_rows, split_rows, P(), P(), P(),
            columns, vector, split_rows, P(), P(), P(), rows, P("dp"), P("dp"),
        ),
        out_specs=(
            rows, rows, columns, columns, columns, vector, vector, split_rows, split_rows, P(), P(), P(),
            columns, vector, split_rows, P(), P(), P(),
        ),
        check_vma=False,
    )
```

```python
import functools

import jax
import jax.numpy as jnp
from jax import lax
from jax.experimental import pallas as pl
from jax.experimental.pallas import tpu as pltpu
from jax.sharding import PartitionSpec as P

HEAD_DIM = 64
LANDMARKS = 64
CONV_TAPS = 33
PINV_STEPS = 6
DOCS = 8
PER_DOC = LANDMARKS // DOCS
SEQ_LEN = 1024
EPSILON = 1e-05
SCALE = HEAD_DIM ** -0.5
HALF = CONV_TAPS // 2
BLOCK = 128
WINDOW = 256
CHUNK = 256
F32 = jnp.float32
BF16 = jnp.bfloat16
NN = (((1,), (0,)), ((), ()))
NT = (((1,), (1,)), ((), ()))
TN = (((0,), (0,)), ((), ()))


def takes(microseconds):
    return pl.CostEstimate(flops=int(microseconds * 1.1e9), bytes_accessed=1, transcendentals=0)


def mm(left, right, dims=NN):
    return lax.dot_general(left, right, dims, preferred_element_type=F32)


def split(value):
    high = value.astype(BF16)
    return high, (value - high.astype(F32)).astype(BF16)


def mm3(left, right, dims=NN):
    lh, ll = left
    rh, rl = right
    return mm(lh, rh, dims) + mm(ll, rh, dims) + mm(lh, rl, dims)


def iota(shape, dim):
    return lax.broadcasted_iota(jnp.int32, shape, dim)


def head_count(width):
    return width // HEAD_DIM


def block_mask(heads):
    shape = (heads * LANDMARKS, heads * HEAD_DIM)
    return iota(shape, 0) // LANDMARKS == iota(shape, 1) // HEAD_DIM


def spread(rows, heads):
    return jnp.where(block_mask(heads), jnp.concatenate([rows] * heads, axis=0), 0.0)


def fold(full, heads):
    return jnp.concatenate(
        [full[h * 64 : (h + 1) * 64, h * 64 : (h + 1) * 64] for h in range(heads)], axis=0
    )


def stack(rows, heads):
    return jnp.concatenate([rows[:, h * 64 : (h + 1) * 64] for h in range(heads)], axis=0)


def unstack(rows, heads):
    return jnp.concatenate([rows[h * 64 : (h + 1) * 64] for h in range(heads)], axis=1)


def block_diag(rows, heads):
    return jnp.where(block_mask(heads), jnp.concatenate([rows] * heads, axis=1), 0.0)


def doc_masks(segment):
    return [jnp.broadcast_to(segment == d, (PER_DOC, segment.shape[1])) for d in range(DOCS)]


def pick(full, masks, heads):
    out = []
    for h in range(heads):
        kept = jnp.zeros(masks[0].shape, F32)
        for d in range(DOCS):
            row = h * LANDMARKS + d * PER_DOC
            kept = jnp.where(masks[d], full[row : row + PER_DOC], kept)
        out.append(kept)
    return out


def place(compact, masks, heads):
    return jnp.concatenate(
        [jnp.where(masks[d], compact[h], 0.0) for h in range(heads) for d in range(DOCS)], axis=0
    )


def per_doc(rows, masks):
    out = jnp.zeros(masks[0].shape, F32)
    for d in range(DOCS):
        out = jnp.where(masks[d], rows[d * PER_DOC : (d + 1) * PER_DOC], out)
    return out


def rows_to_lanes(full, scratch, heads):
    rows = heads * LANDMARKS
    lane_doc = (iota((rows, 128), 1) // PER_DOC) % DOCS
    row_doc = (iota((rows, 128), 0) // PER_DOC) % DOCS
    kept = jnp.where(lane_doc == row_doc, full, 0.0)
    for shift in (8, 16, 32):
        kept = kept + pltpu.roll(kept, shift, 1)
    scratch[0:rows, :] = kept
    count = heads * DOCS
    group = iota((count, 128), 1) // PER_DOC
    out = jnp.zeros((count, 128), F32)
    for i in range(PER_DOC):
        out = jnp.where(group == i, scratch[pl.ds(i, count, stride=PER_DOC), :], out)
    return jnp.concatenate([out, jnp.zeros((128 - count, 128), F32)], axis=0).T[0:64]


def lanes_to_rows(blocks, heads):
    full = jnp.concatenate([blocks, jnp.zeros((64, 128), F32)], axis=0).T
    return full[0 : heads * DOCS]


def apply_blocks(coef, operand_ref, result_ref, heads, transposed):
    count = heads * DOCS
    pieces = [operand_ref[pl.ds(j, count, stride=PER_DOC), :] for j in range(PER_DOC)]
    for i in range(PER_DOC):
        total = jnp.zeros(pieces[0].shape, F32)
        for j in range(PER_DOC):
            k = j * PER_DOC + i if transposed else i * PER_DOC + j
            total = total + coef[:, k : k + 1] * pieces[j]
        result_ref[pl.ds(i, count, stride=PER_DOC), :] = total


def bm(left, right):
    a = left.reshape(8, 8, -1)
    b = right.reshape(8, 8, -1)
    total = a[:, 0:1] * b[0:1]
    for k in range(1, 8):
        total = total + a[:, k : k + 1] * b[k : k + 1]
    return total.reshape(64, -1)


def bm_tn(left, right):
    rows = []
    for i in range(8):
        total = left[i : i + 1] * right[0:8]
        for k in range(1, 8):
            total = total + left[k * 8 + i : k * 8 + i + 1] * right[k * 8 : k * 8 + 8]
        rows.append(total)
    return jnp.concatenate(rows, axis=0)


def flip(blocks, scratch):
    scratch[0:64, :] = blocks
    return jnp.concatenate([scratch[pl.ds(i, 8, stride=8), :] for i in range(8)], axis=0)


def lane_eye():
    row = iota((64, 128), 0)
    return jnp.where(row // 8 == row % 8, 1.0, 0.0)


def column_sums(blocks):
    total = blocks[0:8]
    for i in range(1, 8):
        total = total + blocks[i * 8 : i * 8 + 8]
    return total


def row_sums(blocks):
    return jnp.concatenate(
        [jnp.sum(blocks[i * 8 : i * 8 + 8], axis=0, keepdims=True) for i in range(8)], axis=0
    )


def head_lanes(h):
    return iota((8, 128), 1) // DOCS == h


def head_most(sums, heads):
    out = jnp.ones((1, 128), F32)
    for h in range(heads):
        mask = head_lanes(h)
        most = jnp.max(jnp.max(jnp.where(mask, sums, -1e30), axis=1, keepdims=True), axis=0, keepdims=True)
        out = jnp.where(mask[0:1], most, out)
    return out


def head_total(values, heads):
    out = jnp.zeros((1, 128), F32)
    for h in range(heads):
        mask = head_lanes(h)
        total = jnp.sum(jnp.sum(jnp.where(mask, values, 0.0), axis=1, keepdims=True), axis=0, keepdims=True)
        out = jnp.where(mask[0:1], total, out)
    return out


def same_document(segment, seg_pad, start):
    rows = jnp.broadcast_to(segment[:, start : start + BLOCK], (BLOCK, BLOCK)).T
    return jnp.concatenate([rows, rows], axis=1) == seg_pad[0:1, start : start + WINDOW]


def toeplitz(taps_row):
    return pltpu.roll(jnp.broadcast_to(taps_row, (BLOCK, WINDOW)), 0, 1, stride=1, stride_axis=0)


def pad_segment(seg_pad, segment):
    seg_pad[:, 0:128] = jnp.zeros((8, 128), F32)
    seg_pad[:, 0:SEQ_LEN] = jnp.broadcast_to(pltpu.roll(segment, HALF, 1), (8, SEQ_LEN))
    seg_pad[:, SEQ_LEN:] = jnp.broadcast_to(segment[:, SEQ_LEN - 1 : SEQ_LEN], (8, WINDOW))


def attend_forward_kernel(
    where_ref, tokens_ref, wq_ref, wk_ref, wv_ref, bq_ref, bv_ref, taps_ref, w_out_ref, seg_ref, mark_ref,
    keep_a_ref, keep_b_ref, send_a_ref, send_b_ref, q_ref, k_ref, v_ref, att_ref, p1_ref, p3_ref, qm_ref, km_ref, ctx_ref, bl_ref, count_ref, mid_ref, steps_ref, inverse_ref,
    padded, seg_pad, scratch, band,
):
    width = wq_ref.shape[0]
    heads = head_count(width)
    tokens = tokens_ref.at[0]
    rows = 256

    def project(i, carry):
        at = pl.ds(pl.multiple_of(i * rows, rows), rows)
        x = tokens[at, :]
        q_ref[at, :] = (mm(x, wq_ref[...], NT) + bq_ref[...]).astype(BF16)
        k_ref[at, :] = mm(x, wk_ref[...], NT).astype(BF16)
        value = (mm(x, wv_ref[...], NT) + bv_ref[...]).astype(BF16)
        v_ref[at, :] = value
        padded[pl.ds(pl.multiple_of(i * rows + HALF, 16), rows), :] = value
        return carry

    padded[0:HALF, :] = jnp.zeros((HALF, width), BF16)
    padded[SEQ_LEN + HALF :, :] = jnp.zeros((WINDOW - HALF, width), BF16)
    lax.fori_loop(0, SEQ_LEN // rows, project, 0)

    segment = seg_ref[0].astype(F32)
    masks = doc_masks(segment)
    one_hot = mark_ref[0] == iota((LANDMARKS, SEQ_LEN), 0)
    counts = jnp.sum(one_hot.astype(F32), axis=1, keepdims=True)
    pool = one_hot.astype(BF16)
    q_marks = mm(pool, q_ref[...]) / counts
    k_marks = mm(pool, k_ref[...]) / counts
    count_ref[...] = jnp.broadcast_to(counts, (LANDMARKS, 128))
    qm_ref[...] = q_marks
    km_ref[...] = k_marks
    k_block = split(spread(k_marks, heads))
    q_wide = spread(q_marks, heads)
    q_block = split(q_wide)

    queries = q_ref[...]
    scores = pick(mm(k_block[0], queries, NT) + mm(k_block[1], queries, NT), masks, heads)
    first = []
    for h in range(heads):
        s = scores[h] * SCALE
        e = jnp.exp(s - jnp.max(s, axis=0, keepdims=True))
        first.append(e / jnp.sum(e, axis=0, keepdims=True))
    p1_ref[...] = jnp.concatenate(first, axis=0)

    keys = k_ref[...]
    scores = pick(mm(q_block[0], keys, NT) + mm(q_block[1], keys, NT), masks, heads)
    last = []
    for h in range(heads):
        s = scores[h] * SCALE
        most = jnp.concatenate(
            [jnp.max(jnp.where(masks[d], s, -1e30), axis=1, keepdims=True) for d in range(DOCS)], axis=0
        )
        e = jnp.exp(s - per_doc(most, masks))
        total = jnp.concatenate(
            [jnp.sum(jnp.where(masks[d], e, 0.0), axis=1, keepdims=True) for d in range(DOCS)], axis=0
        )
        last.append(e / per_doc(total, masks))
    p3_ref[...] = jnp.concatenate(last, axis=0)

    weights = split(place(last, masks, heads))
    values = v_ref[...]
    context = fold(mm(weights[0], values) + mm(weights[1], values), heads)
    ctx_ref[...] = context

    twice = jnp.concatenate([k_marks, k_marks], axis=0)
    grid = lax.dot_general(q_wide, twice, NT, precision=lax.Precision.HIGHEST, preferred_element_type=F32)
    scores = (rows_to_lanes(grid, scratch, heads) * SCALE).reshape(8, 8, 128)
    e = jnp.exp(scores - jnp.max(scores, axis=1, keepdims=True))
    middle = (e / jnp.sum(e, axis=1, keepdims=True)).reshape(64, 128)
    used = iota((64, 128), 1) < heads * DOCS
    middle = jnp.where(used, middle, 0.0)
    mid_ref[...] = middle
    norm = head_most(column_sums(middle), heads) * head_most(row_sums(middle), heads)
    eye = lane_eye()

    def step(n, inverse):
        product = bm(middle, inverse)
        second = 15.0 * eye - bm(product, 7.0 * eye - product)
        third = 13.0 * eye - bm(product, second)
        steps_ref[n, 0] = inverse
        steps_ref[n, 1] = product
        steps_ref[n, 2] = second
        steps_ref[n, 3] = third
        return 0.25 * bm(inverse, third)

    inverse = lax.fori_loop(0, PINV_STEPS, step, flip(middle, scratch) / norm)
    inverse_ref[...] = inverse
    coef = lanes_to_rows(inverse, heads)
    apply_blocks(coef, ctx_ref, bl_ref, heads, False)
    blended = split(block_diag(bl_ref[...], heads))
    weights = split(place(first, masks, heads))
    attended = mm3(weights, blended, TN)

    for h in range(heads):
        band[h] = toeplitz(taps_ref[h : h + 1, :]).astype(BF16)
    pad_segment(seg_pad, segment)
    att_ref[...] = attended.astype(BF16)
    lane_head = iota((BLOCK, width), 1) // HEAD_DIM
    scratch_f = attended

    for b in range(SEQ_LEN // BLOCK):
        start = b * BLOCK
        rows_at = pl.ds(start, BLOCK)
        same = same_document(segment, seg_pad, start)
        window = padded[pl.ds(start, WINDOW), :]
        total = scratch_f[start : start + BLOCK]
        for h in range(heads):
            part = mm(jnp.where(same, band[h], 0), window)
            total = total + jnp.where(lane_head == h, part, 0.0)
        att_ref[rows_at, :] = total.astype(BF16)

    half = SEQ_LEN // 2
    core = where_ref[1]
    weight = w_out_ref[...]
    for base, refs in ((core, (keep_a_ref, keep_b_ref)), (1 - core, (send_a_ref, send_b_ref))):
        for i, ref in enumerate(refs):
            at = pl.ds(pl.multiple_of(base * half + i * CHUNK, CHUNK), CHUNK)
            ref[...] = mm(att_ref[at, :], weight).astype(BF16)


def attend_forward(where, tokens, wq, wk, wv, bq, bv, taps, w_out, segments, marks):
    dim = tokens.shape[2]
    width = wq.shape[0]
    heads = head_count(width)

    def whole(*shape):
        return pl.BlockSpec(shape, lambda i, w: (0,) * len(shape))

    def one(*shape):
        return pl.BlockSpec((1,) + shape, lambda i, w: (w[0],) + (0,) * len(shape))

    outs = [
        *[((CHUNK, dim), BF16)] * 4,
        ((SEQ_LEN, width), BF16), ((SEQ_LEN, width), BF16), ((SEQ_LEN, width), BF16), ((SEQ_LEN, width), BF16),
        ((heads * 8, SEQ_LEN), F32), ((heads * 8, SEQ_LEN), F32),
        ((LANDMARKS, width), F32), ((LANDMARKS, width), F32),
        ((heads * LANDMARKS, HEAD_DIM), F32), ((heads * LANDMARKS, HEAD_DIM), F32),
        ((LANDMARKS, 128), F32), ((64, 128), F32), ((PINV_STEPS, 4, 64, 128), F32), ((64, 128), F32),
    ]
    return pl.pallas_call(
        attend_forward_kernel,
        out_shape=[jax.ShapeDtypeStruct(s, t) for s, t in outs],
        grid_spec=pltpu.PrefetchScalarGridSpec(
            num_scalar_prefetch=1,
            grid=(1,),
            in_specs=[
                one(SEQ_LEN, dim), whole(width, dim), whole(width, dim), whole(width, dim), whole(1, width), whole(1, width),
                whole(heads, WINDOW), whole(width, dim), one(1, SEQ_LEN), one(1, SEQ_LEN),
            ],
            out_specs=[whole(*s) for s, t in outs],
            scratch_shapes=[
                pltpu.VMEM((SEQ_LEN + WINDOW, width), BF16),
                pltpu.VMEM((8, SEQ_LEN + WINDOW), F32),
                pltpu.VMEM((heads * LANDMARKS, 128), F32),
                pltpu.VMEM((heads, BLOCK, WINDOW), BF16),
            ],
        ),
        compiler_params=pltpu.CompilerParams(vmem_limit_bytes=56 << 20),
        cost_estimate=takes(12),
    )(where, tokens, wq, wk, wv, bq, bv, taps, w_out, segments, marks)


def diagonal_sums(band):
    row = iota(band.shape, 0)
    for bit in range(7):
        shift = 1 << bit
        moved = pltpu.roll(band, WINDOW - shift, 1)
        band = jnp.where((row // shift) % 2 == 1, moved, band)
    return jnp.sum(band, axis=0, keepdims=True)


def plus(ref, at, value):
    return value if ref is None else ref[at] + value


def sums_refs(final, where_ref, refs, turn):
    if not final:
        weights_ref, *refs = refs
        return None, None, weights_ref, refs, lambda: None
    prev_ref, prev_small_ref, kept_ref, sent_ref, *refs = refs
    *refs, weights_ref = refs

    def finish():
        half = kept_ref.shape[0]
        bit = where_ref[2 + turn]
        kept_ref[...] = weights_ref[pl.ds(pl.multiple_of(bit * half, half), half), :]
        sent_ref[...] = weights_ref[pl.ds(pl.multiple_of((1 - bit) * half, half), half), :].astype(BF16)

    return prev_ref, prev_small_ref, weights_ref, refs, finish


def attend_back_values_kernel(
    final, where_ref, mine_ref, theirs_ref, tokens_ref, taps_ref, w_out_ref, seg_ref,
    v_ref, att_ref, p1_ref, p3_ref, ctx_ref, bl_ref, inverse_ref, *refs
):
    prev_ref, prev_small_ref, weights_ref, refs, finish = sums_refs(final, where_ref, refs, 0)
    small_ref, dv_ref, ds1_ref, ds3_ref, dbl_ref, dctx_ref, grad_ref, up_ref, value_ref, seg_pad, band, corr = refs
    width = v_ref.shape[1]
    heads = head_count(width)
    half = SEQ_LEN // 2
    core = where_ref[1]

    grad_ref[0:HALF, :] = jnp.zeros((HALF, width), BF16)
    grad_ref[SEQ_LEN + HALF :, :] = jnp.zeros((WINDOW - HALF, width), BF16)
    value_ref[0:HALF, :] = jnp.zeros((HALF, width), BF16)
    value_ref[SEQ_LEN + HALF :, :] = jnp.zeros((WINDOW - HALF, width), BF16)
    value_ref[HALF : SEQ_LEN + HALF, :] = v_ref[...]
    for base, ref in ((core, mine_ref), (1 - core, theirs_ref)):
        for i in range(half // CHUNK):
            at = pl.ds(i * CHUNK, CHUNK)
            to = pl.multiple_of(base * half + i * CHUNK, CHUNK)
            up_ref[pl.ds(to, CHUNK), :] = ref[at, :]
            grad_ref[pl.ds(pl.multiple_of(to + HALF, HALF), CHUNK), :] = mm(ref[at, :], w_out_ref[...], NT).astype(BF16)
    at = (slice(width, 2 * width), slice(None))
    weights_ref[at] = plus(prev_ref, at, mm(att_ref[...], up_ref[...], TN))

    segment = seg_ref[0].astype(F32)
    masks = doc_masks(segment)
    first = [p1_ref[h * 8 : h * 8 + 8, :] for h in range(heads)]
    last = [p3_ref[h * 8 : h * 8 + 8, :] for h in range(heads)]
    gradient = grad_ref[HALF : SEQ_LEN + HALF, :]
    values = v_ref[...]

    first_wide = split(place(first, masks, heads))
    dbl = fold(mm(first_wide[0], gradient) + mm(first_wide[1], gradient), heads)
    dbl_ref[...] = dbl
    blended = split(block_diag(bl_ref[...], heads))
    dfirst = pick(mm(blended[0], gradient, NT) + mm(blended[1], gradient, NT), masks, heads)
    for h in range(heads):
        ds1_ref[h * 8 : h * 8 + 8, :] = (
            SCALE * first[h] * (dfirst[h] - jnp.sum(first[h] * dfirst[h], axis=0, keepdims=True))
        )

    apply_blocks(lanes_to_rows(inverse_ref[...], heads), dbl_ref, dctx_ref, heads, True)
    dctx = dctx_ref[...]
    dctx_wide = split(block_diag(dctx, heads))
    dlast = pick(mm(dctx_wide[0], values, NT) + mm(dctx_wide[1], values, NT), masks, heads)
    inner = jnp.sum(dctx * ctx_ref[...], axis=1, keepdims=True)
    for h in range(heads):
        ds3_ref[h * 8 : h * 8 + 8, :] = (
            SCALE * last[h] * (dlast[h] - per_doc(inner[h * 64 : (h + 1) * 64], masks))
        )
    last_wide = place(last, masks, heads).astype(BF16)
    dvalue = mm(last_wide, dctx_wide[0], TN) + mm(last_wide, dctx_wide[1], TN)

    for h in range(heads):
        band[h] = toeplitz(taps_ref[h : h + 1, :]).astype(BF16)
        corr[h] = jnp.zeros((BLOCK, WINDOW), F32)
    pad_segment(seg_pad, segment)
    lane_head = iota((BLOCK, width), 1) // HEAD_DIM
    for b in range(SEQ_LEN // BLOCK):
        begin = b * BLOCK
        same = same_document(segment, seg_pad, begin)
        window = grad_ref[begin : begin + WINDOW, :]
        near = value_ref[begin : begin + WINDOW, :]
        block = grad_ref[begin + HALF : begin + HALF + BLOCK, :]
        total = dvalue[begin : begin + BLOCK]
        for h in range(heads):
            taps = jnp.where(same, band[h], 0)
            part = mm(taps, window)
            total = total + jnp.where(lane_head == h, part, 0.0)
            mine = lane_head == h
            part = mm(jnp.where(mine, block, 0), near, NT)
            corr[h] = corr[h] + jnp.where(same, part, 0.0)
        dv_ref[begin : begin + BLOCK, :] = total.astype(BF16)

    small_ref[...] = jnp.zeros(small_ref.shape, F32)
    for h in range(heads):
        at = (slice(h, h + 1), slice(None))
        small_ref[at] = plus(prev_small_ref, at, diagonal_sums(corr[h]))
    at = (slice(heads + 1, heads + 2), slice(0, width))
    small_ref[at] = plus(prev_small_ref, at, jnp.sum(dv_ref[...].astype(F32), axis=0, keepdims=True))
    at = (slice(0, width), slice(None))
    weights_ref[at] = plus(prev_ref, at, mm(dv_ref[...], tokens_ref[0], TN))
    finish()


def attend_back_queries_kernel(
    final, where_ref, tokens_ref, seg_ref, mark_ref,
    q_ref, k_ref, qm_ref, km_ref, ctx_ref, count_ref, mid_ref, steps_ref, ds1_ref, ds3_ref, dbl_ref, *refs
):
    prev_ref, prev_small_ref, weights_ref, refs, finish = sums_refs(final, where_ref, refs, 1)
    small_ref, dq_ref, dk_ref, scratch, scratch_b, dqm_ref, dkm_ref, stack_ref = refs
    width = q_ref.shape[1]
    heads = head_count(width)
    masks = doc_masks(seg_ref[0].astype(F32))
    pool = (mark_ref[0] == iota((LANDMARKS, SEQ_LEN), 0)).astype(BF16)
    queries = q_ref[...]
    keys = k_ref[...]
    dscore_one = split(place([ds1_ref[h * 8 : h * 8 + 8, :] for h in range(heads)], masks, heads))
    dscore_last = split(place([ds3_ref[h * 8 : h * 8 + 8, :] for h in range(heads)], masks, heads))
    dkm = fold(mm(dscore_one[0], queries) + mm(dscore_one[1], queries), heads)
    dqm = fold(mm(dscore_last[0], keys) + mm(dscore_last[1], keys), heads)

    context = unstack(ctx_ref[...], heads)
    grid = lax.dot_general(
        block_diag(dbl_ref[...], heads), jnp.concatenate([context, context], axis=0), NT,
        precision=lax.Precision.HIGHEST, preferred_element_type=F32,
    )
    dinverse = rows_to_lanes(grid, scratch, heads)
    middle = mid_ref[...]
    eye = lane_eye()

    def step(n, carry):
        dz, dmid = carry
        n = PINV_STEPS - 1 - n
        z = steps_ref[n, 0]
        product = steps_ref[n, 1]
        second = steps_ref[n, 2]
        third = steps_ref[n, 3]
        dthird = 0.25 * bm_tn(z, dz)
        dz_next = 0.25 * bm(dz, flip(third, scratch_b.at[0]))
        dsecond = -bm_tn(product, dthird)
        dprod = -bm(dthird, flip(second, scratch_b.at[1])) - bm(dsecond, flip(7.0 * eye - product, scratch_b.at[2]))
        dprod = dprod + bm_tn(product, dsecond)
        dmid = dmid + bm(dprod, flip(z, scratch_b.at[3]))
        dz_next = dz_next + bm_tn(middle, dprod)
        return dz_next, dmid

    dz, dmid = lax.fori_loop(0, PINV_STEPS, step, (dinverse, jnp.zeros((64, 128), F32)))
    columns = column_sums(middle)
    across = row_sums(middle)
    column_most = head_most(columns, heads)
    row_most = head_most(across, heads)
    start = flip(middle, scratch) / (column_most * row_most)
    dmid = dmid + flip(dz, scratch) / (column_most * row_most)
    total = jnp.sum(dz * start, axis=0, keepdims=True)
    total = head_total(jnp.where(iota((8, 128), 0) == 0, jnp.broadcast_to(total, (8, 128)), 0.0), heads)
    hit = jnp.where(columns == column_most, 1.0, 0.0)
    dcolumns = -total / column_most * hit / jnp.maximum(head_total(hit, heads), 1.0)
    hit = jnp.where(across == row_most, 1.0, 0.0)
    drows = -total / row_most * hit / jnp.maximum(head_total(hit, heads), 1.0)
    dmid = dmid + jnp.concatenate([dcolumns + drows[i : i + 1] for i in range(8)], axis=0)
    dgrid = jnp.concatenate(
        [
            SCALE * middle[i * 8 : i * 8 + 8]
            * (dmid[i * 8 : i * 8 + 8] - jnp.sum(middle[i * 8 : i * 8 + 8] * dmid[i * 8 : i * 8 + 8], axis=0, keepdims=True))
            for i in range(8)
        ],
        axis=0,
    )
    coef = lanes_to_rows(dgrid, heads)
    q_stack = stack(qm_ref[...], heads)
    k_stack = stack(km_ref[...], heads)
    stack_ref[...] = k_stack
    apply_blocks(coef, stack_ref, dqm_ref, heads, False)
    stack_ref[...] = q_stack
    apply_blocks(coef, stack_ref, dkm_ref, heads, True)

    dqm = dqm + dqm_ref[...]
    dkm = dkm + dkm_ref[...]
    counts = count_ref[:, 0:1]
    dqm = split(unstack(dqm, heads) / counts)
    dkm = split(unstack(dkm, heads) / counts)
    k_wide = split(spread(km_ref[...], heads))
    q_wide = split(spread(qm_ref[...], heads))

    def pulled(scores, wide, marks):
        left = jnp.concatenate([scores[0], pool], axis=0)
        return mm(left, jnp.concatenate([wide[0], marks[0]], axis=0), TN) + mm(
            left, jnp.concatenate([wide[1], marks[1]], axis=0), TN
        )

    dq_ref[...] = pulled(dscore_one, k_wide, dqm).astype(BF16)
    dk_ref[...] = pulled(dscore_last, q_wide, dkm).astype(BF16)

    small_ref[...] = jnp.zeros(small_ref.shape, F32)
    at = (slice(heads, heads + 1), slice(0, width))
    small_ref[...] = plus(prev_small_ref, (slice(None), slice(None)), small_ref[...])
    small_ref[at] = plus(prev_small_ref, at, jnp.sum(dq_ref[...].astype(F32), axis=0, keepdims=True))
    tokens = tokens_ref[0]
    for n, ref in enumerate((dq_ref, dk_ref)):
        at = (slice(n * width, (n + 1) * width), slice(None))
        weights_ref[at] = plus(prev_ref, at, mm(ref[...], tokens, TN))
    finish()


def attend_back_tokens_kernel(where_ref, *refs):
    ins, weights, outs = refs[:6], [ref[...] for ref in refs[6:9]], refs[9:]
    for n in range(2):
        outs[n][...] = sum(mm(ref[...], w) for ref, w in zip(ins[3 * n : 3 * n + 3], weights)).astype(BF16)


def attend_back_tokens(where, parts, weights):
    width, dim = weights[0].shape
    step = 256
    count = SEQ_LEN // 2 // step

    def rows(near):
        def at(i, w):
            return ((w[1] if near else 1 - w[1]) * count + i, 0)

        return pl.BlockSpec((step, width), at)

    return pl.pallas_call(
        attend_back_tokens_kernel,
        out_shape=[jax.ShapeDtypeStruct((SEQ_LEN // 2, dim), BF16)] * 2,
        grid_spec=pltpu.PrefetchScalarGridSpec(
            num_scalar_prefetch=1,
            grid=(count,),
            in_specs=[rows(True)] * 3 + [rows(False)] * 3 + [pl.BlockSpec((width, dim), lambda i, w: (0, 0))] * 3,
            out_specs=[pl.BlockSpec((step, dim), lambda i, w: (i, 0))] * 2,
        ),
        compiler_params=pltpu.CompilerParams(vmem_limit_bytes=40 << 20),
        cost_estimate=takes(3),
    )(where, *parts, *parts, *weights)


def whole(shape):
    return pl.BlockSpec(shape, lambda i, w: (0,) * len(shape))


def chosen(shape):
    return pl.BlockSpec((1,) + shape, lambda i, w: (w[0],) + (0,) * len(shape))


def sums_outs(width, dim, final):
    return [((width, dim), F32), ((width, dim), BF16)] if final else [((2 * width, dim), F32)]


def back_call(kernel, where, ins, specs, outs, scratch, final):
    return pl.pallas_call(
        kernel,
        out_shape=[jax.ShapeDtypeStruct(s, t) for s, t in outs],
        grid_spec=pltpu.PrefetchScalarGridSpec(
            num_scalar_prefetch=1, grid=(1,), in_specs=specs, out_specs=[whole(s) for s, t in outs], scratch_shapes=scratch
        ),
        compiler_params=pltpu.CompilerParams(vmem_limit_bytes=56 << 20),
        cost_estimate=takes(0.1 if final else 11),
    )(where, *ins)


def attend_back_values(where, mine, theirs, tokens, taps, w_out, segments, saved, prev=()):
    dim = tokens.shape[2]
    q, k, v, att, p1, p3, qm, km, ctx, bl, count, mid, steps, inverse = saved
    width = v.shape[1]
    heads = head_count(width)
    final = len(prev) > 0
    rest = (v, att, p1, p3, ctx, bl, inverse, *prev)
    specs = [
        whole(mine.shape), whole(theirs.shape), chosen((SEQ_LEN, dim)), whole(taps.shape), whole(w_out.shape), chosen((1, SEQ_LEN)),
        *[whole(x.shape) for x in rest],
    ]
    outs = [
        *sums_outs(width, dim, final), ((8, WINDOW), F32), ((SEQ_LEN, width), BF16), (p1.shape, F32), (p3.shape, F32),
        (bl.shape, F32), (ctx.shape, F32),
    ]
    scratch = [
        pltpu.VMEM((SEQ_LEN + WINDOW, width), BF16),
        pltpu.VMEM((SEQ_LEN, dim), BF16),
        pltpu.VMEM((SEQ_LEN + WINDOW, width), BF16),
        pltpu.VMEM((8, SEQ_LEN + WINDOW), F32),
        pltpu.VMEM((heads, BLOCK, WINDOW), BF16),
        pltpu.VMEM((heads, BLOCK, WINDOW), F32),
        *([pltpu.VMEM((2 * width, dim), F32)] if final else []),
    ]
    kernel = functools.partial(attend_back_values_kernel, final)
    return back_call(kernel, where, (mine, theirs, tokens, taps, w_out, segments, *rest), specs, outs, scratch, final)


def attend_back_queries(where, tokens, segments, marks, saved, part, prev=()):
    dim = tokens.shape[2]
    q, k, v, att, p1, p3, qm, km, ctx, bl, count, mid, steps, inverse = saved
    ds1, ds3, dbl = part
    width = q.shape[1]
    heads = head_count(width)
    final = len(prev) > 0
    rest = (q, k, qm, km, ctx, count, mid, steps, ds1, ds3, dbl, *prev)
    specs = [chosen((SEQ_LEN, dim)), chosen((1, SEQ_LEN)), chosen((1, SEQ_LEN)), *[whole(x.shape) for x in rest]]
    outs = [*sums_outs(width, dim, final), ((8, WINDOW), F32), ((SEQ_LEN, width), BF16), ((SEQ_LEN, width), BF16)]
    scratch = [
        pltpu.VMEM((heads * LANDMARKS, 128), F32),
        pltpu.VMEM((4, 64, 128), F32),
        *[pltpu.VMEM((heads * LANDMARKS, HEAD_DIM), F32)] * 3,
        *([pltpu.VMEM((2 * width, dim), F32)] if final else []),
    ]
    kernel = functools.partial(attend_back_queries_kernel, final)
    return back_call(kernel, where, (tokens, segments, marks, *rest), specs, outs, scratch, final)


ERFC = (
    0.12694266047513267, 0.12694157407364748, 0.11413597639508828, 0.08762459251766126, 0.05998263605520133,
    -0.01120062503236582, 0.07123816174906503, -0.1503297151041413, 0.09536518640917925, -0.020700440227622966,
)


def normal_cdf(value):
    size = jnp.abs(value)
    t = 1.0 / (1.0 + 0.31819805153394637 * size)
    poly = ERFC[-1]
    for coef in ERFC[-2::-1]:
        poly = poly * t + coef
    bell = jnp.exp(-0.5 * size * size)
    tail = bell * (t * poly)
    return jnp.where(value > 0.0, 1.0 - tail, tail), bell


def up_down_kernel(*refs):
    count = (len(refs) - 3) // 4
    w_up_ref, b_up_ref, w_down_ref = refs[count : count + 3]
    outs = refs[count + 3 :]
    for n in range(count):
        act_ref, slope_ref, part_ref = outs[3 * n : 3 * n + 3]
        hidden = mm(refs[n][...], w_up_ref[...]) + b_up_ref[...]
        below, bell = normal_cdf(hidden)
        act = (hidden * below).astype(BF16)
        act_ref[...] = act
        slope_ref[...] = (below + hidden * (bell * 0.3989422804014327)).astype(BF16)
        part_ref[...] = mm(act, w_down_ref[...]).astype(BF16)


def fixed(*shape):
    return pl.BlockSpec(shape, lambda i: (0,) * len(shape), pipeline_mode=pl.Buffered(1))


def strip(rows, width):
    return pl.BlockSpec((rows, width), lambda i: (i, 0))


def up_down(blocks, w_up, b_up, w_down):
    rows, dim = blocks[0].shape
    units = w_up.shape[1]
    step = 128
    total = rows * len(blocks)
    out = pl.pallas_call(
        up_down_kernel,
        out_shape=[jax.ShapeDtypeStruct((rows, w), BF16) for w in (units, units, dim)] * len(blocks),
        grid=(rows // step,),
        in_specs=[strip(step, dim)] * len(blocks) + [fixed(dim, units), fixed(1, units), fixed(units, dim)],
        out_specs=[strip(step, units), strip(step, units), strip(step, dim)] * len(blocks),
        compiler_params=pltpu.CompilerParams(vmem_limit_bytes=40 << 20),
        cost_estimate=takes(total * 0.007),
    )(*blocks, w_up, b_up, w_down)
    return [out[3 * n : 3 * n + 3] for n in range(len(blocks))]


def up_down_back_kernel(*refs):
    count = (len(refs) - 2) // 4
    w_up_ref, w_down_ref = refs[2 * count : 2 * count + 2]
    outs = refs[2 * count + 2 :]
    for n in range(count):
        grad_ref, slope_ref = refs[2 * n : 2 * n + 2]
        hidden = (mm(grad_ref[...], w_down_ref[...], NT) * slope_ref[...].astype(F32)).astype(BF16)
        outs[2 * n][...] = hidden
        outs[2 * n + 1][...] = mm(hidden, w_up_ref[...], NT).astype(BF16)


def up_down_back(pairs, w_up, w_down):
    rows, dim = pairs[0][0].shape
    units = w_up.shape[1]
    step = 128
    total = rows * len(pairs)
    out = pl.pallas_call(
        up_down_back_kernel,
        out_shape=[jax.ShapeDtypeStruct((rows, w), BF16) for w in (units, dim)] * len(pairs),
        grid=(rows // step,),
        in_specs=[strip(step, dim), strip(step, units)] * len(pairs) + [fixed(dim, units), fixed(units, dim)],
        out_specs=[strip(step, units), strip(step, dim)] * len(pairs),
        compiler_params=pltpu.CompilerParams(vmem_limit_bytes=40 << 20),
        cost_estimate=takes(total * 0.007),
    )(*[x for pair in pairs for x in pair], w_up, w_down)
    return [out[2 * n : 2 * n + 2] for n in range(len(pairs))]


def up_down_weights_kernel(final, bits_ref, *refs):
    outs = refs[-7:] if final else refs[-3:]
    ins = refs[: len(refs) - len(outs)]
    prev, ins = (ins[-3:], ins[:-3]) if final else ((), ins)
    down_ref, up_ref = outs[-2:] if final else outs[:2]
    bias_ref = outs[4] if final else outs[2]

    @pl.when(pl.program_id(0) == 0)
    def _():
        for n, ref in enumerate((down_ref, up_ref, bias_ref)):
            ref[...] = prev[n][...] if final else jnp.zeros(ref.shape, F32)

    for n in range(len(ins) // 4):
        act_ref, grad_ref, low_ref, hidden_ref = ins[4 * n : 4 * n + 4]
        hidden = hidden_ref[...]
        down_ref[...] += mm(act_ref[...], grad_ref[...], TN)
        up_ref[...] += mm(low_ref[...], hidden, TN)
        bias_ref[0:1, :] += jnp.sum(hidden.astype(F32), axis=0, keepdims=True)

    if final:

        @pl.when(pl.program_id(0) == pl.num_programs(0) - 1)
        def _():
            for n, ref in enumerate((down_ref, up_ref)):
                half = ref.shape[0] // 2
                bit = bits_ref[2 + n]
                outs[2 * n][...] = ref[pl.ds(pl.multiple_of(bit * half, half), half), :]
                outs[2 * n + 1][...] = ref[pl.ds(pl.multiple_of((1 - bit) * half, half), half), :].astype(BF16)


def up_down_weights(bits, blocks, prev=()):
    rows, units = blocks[0][0].shape
    dim = blocks[0][1].shape[1]
    step = 256
    final = len(prev) > 0
    sums = [((units, dim), F32), ((dim, units), F32)]
    outs = sums
    if final:
        outs = [o for (r, c), t in sums for o in (((r // 2, c), F32), ((r // 2, c), BF16))]
    outs = [*outs, ((8, units), F32)]

    def strips(width):
        return pl.BlockSpec((step, width), lambda i, w: (i, 0))

    def once(shape):
        return pl.BlockSpec(shape, lambda i, w: (0, 0), pipeline_mode=pl.Buffered(1))

    return pl.pallas_call(
        functools.partial(up_down_weights_kernel, final),
        out_shape=[jax.ShapeDtypeStruct(s, t) for s, t in outs],
        grid_spec=pltpu.PrefetchScalarGridSpec(
            num_scalar_prefetch=1,
            grid=(rows // step,),
            in_specs=[strips(units), strips(dim), strips(dim), strips(units)] * len(blocks) + [once(p.shape) for p in prev],
            out_specs=[once(s) for s, t in outs],
            scratch_shapes=[pltpu.VMEM(s, t) for s, t in sums] if final else [],
        ),
        compiler_params=pltpu.CompilerParams(vmem_limit_bytes=40 << 20),
        cost_estimate=takes(5),
    )(bits, *[x for block in blocks for x in block], *prev)


def swap(value, mask, axis="tensor"):
    count = lax.axis_size(axis)
    return lax.ppermute(value, axis, [(i, i ^ mask) for i in range(count)])


class Total:
    def __init__(self, kept, sent, first, axis):
        masks = [1 << n for n in range(lax.axis_size(axis).bit_length() - 1)]
        masks.insert(0, masks.pop(first))
        self.order = masks + masks[-2::-1]
        self.count = len(masks)
        self.axis = axis
        self.index = lax.axis_index(axis)
        self.kept = kept
        self.level = 0
        self.begin(sent)

    def bit(self, n):
        return ((self.index & self.order[n]) != 0).astype(jnp.int32)

    def begin(self, sent):
        self.sent = sent
        self.got = swap(sent, self.order[self.level], self.axis)
        self.level += 1

    def step(self, *others):
        got = after(self.got, *others)
        if self.level < self.count - 1:
            half = got.shape[0] // 2
            bit = self.bit(self.level)

            def rows(which):
                at = which * half
                kept = lax.dynamic_slice_in_dim(self.kept, at, half, 0)
                return kept + lax.dynamic_slice_in_dim(got, at, half, 0).astype(F32)

            sent = rows(1 - bit).astype(BF16)
            self.kept = rows(bit)
        elif self.level == self.count - 1:
            sent = self.kept = (self.kept + got.astype(F32)).astype(BF16)
        elif self.level == self.count:
            sent = self.kept = (self.kept.astype(F32) + got.astype(F32)).astype(BF16)
        else:
            bit = self.bit(self.level - 1) > 0
            sent = self.kept = jnp.concatenate([jnp.where(bit, got, self.kept), jnp.where(bit, self.kept, got)], axis=0)
        if self.level < len(self.order):
            self.begin(sent)
        return sent

    def finish(self):
        while self.level < len(self.order):
            self.step()
        return self.step()


def swap_pieces(value):
    step = value.shape[0] // 4
    return jnp.concatenate([swap(value[n * step : (n + 1) * step], 1) for n in range(4)], axis=0)


def after(value, *others):
    return lax.optimization_barrier((value,) + others)[0]


def normalize(value):
    centered = value - jnp.mean(value, axis=-1, keepdims=True)
    inv = lax.rsqrt(jnp.mean(centered * centered, axis=-1, keepdims=True) + EPSILON)
    return centered * inv, inv


def norm_back(grad, gain, unit, inv):
    r = grad * gain
    back = (r - jnp.mean(r, axis=-1, keepdims=True) - unit * jnp.mean(r * unit, axis=-1, keepdims=True)) * inv
    return back, jnp.sum(grad * unit, axis=0), jnp.sum(grad, axis=0)


def per_device(
    tokens, w_query, w_key, w_value, b_query, b_value, conv_taps, w_out, b_out, gain_one, shift_one, w_up, b_up, w_down,
    b_down, gain_two, shift_two, cotangent, segment_ids, landmark_ids,
):
    dim = tokens.shape[1]
    width = w_query.shape[1]
    units = w_up.shape[1]
    heads = head_count(width)
    seqs = tokens.shape[0] // SEQ_LEN
    me = lax.axis_index("tensor")
    core, chip = me % 2, me // 2
    own_rows = cotangent.shape[0]
    sequences = tokens.reshape(seqs, SEQ_LEN, dim)
    segments = segment_ids.reshape(seqs, 1, SEQ_LEN)
    marks = landmark_ids.reshape(seqs, 1, SEQ_LEN)
    place_dp = lax.axis_index("dp")
    bits = [place_dp % 2, place_dp // 2 % 2]
    at_own = jnp.stack([chip, core, *bits]).astype(jnp.int32)
    at_far = jnp.stack([1 - chip, core, *bits]).astype(jnp.int32)
    taps = jnp.pad(conv_taps, ((0, 0), (0, WINDOW - CONV_TAPS)))
    taps_back = jnp.pad(conv_taps[:, ::-1], ((0, 0), (0, WINDOW - CONV_TAPS)))
    wq, wk, wv = w_query.T, w_key.T, w_value.T
    bias = b_up[None]

    def forward(at):
        return attend_forward(
            at, sequences, wq, wk, wv, b_query[None], b_value[None], taps, w_out, segments, marks
        )

    def halves(first, second):
        return jnp.concatenate([first, second], axis=0)

    far = forward(at_far)
    owed = halves(far[0] + swap(far[2], 1), far[1] + swap(far[3], 1))
    own = forward(after(at_own, owed))
    through = swap(owed, 2)
    near = halves(swap(own[2], 1), swap(own[3], 1))
    summed = halves(own[0], own[1]).astype(F32) + near.astype(F32) + through.astype(F32)
    own_tokens = lax.dynamic_slice_in_dim(tokens, me * own_rows, own_rows, 0).astype(F32)
    unit_one, inv_one = normalize(own_tokens + summed + b_out)
    normed = unit_one * gain_one + shift_one

    def feed(whole_mine, run, meanwhile=None):
        mine = [whole_mine[:CHUNK], whole_mine[CHUNK:]]
        near = [swap(m, 1) for m in mine]
        got = [swap(m, 2) for m in mine]
        blocks = [*mine, *near]
        results = run(blocks, 0)
        gate = results[0][-1] if meanwhile is None else meanwhile(blocks, results)
        through = []
        for c in range(2):
            pair = [after(got[c], gate)]
            pair.append(swap_pieces(pair[0]))
            done = run(pair, len(blocks))
            blocks, results = blocks + pair, results + done
            gate = done[0][-1] + swap_pieces(done[1][-1])
            if c > 0:
                through[0], gate = lax.optimization_barrier((through[0], gate))
            through.append(swap(gate, 2))
        sums = [
            results[c][-1].astype(F32) + swap(results[2 + c][-1], 1).astype(F32) + through[c].astype(F32) for c in range(2)
        ]
        return blocks, results, halves(*sums), gate

    lows, acts, branch, _ = feed(normed.astype(BF16), lambda blocks, n: up_down(blocks, w_up, bias, w_down))
    unit_two, inv_two = normalize(normed + branch + b_down)
    output = (unit_two * gain_two + shift_two).astype(BF16)
    grad_pre_out, grad_gain_two, grad_shift_two = norm_back(cotangent.astype(F32), gain_two, unit_two, inv_two)
    grad_b_down = jnp.sum(grad_pre_out, axis=0)
    grad_low = lax.optimization_barrier(grad_pre_out.astype(BF16))
    unit_low = lax.optimization_barrier(unit_one.astype(BF16))

    sums = []

    def weigh_own(grads, backs):
        blocks = [(acts[n][0], grads[n], lows[n], backs[n][0]) for n in range(4)]
        sums.extend(up_down_weights(at_own, blocks))
        return sums[0]

    grads, backs, back_normed, owed = feed(
        grad_low,
        lambda blocks, n: up_down_back([(b, acts[n + i][1]) for i, b in enumerate(blocks)], w_up, w_down),
        weigh_own,
    )
    blocks = [(acts[n][0], grads[n], lows[n], backs[n][0]) for n in range(4, 8)]
    blocks[0] = (after(blocks[0][0], owed), *blocks[0][1:])
    down_kept, down_sent, up_kept, up_sent, d_bias = up_down_weights(at_own, blocks, sums)
    back_normed = after(back_normed, down_sent, up_sent)
    down = Total(down_kept, down_sent, 0, "dp")
    up = Total(up_kept, up_sent, 1, "dp")
    grad_pre_norm, grad_gain_one, grad_shift_one = norm_back(
        grad_low.astype(F32) + back_normed, gain_one, unit_low.astype(F32), inv_one
    )
    grad_b_out = jnp.sum(grad_pre_norm, axis=0)
    top = lax.optimization_barrier(grad_pre_norm.astype(BF16))
    near = swap(top, 1)
    over = swap(top, 2)

    def values(at, mine, theirs, saved, prev=()):
        return attend_back_values(at, mine, theirs, sequences, taps_back, w_out, segments, saved, prev)

    def queries(at, saved, part, prev=()):
        return attend_back_queries(at, sequences, segments, marks, saved, part, prev)

    def both(*others):
        return down.step(*others), up.step(*others)

    norms = jnp.stack([grad_gain_one, grad_shift_one, grad_b_out, grad_gain_two, grad_shift_two, grad_b_down])
    own_v = values(after(at_own, *both(top)), top, near, own[4:])
    own_q = queries(after(at_own, *both(own_v[0])), own[4:], own_v[3:6])
    norms = norms + after(swap(norms, 1), own_q[0])
    far_v = values(after(at_far, own_q[0]), over, swap(over, 1), far[4:], own_v[0:2])
    norms = norms + after(swap(norms, 2), far_v[0])
    one = Total(far_v[0], far_v[1], 0, "dp")
    far_q = queries(after(at_far, *both(far_v[0])), far[4:], far_v[4:7], own_q[0:2])
    two = Total(far_q[0], far_q[1], 1, "dp")
    far_x = attend_back_tokens(at_far, (far_q[3], far_q[4], far_v[3]), (wq, wk, wv))
    owed = far_x[0] + swap(far_x[1], 1)
    through = swap(owed, 2)
    own_x = attend_back_tokens(at_own, (after(own_q[2], owed), own_q[3], own_v[2]), (wq, wk, wv))
    near = swap(own_x[1], 1)
    small = jnp.concatenate(
        [norms, d_bias[0:1], jnp.pad((far_v[2] + far_q[2])[0 : heads + 2], ((0, 0), (0, dim - WINDOW)))], axis=0
    )
    one.step(far_q[0])
    down.got, up.got, one.got, two.got = lax.optimization_barrier((down.got, up.got, one.got, two.got))
    for part in (two, one, up, down):
        part.step()
    mask = 1
    while mask < lax.axis_size("dp"):
        got = swap(small, mask, "dp")
        if mask == 1:
            got, one.got, two.got = lax.optimization_barrier((got, one.got, two.got))
            two.step()
            one.step()
            down.got, up.got, two.got = lax.optimization_barrier((down.got, up.got, two.got))
        elif mask == 2:
            got, one.got, two.got = lax.optimization_barrier((got, one.got, two.got))
            two.step()
            one.step()
        elif mask == 4:
            got, one.got, two.got, through = lax.optimization_barrier((got, one.got, two.got, through))
            two.step()
        small = small + got
        mask *= 2
    input_grad = top.astype(F32) + own_x[0].astype(F32) + near.astype(F32) + through.astype(F32)
    value_out = one.finish().astype(F32)
    query_key = two.finish().astype(F32)
    down_sum = down.finish().astype(F32)
    up_sum = up.finish().astype(F32)

    return (
        output,
        input_grad,
        query_key[0:width].T,
        query_key[width:].T,
        value_out[0:width].T,
        small[7 + heads, 0:width],
        small[8 + heads, 0:width],
        small[7 : 7 + heads, 0:CONV_TAPS],
        value_out[width:],
        small[2],
        small[0],
        small[1],
        up_sum,
        small[6, 0:units],
        down_sum,
        small[5],
        small[3],
        small[4],
    )


def solution(mesh):
    rows = P(("dp", "tensor"), None)
    columns = P(None, "tensor")
    split_rows = P("tensor", None)
    vector = P("tensor")
    return jax.shard_map(
        per_device,
        mesh=mesh,
        in_specs=(
            P("dp", None), columns, columns, columns, vector, vector, split_rows, split_rows, P(), P(), P(),
            columns, vector, split_rows, P(), P(), P(), rows, P("dp"), P("dp"),
        ),
        out_specs=(
            rows, rows, columns, columns, columns, vector, vector, split_rows, split_rows, P(), P(), P(),
            columns, vector, split_rows, P(), P(), P(),
        ),
        check_vma=False,
    )
```

```python
import functools

import jax
import jax.numpy as jnp
from jax import lax
from jax.experimental import pallas as pl
from jax.experimental.pallas import tpu as pltpu
from jax.sharding import PartitionSpec as P

HEAD_DIM = 64
LANDMARKS = 64
CONV_TAPS = 33
PINV_STEPS = 6
DOCS = 8
PER_DOC = LANDMARKS // DOCS
SEQ_LEN = 1024
EPSILON = 1e-05
SCALE = HEAD_DIM ** -0.5
HALF = CONV_TAPS // 2
BLOCK = 128
WINDOW = 256
CHUNK = 256
F32 = jnp.float32
BF16 = jnp.bfloat16
NN = (((1,), (0,)), ((), ()))
NT = (((1,), (1,)), ((), ()))
TN = (((0,), (0,)), ((), ()))


def takes(microseconds):
    return pl.CostEstimate(flops=int(microseconds * 1.1e9), bytes_accessed=1, transcendentals=0)


def mm(left, right, dims=NN):
    return lax.dot_general(left, right, dims, preferred_element_type=F32)


def split(value):
    high = value.astype(BF16)
    return high, (value - high.astype(F32)).astype(BF16)


def mm3(left, right, dims=NN):
    lh, ll = left
    rh, rl = right
    return mm(lh, rh, dims) + mm(ll, rh, dims) + mm(lh, rl, dims)


def iota(shape, dim):
    return lax.broadcasted_iota(jnp.int32, shape, dim)


def head_count(width):
    return width // HEAD_DIM


def block_mask(heads):
    shape = (heads * LANDMARKS, heads * HEAD_DIM)
    return iota(shape, 0) // LANDMARKS == iota(shape, 1) // HEAD_DIM


def spread(rows, heads):
    return jnp.where(block_mask(heads), jnp.concatenate([rows] * heads, axis=0), 0.0)


def fold(full, heads):
    return jnp.concatenate(
        [full[h * 64 : (h + 1) * 64, h * 64 : (h + 1) * 64] for h in range(heads)], axis=0
    )


def stack(rows, heads):
    return jnp.concatenate([rows[:, h * 64 : (h + 1) * 64] for h in range(heads)], axis=0)


def unstack(rows, heads):
    return jnp.concatenate([rows[h * 64 : (h + 1) * 64] for h in range(heads)], axis=1)


def block_diag(rows, heads):
    return jnp.where(block_mask(heads), jnp.concatenate([rows] * heads, axis=1), 0.0)


def doc_masks(segment):
    return [jnp.broadcast_to(segment == d, (PER_DOC, segment.shape[1])) for d in range(DOCS)]


def pick(full, masks, heads):
    out = []
    for h in range(heads):
        kept = jnp.zeros(masks[0].shape, F32)
        for d in range(DOCS):
            row = h * LANDMARKS + d * PER_DOC
            kept = jnp.where(masks[d], full[row : row + PER_DOC], kept)
        out.append(kept)
    return out


def place(compact, masks, heads):
    return jnp.concatenate(
        [jnp.where(masks[d], compact[h], 0.0) for h in range(heads) for d in range(DOCS)], axis=0
    )


def per_doc(rows, masks):
    out = jnp.zeros(masks[0].shape, F32)
    for d in range(DOCS):
        out = jnp.where(masks[d], rows[d * PER_DOC : (d + 1) * PER_DOC], out)
    return out


def rows_to_lanes(full, scratch, heads):
    rows = heads * LANDMARKS
    lane_doc = (iota((rows, 128), 1) // PER_DOC) % DOCS
    row_doc = (iota((rows, 128), 0) // PER_DOC) % DOCS
    kept = jnp.where(lane_doc == row_doc, full, 0.0)
    for shift in (8, 16, 32):
        kept = kept + pltpu.roll(kept, shift, 1)
    scratch[0:rows, :] = kept
    count = heads * DOCS
    group = iota((count, 128), 1) // PER_DOC
    out = jnp.zeros((count, 128), F32)
    for i in range(PER_DOC):
        out = jnp.where(group == i, scratch[pl.ds(i, count, stride=PER_DOC), :], out)
    return jnp.concatenate([out, jnp.zeros((128 - count, 128), F32)], axis=0).T[0:64]


def lanes_to_rows(blocks, heads):
    full = jnp.concatenate([blocks, jnp.zeros((64, 128), F32)], axis=0).T
    return full[0 : heads * DOCS]


def apply_blocks(coef, operand_ref, result_ref, heads, transposed):
    count = heads * DOCS
    pieces = [operand_ref[pl.ds(j, count, stride=PER_DOC), :] for j in range(PER_DOC)]
    for i in range(PER_DOC):
        total = jnp.zeros(pieces[0].shape, F32)
        for j in range(PER_DOC):
            k = j * PER_DOC + i if transposed else i * PER_DOC + j
            total = total + coef[:, k : k + 1] * pieces[j]
        result_ref[pl.ds(i, count, stride=PER_DOC), :] = total


def bm(left, right):
    a = left.reshape(8, 8, -1)
    b = right.reshape(8, 8, -1)
    total = a[:, 0:1] * b[0:1]
    for k in range(1, 8):
        total = total + a[:, k : k + 1] * b[k : k + 1]
    return total.reshape(64, -1)


def bm_tn(left, right):
    rows = []
    for i in range(8):
        total = left[i : i + 1] * right[0:8]
        for k in range(1, 8):
            total = total + left[k * 8 + i : k * 8 + i + 1] * right[k * 8 : k * 8 + 8]
        rows.append(total)
    return jnp.concatenate(rows, axis=0)


def flip(blocks, scratch):
    scratch[0:64, :] = blocks
    return jnp.concatenate([scratch[pl.ds(i, 8, stride=8), :] for i in range(8)], axis=0)


def lane_eye():
    row = iota((64, 128), 0)
    return jnp.where(row // 8 == row % 8, 1.0, 0.0)


def column_sums(blocks):
    total = blocks[0:8]
    for i in range(1, 8):
        total = total + blocks[i * 8 : i * 8 + 8]
    return total


def row_sums(blocks):
    return jnp.concatenate(
        [jnp.sum(blocks[i * 8 : i * 8 + 8], axis=0, keepdims=True) for i in range(8)], axis=0
    )


def head_lanes(h):
    return iota((8, 128), 1) // DOCS == h


def head_most(sums, heads):
    out = jnp.ones((1, 128), F32)
    for h in range(heads):
        mask = head_lanes(h)
        most = jnp.max(jnp.max(jnp.where(mask, sums, -1e30), axis=1, keepdims=True), axis=0, keepdims=True)
        out = jnp.where(mask[0:1], most, out)
    return out


def head_total(values, heads):
    out = jnp.zeros((1, 128), F32)
    for h in range(heads):
        mask = head_lanes(h)
        total = jnp.sum(jnp.sum(jnp.where(mask, values, 0.0), axis=1, keepdims=True), axis=0, keepdims=True)
        out = jnp.where(mask[0:1], total, out)
    return out


def same_document(segment, seg_pad, start):
    rows = jnp.broadcast_to(segment[:, start : start + BLOCK], (BLOCK, BLOCK)).T
    return jnp.concatenate([rows, rows], axis=1) == seg_pad[0:1, start : start + WINDOW]


def toeplitz(taps_ref, h, scratch):
    scratch[0:8, 0:WINDOW] = jnp.zeros((8, WINDOW), F32)
    scratch[0:1, 0:CONV_TAPS] = taps_ref[h : h + 1, :]
    taps_row = scratch[0:1, 0:WINDOW]
    return pltpu.roll(jnp.broadcast_to(taps_row, (BLOCK, WINDOW)), 0, 1, stride=1, stride_axis=0)


def pad_segment(seg_pad, segment):
    seg_pad[:, 0:128] = jnp.zeros((8, 128), F32)
    seg_pad[:, 0:SEQ_LEN] = jnp.broadcast_to(pltpu.roll(segment, HALF, 1), (8, SEQ_LEN))
    seg_pad[:, SEQ_LEN:] = jnp.broadcast_to(segment[:, SEQ_LEN - 1 : SEQ_LEN], (8, WINDOW))


def attend_forward_kernel(
    where_ref, tokens_ref, wq_ref, wk_ref, wv_ref, bq_ref, bv_ref, taps_ref, w_out_ref, seg_ref, mark_ref,
    keep_a_ref, keep_b_ref, send_a_ref, send_b_ref, q_ref, k_ref, v_ref, att_ref, p1_ref, p3_ref, qm_ref, km_ref, ctx_ref, bl_ref, count_ref, mid_ref, steps_ref, inverse_ref,
    padded, seg_pad, scratch, band,
):
    width = wq_ref.shape[0]
    heads = head_count(width)
    tokens = tokens_ref.at[0]
    rows = 256

    def project(i, carry):
        at = pl.ds(pl.multiple_of(i * rows, rows), rows)
        x = tokens[at, :]
        q_ref[at, :] = (mm(x, wq_ref[...], NT) + bq_ref[...]).astype(BF16)
        k_ref[at, :] = mm(x, wk_ref[...], NT).astype(BF16)
        value = (mm(x, wv_ref[...], NT) + bv_ref[...]).astype(BF16)
        v_ref[at, :] = value
        padded[pl.ds(pl.multiple_of(i * rows + HALF, 16), rows), :] = value
        return carry

    padded[0:HALF, :] = jnp.zeros((HALF, width), BF16)
    padded[SEQ_LEN + HALF :, :] = jnp.zeros((WINDOW - HALF, width), BF16)
    lax.fori_loop(0, SEQ_LEN // rows, project, 0)

    segment = seg_ref[0].astype(F32)
    masks = doc_masks(segment)
    one_hot = mark_ref[0] == iota((LANDMARKS, SEQ_LEN), 0)
    counts = jnp.sum(one_hot.astype(F32), axis=1, keepdims=True)
    pool = one_hot.astype(BF16)
    q_marks = mm(pool, q_ref[...]) / counts
    k_marks = mm(pool, k_ref[...]) / counts
    count_ref[...] = jnp.broadcast_to(counts, (LANDMARKS, 128))
    qm_ref[...] = q_marks
    km_ref[...] = k_marks
    k_block = split(spread(k_marks, heads))
    q_wide = spread(q_marks, heads)
    q_block = split(q_wide)

    queries = q_ref[...]
    scores = pick(mm(k_block[0], queries, NT) + mm(k_block[1], queries, NT), masks, heads)
    first = []
    for h in range(heads):
        s = scores[h] * SCALE
        e = jnp.exp(s - jnp.max(s, axis=0, keepdims=True))
        first.append(e / jnp.sum(e, axis=0, keepdims=True))
    p1_ref[...] = jnp.concatenate(first, axis=0)

    keys = k_ref[...]
    scores = pick(mm(q_block[0], keys, NT) + mm(q_block[1], keys, NT), masks, heads)
    last = []
    for h in range(heads):
        s = scores[h] * SCALE
        most = jnp.concatenate(
            [jnp.max(jnp.where(masks[d], s, -1e30), axis=1, keepdims=True) for d in range(DOCS)], axis=0
        )
        e = jnp.exp(s - per_doc(most, masks))
        total = jnp.concatenate(
            [jnp.sum(jnp.where(masks[d], e, 0.0), axis=1, keepdims=True) for d in range(DOCS)], axis=0
        )
        last.append(e / per_doc(total, masks))
    p3_ref[...] = jnp.concatenate(last, axis=0)

    weights = split(place(last, masks, heads))
    values = v_ref[...]
    context = fold(mm(weights[0], values) + mm(weights[1], values), heads)
    ctx_ref[...] = context

    twice = jnp.concatenate([k_marks, k_marks], axis=0)
    grid = lax.dot_general(q_wide, twice, NT, precision=lax.Precision.HIGHEST, preferred_element_type=F32)
    scores = (rows_to_lanes(grid, scratch, heads) * SCALE).reshape(8, 8, 128)
    e = jnp.exp(scores - jnp.max(scores, axis=1, keepdims=True))
    middle = (e / jnp.sum(e, axis=1, keepdims=True)).reshape(64, 128)
    used = iota((64, 128), 1) < heads * DOCS
    middle = jnp.where(used, middle, 0.0)
    mid_ref[...] = middle
    norm = head_most(column_sums(middle), heads) * head_most(row_sums(middle), heads)
    eye = lane_eye()

    def step(n, inverse):
        product = bm(middle, inverse)
        second = 15.0 * eye - bm(product, 7.0 * eye - product)
        third = 13.0 * eye - bm(product, second)
        steps_ref[n, 0] = inverse
        steps_ref[n, 1] = product
        steps_ref[n, 2] = second
        steps_ref[n, 3] = third
        return 0.25 * bm(inverse, third)

    inverse = lax.fori_loop(0, PINV_STEPS, step, flip(middle, scratch) / norm)
    inverse_ref[...] = inverse
    coef = lanes_to_rows(inverse, heads)
    apply_blocks(coef, ctx_ref, bl_ref, heads, False)
    blended = split(block_diag(bl_ref[...], heads))
    weights = split(place(first, masks, heads))
    attended = mm3(weights, blended, TN)

    for h in range(heads):
        band[h] = toeplitz(taps_ref, h, seg_pad).astype(BF16)
    pad_segment(seg_pad, segment)
    att_ref[...] = attended.astype(BF16)
    lane_head = iota((BLOCK, width), 1) // HEAD_DIM
    scratch_f = attended

    for b in range(SEQ_LEN // BLOCK):
        start = b * BLOCK
        rows_at = pl.ds(start, BLOCK)
        same = same_document(segment, seg_pad, start)
        window = padded[pl.ds(start, WINDOW), :]
        total = scratch_f[start : start + BLOCK]
        for h in range(heads):
            part = mm(jnp.where(same, band[h], 0), window)
            total = total + jnp.where(lane_head == h, part, 0.0)
        att_ref[rows_at, :] = total.astype(BF16)

    half = SEQ_LEN // 2
    core = where_ref[1]
    weight = w_out_ref[...]
    for base, refs in ((core, (keep_a_ref, keep_b_ref)), (1 - core, (send_a_ref, send_b_ref))):
        for i, ref in enumerate(refs):
            at = pl.ds(pl.multiple_of(base * half + i * CHUNK, CHUNK), CHUNK)
            ref[...] = mm(att_ref[at, :], weight).astype(BF16)


def attend_forward(where, tokens, wq, wk, wv, bq, bv, taps, w_out, segments, marks):
    dim = tokens.shape[2]
    width = wq.shape[0]
    heads = head_count(width)

    def whole(*shape):
        return pl.BlockSpec(shape, lambda i, w: (0,) * len(shape))

    def one(*shape):
        return pl.BlockSpec((1,) + shape, lambda i, w: (w[0],) + (0,) * len(shape))

    outs = [
        *[((CHUNK, dim), BF16)] * 4,
        ((SEQ_LEN, width), BF16), ((SEQ_LEN, width), BF16), ((SEQ_LEN, width), BF16), ((SEQ_LEN, width), BF16),
        ((heads * 8, SEQ_LEN), F32), ((heads * 8, SEQ_LEN), F32),
        ((LANDMARKS, width), F32), ((LANDMARKS, width), F32),
        ((heads * LANDMARKS, HEAD_DIM), F32), ((heads * LANDMARKS, HEAD_DIM), F32),
        ((LANDMARKS, 128), F32), ((64, 128), F32), ((PINV_STEPS, 4, 64, 128), F32), ((64, 128), F32),
    ]
    return pl.pallas_call(
        attend_forward_kernel,
        out_shape=[jax.ShapeDtypeStruct(s, t) for s, t in outs],
        grid_spec=pltpu.PrefetchScalarGridSpec(
            num_scalar_prefetch=1,
            grid=(1,),
            in_specs=[
                one(SEQ_LEN, dim), whole(width, dim), whole(width, dim), whole(width, dim), whole(1, width), whole(1, width),
                whole(heads, CONV_TAPS), whole(width, dim), one(1, SEQ_LEN), one(1, SEQ_LEN),
            ],
            out_specs=[whole(*s) for s, t in outs],
            scratch_shapes=[
                pltpu.VMEM((SEQ_LEN + WINDOW, width), BF16),
                pltpu.VMEM((8, SEQ_LEN + WINDOW), F32),
                pltpu.VMEM((heads * LANDMARKS, 128), F32),
                pltpu.VMEM((heads, BLOCK, WINDOW), BF16),
            ],
        ),
        compiler_params=pltpu.CompilerParams(vmem_limit_bytes=56 << 20),
        cost_estimate=takes(12),
    )(where, tokens, wq, wk, wv, bq, bv, taps, w_out, segments, marks)


def diagonal_sums(band):
    row = iota(band.shape, 0)
    for bit in range(7):
        shift = 1 << bit
        moved = pltpu.roll(band, WINDOW - shift, 1)
        band = jnp.where((row // shift) % 2 == 1, moved, band)
    return jnp.sum(band, axis=0, keepdims=True)


def plus(ref, at, value):
    return value if ref is None else ref[at] + value


def sums_refs(final, where_ref, refs, turn):
    if not final:
        weights_ref, *refs = refs
        return None, None, weights_ref, refs, lambda: None
    prev_ref, prev_small_ref, kept_ref, sent_ref, *refs = refs
    *refs, weights_ref = refs

    def finish():
        half = kept_ref.shape[0]
        bit = where_ref[2 + turn]
        kept_ref[...] = weights_ref[pl.ds(pl.multiple_of(bit * half, half), half), :]
        sent_ref[...] = weights_ref[pl.ds(pl.multiple_of((1 - bit) * half, half), half), :].astype(BF16)

    return prev_ref, prev_small_ref, weights_ref, refs, finish


def attend_back_values_kernel(
    final, where_ref, mine_ref, theirs_ref, tokens_ref, taps_ref, w_out_ref, seg_ref,
    v_ref, att_ref, p1_ref, p3_ref, ctx_ref, bl_ref, inverse_ref, *refs
):
    prev_ref, prev_small_ref, weights_ref, refs, finish = sums_refs(final, where_ref, refs, 0)
    small_ref, dv_ref, ds1_ref, ds3_ref, dbl_ref, dctx_ref, grad_ref, up_ref, value_ref, seg_pad, band, corr = refs
    width = v_ref.shape[1]
    heads = head_count(width)
    half = SEQ_LEN // 2
    core = where_ref[1]

    grad_ref[0:HALF, :] = jnp.zeros((HALF, width), BF16)
    grad_ref[SEQ_LEN + HALF :, :] = jnp.zeros((WINDOW - HALF, width), BF16)
    value_ref[0:HALF, :] = jnp.zeros((HALF, width), BF16)
    value_ref[SEQ_LEN + HALF :, :] = jnp.zeros((WINDOW - HALF, width), BF16)
    value_ref[HALF : SEQ_LEN + HALF, :] = v_ref[...]
    for base, ref in ((core, mine_ref), (1 - core, theirs_ref)):
        for i in range(half // CHUNK):
            at = pl.ds(i * CHUNK, CHUNK)
            to = pl.multiple_of(base * half + i * CHUNK, CHUNK)
            up_ref[pl.ds(to, CHUNK), :] = ref[at, :]
            grad_ref[pl.ds(pl.multiple_of(to + HALF, HALF), CHUNK), :] = mm(ref[at, :], w_out_ref[...], NT).astype(BF16)
    at = (slice(width, 2 * width), slice(None))
    weights_ref[at] = plus(prev_ref, at, mm(att_ref[...], up_ref[...], TN))

    segment = seg_ref[0].astype(F32)
    masks = doc_masks(segment)
    first = [p1_ref[h * 8 : h * 8 + 8, :] for h in range(heads)]
    last = [p3_ref[h * 8 : h * 8 + 8, :] for h in range(heads)]
    gradient = grad_ref[HALF : SEQ_LEN + HALF, :]
    values = v_ref[...]

    first_wide = split(place(first, masks, heads))
    dbl = fold(mm(first_wide[0], gradient) + mm(first_wide[1], gradient), heads)
    dbl_ref[...] = dbl
    blended = split(block_diag(bl_ref[...], heads))
    dfirst = pick(mm(blended[0], gradient, NT) + mm(blended[1], gradient, NT), masks, heads)
    for h in range(heads):
        ds1_ref[h * 8 : h * 8 + 8, :] = (
            SCALE * first[h] * (dfirst[h] - jnp.sum(first[h] * dfirst[h], axis=0, keepdims=True))
        )

    apply_blocks(lanes_to_rows(inverse_ref[...], heads), dbl_ref, dctx_ref, heads, True)
    dctx = dctx_ref[...]
    dctx_wide = split(block_diag(dctx, heads))
    dlast = pick(mm(dctx_wide[0], values, NT) + mm(dctx_wide[1], values, NT), masks, heads)
    inner = jnp.sum(dctx * ctx_ref[...], axis=1, keepdims=True)
    for h in range(heads):
        ds3_ref[h * 8 : h * 8 + 8, :] = (
            SCALE * last[h] * (dlast[h] - per_doc(inner[h * 64 : (h + 1) * 64], masks))
        )
    last_wide = place(last, masks, heads).astype(BF16)
    dvalue = mm(last_wide, dctx_wide[0], TN) + mm(last_wide, dctx_wide[1], TN)

    for h in range(heads):
        band[h] = toeplitz(taps_ref, h, seg_pad).astype(BF16)
        corr[h] = jnp.zeros((BLOCK, WINDOW), F32)
    pad_segment(seg_pad, segment)
    lane_head = iota((BLOCK, width), 1) // HEAD_DIM
    for b in range(SEQ_LEN // BLOCK):
        begin = b * BLOCK
        same = same_document(segment, seg_pad, begin)
        window = grad_ref[begin : begin + WINDOW, :]
        near = value_ref[begin : begin + WINDOW, :]
        block = grad_ref[begin + HALF : begin + HALF + BLOCK, :]
        total = dvalue[begin : begin + BLOCK]
        for h in range(heads):
            taps = jnp.where(same, band[h], 0)
            part = mm(taps, window)
            total = total + jnp.where(lane_head == h, part, 0.0)
            mine = lane_head == h
            part = mm(jnp.where(mine, block, 0), near, NT)
            corr[h] = corr[h] + jnp.where(same, part, 0.0)
        dv_ref[begin : begin + BLOCK, :] = total.astype(BF16)

    small_ref[...] = jnp.zeros(small_ref.shape, F32)
    for h in range(heads):
        at = (slice(h, h + 1), slice(None))
        small_ref[at] = plus(prev_small_ref, at, diagonal_sums(corr[h]))
    at = (slice(heads + 1, heads + 2), slice(0, width))
    small_ref[at] = plus(prev_small_ref, at, jnp.sum(dv_ref[...].astype(F32), axis=0, keepdims=True))
    at = (slice(0, width), slice(None))
    weights_ref[at] = plus(prev_ref, at, mm(dv_ref[...], tokens_ref[0], TN))
    finish()


def attend_back_queries_kernel(
    final, where_ref, tokens_ref, seg_ref, mark_ref,
    q_ref, k_ref, qm_ref, km_ref, ctx_ref, count_ref, mid_ref, steps_ref, ds1_ref, ds3_ref, dbl_ref, *refs
):
    prev_ref, prev_small_ref, weights_ref, refs, finish = sums_refs(final, where_ref, refs, 1)
    small_ref, dq_ref, dk_ref, scratch, scratch_b, dqm_ref, dkm_ref, stack_ref = refs
    width = q_ref.shape[1]
    heads = head_count(width)
    masks = doc_masks(seg_ref[0].astype(F32))
    pool = (mark_ref[0] == iota((LANDMARKS, SEQ_LEN), 0)).astype(BF16)
    queries = q_ref[...]
    keys = k_ref[...]
    dscore_one = split(place([ds1_ref[h * 8 : h * 8 + 8, :] for h in range(heads)], masks, heads))
    dscore_last = split(place([ds3_ref[h * 8 : h * 8 + 8, :] for h in range(heads)], masks, heads))
    dkm = fold(mm(dscore_one[0], queries) + mm(dscore_one[1], queries), heads)
    dqm = fold(mm(dscore_last[0], keys) + mm(dscore_last[1], keys), heads)

    context = unstack(ctx_ref[...], heads)
    grid = lax.dot_general(
        block_diag(dbl_ref[...], heads), jnp.concatenate([context, context], axis=0), NT,
        precision=lax.Precision.HIGHEST, preferred_element_type=F32,
    )
    dinverse = rows_to_lanes(grid, scratch, heads)
    middle = mid_ref[...]
    eye = lane_eye()

    def step(n, carry):
        dz, dmid = carry
        n = PINV_STEPS - 1 - n
        z = steps_ref[n, 0]
        product = steps_ref[n, 1]
        second = steps_ref[n, 2]
        third = steps_ref[n, 3]
        dthird = 0.25 * bm_tn(z, dz)
        dz_next = 0.25 * bm(dz, flip(third, scratch_b.at[0]))
        dsecond = -bm_tn(product, dthird)
        dprod = -bm(dthird, flip(second, scratch_b.at[1])) - bm(dsecond, flip(7.0 * eye - product, scratch_b.at[2]))
        dprod = dprod + bm_tn(product, dsecond)
        dmid = dmid + bm(dprod, flip(z, scratch_b.at[3]))
        dz_next = dz_next + bm_tn(middle, dprod)
        return dz_next, dmid

    dz, dmid = lax.fori_loop(0, PINV_STEPS, step, (dinverse, jnp.zeros((64, 128), F32)))
    columns = column_sums(middle)
    across = row_sums(middle)
    column_most = head_most(columns, heads)
    row_most = head_most(across, heads)
    start = flip(middle, scratch) / (column_most * row_most)
    dmid = dmid + flip(dz, scratch) / (column_most * row_most)
    total = jnp.sum(dz * start, axis=0, keepdims=True)
    total = head_total(jnp.where(iota((8, 128), 0) == 0, jnp.broadcast_to(total, (8, 128)), 0.0), heads)
    hit = jnp.where(columns == column_most, 1.0, 0.0)
    dcolumns = -total / column_most * hit / jnp.maximum(head_total(hit, heads), 1.0)
    hit = jnp.where(across == row_most, 1.0, 0.0)
    drows = -total / row_most * hit / jnp.maximum(head_total(hit, heads), 1.0)
    dmid = dmid + jnp.concatenate([dcolumns + drows[i : i + 1] for i in range(8)], axis=0)
    dgrid = jnp.concatenate(
        [
            SCALE * middle[i * 8 : i * 8 + 8]
            * (dmid[i * 8 : i * 8 + 8] - jnp.sum(middle[i * 8 : i * 8 + 8] * dmid[i * 8 : i * 8 + 8], axis=0, keepdims=True))
            for i in range(8)
        ],
        axis=0,
    )
    coef = lanes_to_rows(dgrid, heads)
    q_stack = stack(qm_ref[...], heads)
    k_stack = stack(km_ref[...], heads)
    stack_ref[...] = k_stack
    apply_blocks(coef, stack_ref, dqm_ref, heads, False)
    stack_ref[...] = q_stack
    apply_blocks(coef, stack_ref, dkm_ref, heads, True)

    dqm = dqm + dqm_ref[...]
    dkm = dkm + dkm_ref[...]
    counts = count_ref[:, 0:1]
    dqm = split(unstack(dqm, heads) / counts)
    dkm = split(unstack(dkm, heads) / counts)
    k_wide = split(spread(km_ref[...], heads))
    q_wide = split(spread(qm_ref[...], heads))

    def pulled(scores, wide, marks):
        left = jnp.concatenate([scores[0], pool], axis=0)
        return mm(left, jnp.concatenate([wide[0], marks[0]], axis=0), TN) + mm(
            left, jnp.concatenate([wide[1], marks[1]], axis=0), TN
        )

    dq_ref[...] = pulled(dscore_one, k_wide, dqm).astype(BF16)
    dk_ref[...] = pulled(dscore_last, q_wide, dkm).astype(BF16)

    small_ref[...] = jnp.zeros(small_ref.shape, F32)
    at = (slice(heads, heads + 1), slice(0, width))
    small_ref[...] = plus(prev_small_ref, (slice(None), slice(None)), small_ref[...])
    small_ref[at] = plus(prev_small_ref, at, jnp.sum(dq_ref[...].astype(F32), axis=0, keepdims=True))
    tokens = tokens_ref[0]
    for n, ref in enumerate((dq_ref, dk_ref)):
        at = (slice(n * width, (n + 1) * width), slice(None))
        weights_ref[at] = plus(prev_ref, at, mm(ref[...], tokens, TN))
    finish()


def attend_back_tokens_kernel(where_ref, *refs):
    ins, weights, outs = refs[:6], [ref[...] for ref in refs[6:9]], refs[9:]
    for n in range(2):
        outs[n][...] = sum(mm(ref[...], w) for ref, w in zip(ins[3 * n : 3 * n + 3], weights)).astype(BF16)


def attend_back_tokens(where, parts, weights):
    width, dim = weights[0].shape
    step = 256
    count = SEQ_LEN // 2 // step

    def rows(near):
        def at(i, w):
            return ((w[1] if near else 1 - w[1]) * count + i, 0)

        return pl.BlockSpec((step, width), at)

    return pl.pallas_call(
        attend_back_tokens_kernel,
        out_shape=[jax.ShapeDtypeStruct((SEQ_LEN // 2, dim), BF16)] * 2,
        grid_spec=pltpu.PrefetchScalarGridSpec(
            num_scalar_prefetch=1,
            grid=(count,),
            in_specs=[rows(True)] * 3 + [rows(False)] * 3 + [pl.BlockSpec((width, dim), lambda i, w: (0, 0))] * 3,
            out_specs=[pl.BlockSpec((step, dim), lambda i, w: (i, 0))] * 2,
        ),
        compiler_params=pltpu.CompilerParams(vmem_limit_bytes=40 << 20),
        cost_estimate=takes(3),
    )(where, *parts, *parts, *weights)


def whole(shape):
    return pl.BlockSpec(shape, lambda i, w: (0,) * len(shape))


def chosen(shape):
    return pl.BlockSpec((1,) + shape, lambda i, w: (w[0],) + (0,) * len(shape))


def sums_outs(width, dim, final):
    return [((width, dim), F32), ((width, dim), BF16)] if final else [((2 * width, dim), F32)]


def back_call(kernel, where, ins, specs, outs, scratch, final):
    return pl.pallas_call(
        kernel,
        out_shape=[jax.ShapeDtypeStruct(s, t) for s, t in outs],
        grid_spec=pltpu.PrefetchScalarGridSpec(
            num_scalar_prefetch=1, grid=(1,), in_specs=specs, out_specs=[whole(s) for s, t in outs], scratch_shapes=scratch
        ),
        compiler_params=pltpu.CompilerParams(vmem_limit_bytes=56 << 20),
        cost_estimate=takes(0.1 if final else 11),
    )(where, *ins)


def attend_back_values(where, mine, theirs, tokens, taps, w_out, segments, saved, prev=()):
    dim = tokens.shape[2]
    q, k, v, att, p1, p3, qm, km, ctx, bl, count, mid, steps, inverse = saved
    width = v.shape[1]
    heads = head_count(width)
    final = len(prev) > 0
    rest = (v, att, p1, p3, ctx, bl, inverse, *prev)
    specs = [
        whole(mine.shape), whole(theirs.shape), chosen((SEQ_LEN, dim)), whole(taps.shape), whole(w_out.shape), chosen((1, SEQ_LEN)),
        *[whole(x.shape) for x in rest],
    ]
    outs = [
        *sums_outs(width, dim, final), ((8, WINDOW), F32), ((SEQ_LEN, width), BF16), (p1.shape, F32), (p3.shape, F32),
        (bl.shape, F32), (ctx.shape, F32),
    ]
    scratch = [
        pltpu.VMEM((SEQ_LEN + WINDOW, width), BF16),
        pltpu.VMEM((SEQ_LEN, dim), BF16),
        pltpu.VMEM((SEQ_LEN + WINDOW, width), BF16),
        pltpu.VMEM((8, SEQ_LEN + WINDOW), F32),
        pltpu.VMEM((heads, BLOCK, WINDOW), BF16),
        pltpu.VMEM((heads, BLOCK, WINDOW), F32),
        *([pltpu.VMEM((2 * width, dim), F32)] if final else []),
    ]
    kernel = functools.partial(attend_back_values_kernel, final)
    return back_call(kernel, where, (mine, theirs, tokens, taps, w_out, segments, *rest), specs, outs, scratch, final)


def attend_back_queries(where, tokens, segments, marks, saved, part, prev=()):
    dim = tokens.shape[2]
    q, k, v, att, p1, p3, qm, km, ctx, bl, count, mid, steps, inverse = saved
    ds1, ds3, dbl = part
    width = q.shape[1]
    heads = head_count(width)
    final = len(prev) > 0
    rest = (q, k, qm, km, ctx, count, mid, steps, ds1, ds3, dbl, *prev)
    specs = [chosen((SEQ_LEN, dim)), chosen((1, SEQ_LEN)), chosen((1, SEQ_LEN)), *[whole(x.shape) for x in rest]]
    outs = [*sums_outs(width, dim, final), ((8, WINDOW), F32), ((SEQ_LEN, width), BF16), ((SEQ_LEN, width), BF16)]
    scratch = [
        pltpu.VMEM((heads * LANDMARKS, 128), F32),
        pltpu.VMEM((4, 64, 128), F32),
        *[pltpu.VMEM((heads * LANDMARKS, HEAD_DIM), F32)] * 3,
        *([pltpu.VMEM((2 * width, dim), F32)] if final else []),
    ]
    kernel = functools.partial(attend_back_queries_kernel, final)
    return back_call(kernel, where, (tokens, segments, marks, *rest), specs, outs, scratch, final)


ERFC = (
    0.12694266047513267, 0.12694157407364748, 0.11413597639508828, 0.08762459251766126, 0.05998263605520133,
    -0.01120062503236582, 0.07123816174906503, -0.1503297151041413, 0.09536518640917925, -0.020700440227622966,
)


def normal_cdf(value):
    size = jnp.abs(value)
    t = 1.0 / (1.0 + 0.31819805153394637 * size)
    poly = ERFC[-1]
    for coef in ERFC[-2::-1]:
        poly = poly * t + coef
    bell = jnp.exp(-0.5 * size * size)
    tail = bell * (t * poly)
    return jnp.where(value > 0.0, 1.0 - tail, tail), bell


def up_down_kernel(*refs):
    count = (len(refs) - 3) // 4
    w_up_ref, b_up_ref, w_down_ref = refs[count : count + 3]
    outs = refs[count + 3 :]
    for n in range(count):
        act_ref, slope_ref, part_ref = outs[3 * n : 3 * n + 3]
        hidden = mm(refs[n][...], w_up_ref[...]) + b_up_ref[...]
        below, bell = normal_cdf(hidden)
        act = (hidden * below).astype(BF16)
        act_ref[...] = act
        slope_ref[...] = (below + hidden * (bell * 0.3989422804014327)).astype(BF16)
        part_ref[...] = mm(act, w_down_ref[...]).astype(BF16)


def fixed(*shape):
    return pl.BlockSpec(shape, lambda i: (0,) * len(shape), pipeline_mode=pl.Buffered(1))


def strip(rows, width):
    return pl.BlockSpec((rows, width), lambda i: (i, 0))


def up_down(blocks, w_up, b_up, w_down):
    rows, dim = blocks[0].shape
    units = w_up.shape[1]
    step = 128
    total = rows * len(blocks)
    out = pl.pallas_call(
        up_down_kernel,
        out_shape=[jax.ShapeDtypeStruct((rows, w), BF16) for w in (units, units, dim)] * len(blocks),
        grid=(rows // step,),
        in_specs=[strip(step, dim)] * len(blocks) + [fixed(dim, units), fixed(1, units), fixed(units, dim)],
        out_specs=[strip(step, units), strip(step, units), strip(step, dim)] * len(blocks),
        compiler_params=pltpu.CompilerParams(vmem_limit_bytes=40 << 20),
        cost_estimate=takes(total * 0.007),
    )(*blocks, w_up, b_up, w_down)
    return [out[3 * n : 3 * n + 3] for n in range(len(blocks))]


def up_down_back_kernel(*refs):
    count = (len(refs) - 2) // 4
    w_up_ref, w_down_ref = refs[2 * count : 2 * count + 2]
    outs = refs[2 * count + 2 :]
    for n in range(count):
        grad_ref, slope_ref = refs[2 * n : 2 * n + 2]
        hidden = (mm(grad_ref[...], w_down_ref[...], NT) * slope_ref[...].astype(F32)).astype(BF16)
        outs[2 * n][...] = hidden
        outs[2 * n + 1][...] = mm(hidden, w_up_ref[...], NT).astype(BF16)


def up_down_back(pairs, w_up, w_down):
    rows, dim = pairs[0][0].shape
    units = w_up.shape[1]
    step = 128
    total = rows * len(pairs)
    out = pl.pallas_call(
        up_down_back_kernel,
        out_shape=[jax.ShapeDtypeStruct((rows, w), BF16) for w in (units, dim)] * len(pairs),
        grid=(rows // step,),
        in_specs=[strip(step, dim), strip(step, units)] * len(pairs) + [fixed(dim, units), fixed(units, dim)],
        out_specs=[strip(step, units), strip(step, dim)] * len(pairs),
        compiler_params=pltpu.CompilerParams(vmem_limit_bytes=40 << 20),
        cost_estimate=takes(total * 0.007),
    )(*[x for pair in pairs for x in pair], w_up, w_down)
    return [out[2 * n : 2 * n + 2] for n in range(len(pairs))]


def up_down_weights_kernel(final, bits_ref, *refs):
    outs = refs[-7:] if final else refs[-3:]
    ins = refs[: len(refs) - len(outs)]
    prev, ins = (ins[-3:], ins[:-3]) if final else ((), ins)
    down_ref, up_ref = outs[-2:] if final else outs[:2]
    bias_ref = outs[4] if final else outs[2]

    @pl.when(pl.program_id(0) == 0)
    def _():
        for n, ref in enumerate((down_ref, up_ref, bias_ref)):
            ref[...] = prev[n][...] if final else jnp.zeros(ref.shape, F32)

    for n in range(len(ins) // 4):
        act_ref, grad_ref, low_ref, hidden_ref = ins[4 * n : 4 * n + 4]
        hidden = hidden_ref[...]
        down_ref[...] += mm(act_ref[...], grad_ref[...], TN)
        up_ref[...] += mm(low_ref[...], hidden, TN)
        bias_ref[0:1, :] += jnp.sum(hidden.astype(F32), axis=0, keepdims=True)

    if final:

        @pl.when(pl.program_id(0) == pl.num_programs(0) - 1)
        def _():
            for n, ref in enumerate((down_ref, up_ref)):
                half = ref.shape[0] // 2
                bit = bits_ref[2 + n]
                outs[2 * n][...] = ref[pl.ds(pl.multiple_of(bit * half, half), half), :]
                outs[2 * n + 1][...] = ref[pl.ds(pl.multiple_of((1 - bit) * half, half), half), :].astype(BF16)


def up_down_weights(bits, blocks, prev=()):
    rows, units = blocks[0][0].shape
    dim = blocks[0][1].shape[1]
    step = 256
    final = len(prev) > 0
    sums = [((units, dim), F32), ((dim, units), F32)]
    outs = sums
    if final:
        outs = [o for (r, c), t in sums for o in (((r // 2, c), F32), ((r // 2, c), BF16))]
    outs = [*outs, ((8, units), F32)]

    def strips(width):
        return pl.BlockSpec((step, width), lambda i, w: (i, 0))

    def once(shape):
        return pl.BlockSpec(shape, lambda i, w: (0, 0), pipeline_mode=pl.Buffered(1))

    return pl.pallas_call(
        functools.partial(up_down_weights_kernel, final),
        out_shape=[jax.ShapeDtypeStruct(s, t) for s, t in outs],
        grid_spec=pltpu.PrefetchScalarGridSpec(
            num_scalar_prefetch=1,
            grid=(rows // step,),
            in_specs=[strips(units), strips(dim), strips(dim), strips(units)] * len(blocks) + [once(p.shape) for p in prev],
            out_specs=[once(s) for s, t in outs],
            scratch_shapes=[pltpu.VMEM(s, t) for s, t in sums] if final else [],
        ),
        compiler_params=pltpu.CompilerParams(vmem_limit_bytes=40 << 20),
        cost_estimate=takes(5),
    )(bits, *[x for block in blocks for x in block], *prev)


def swap(value, mask, axis="tensor"):
    count = lax.axis_size(axis)
    return lax.ppermute(value, axis, [(i, i ^ mask) for i in range(count)])


class Total:
    def __init__(self, kept, sent, first, axis):
        masks = [1 << n for n in range(lax.axis_size(axis).bit_length() - 1)]
        masks.insert(0, masks.pop(first))
        self.order = masks + masks[-2::-1]
        self.count = len(masks)
        self.axis = axis
        self.index = lax.axis_index(axis)
        self.kept = kept
        self.level = 0
        self.begin(sent)

    def bit(self, n):
        return ((self.index & self.order[n]) != 0).astype(jnp.int32)

    def begin(self, sent):
        self.sent = sent
        self.got = swap(sent, self.order[self.level], self.axis)
        self.level += 1

    def step(self, *others):
        got = after(self.got, *others)
        if self.level < self.count - 1:
            half = got.shape[0] // 2
            bit = self.bit(self.level)

            def rows(which):
                at = which * half
                kept = lax.dynamic_slice_in_dim(self.kept, at, half, 0)
                return kept + lax.dynamic_slice_in_dim(got, at, half, 0).astype(F32)

            sent = rows(1 - bit).astype(BF16)
            self.kept = rows(bit)
        elif self.level == self.count - 1:
            sent = self.kept = (self.kept + got.astype(F32)).astype(BF16)
        elif self.level == self.count:
            sent = self.kept = (self.kept.astype(F32) + got.astype(F32)).astype(BF16)
        else:
            bit = self.bit(self.level - 1) > 0
            sent = self.kept = jnp.concatenate([jnp.where(bit, got, self.kept), jnp.where(bit, self.kept, got)], axis=0)
        if self.level < len(self.order):
            self.begin(sent)
        return sent

    def finish(self):
        while self.level < len(self.order):
            self.step()
        return self.step()


def swap_pieces(value):
    step = value.shape[0] // 4
    return jnp.concatenate([swap(value[n * step : (n + 1) * step], 1) for n in range(4)], axis=0)


def after(value, *others):
    return lax.optimization_barrier((value,) + others)[0]


def normalize(value):
    centered = value - jnp.mean(value, axis=-1, keepdims=True)
    inv = lax.rsqrt(jnp.mean(centered * centered, axis=-1, keepdims=True) + EPSILON)
    return centered * inv, inv


def norm_back(grad, gain, unit, inv):
    r = grad * gain
    back = (r - jnp.mean(r, axis=-1, keepdims=True) - unit * jnp.mean(r * unit, axis=-1, keepdims=True)) * inv
    return back, jnp.sum(grad * unit, axis=0), jnp.sum(grad, axis=0)


def per_device(
    tokens, w_query, w_key, w_value, b_query, b_value, conv_taps, w_out, b_out, gain_one, shift_one, w_up, b_up, w_down,
    b_down, gain_two, shift_two, cotangent, segment_ids, landmark_ids,
):
    dim = tokens.shape[1]
    width = w_query.shape[1]
    units = w_up.shape[1]
    heads = head_count(width)
    seqs = tokens.shape[0] // SEQ_LEN
    me = lax.axis_index("tensor")
    core, chip = me % 2, me // 2
    own_rows = cotangent.shape[0]
    sequences = tokens.reshape(seqs, SEQ_LEN, dim)
    segments = segment_ids.reshape(seqs, 1, SEQ_LEN)
    marks = landmark_ids.reshape(seqs, 1, SEQ_LEN)
    place_dp = lax.axis_index("dp")
    bits = [place_dp % 2, place_dp // 2 % 2]
    at_own = jnp.stack([chip, core, *bits]).astype(jnp.int32)
    at_far = jnp.stack([1 - chip, core, *bits]).astype(jnp.int32)
    taps_back = conv_taps[:, ::-1]
    wq, wk, wv = w_query.T, w_key.T, w_value.T
    bias = b_up[None]

    def forward(at):
        return attend_forward(
            at, sequences, wq, wk, wv, b_query[None], b_value[None], conv_taps, w_out, segments, marks
        )

    def halves(first, second):
        return jnp.concatenate([first, second], axis=0)

    far = forward(at_far)
    owed = halves(far[0], far[1]) + halves(swap(far[2], 1), swap(far[3], 1))
    own = forward(after(at_own, owed))
    through = swap(owed, 2)
    near = halves(swap(own[2], 1), swap(own[3], 1))
    summed = halves(own[0], own[1]).astype(F32) + near.astype(F32) + through.astype(F32)
    own_tokens = lax.dynamic_slice_in_dim(tokens, me * own_rows, own_rows, 0).astype(F32)
    unit_one, inv_one = normalize(own_tokens + summed + b_out)
    normed = unit_one * gain_one + shift_one

    def feed(whole_mine, run, meanwhile=None):
        mine = [whole_mine[:CHUNK], whole_mine[CHUNK:]]
        near = [swap(m, 1) for m in mine]
        got = [swap(m, 2) for m in mine]
        blocks = [*mine, *near]
        results = run(blocks, 0)
        gate = results[0][-1] if meanwhile is None else meanwhile(blocks, results)
        through = []
        for c in range(2):
            pair = [after(got[c], gate)]
            pair.append(swap_pieces(pair[0]))
            done = run(pair, len(blocks))
            blocks, results = blocks + pair, results + done
            gate = done[0][-1] + swap_pieces(done[1][-1])
            if c > 0:
                through[0], gate = lax.optimization_barrier((through[0], gate))
            through.append(swap(gate, 2))
        sums = [
            results[c][-1].astype(F32) + swap(results[2 + c][-1], 1).astype(F32) + through[c].astype(F32) for c in range(2)
        ]
        return blocks, results, halves(*sums), gate

    lows, acts, branch, _ = feed(normed.astype(BF16), lambda blocks, n: up_down(blocks, w_up, bias, w_down))
    unit_two, inv_two = normalize(normed + branch + b_down)
    output = (unit_two * gain_two + shift_two).astype(BF16)
    grad_pre_out, grad_gain_two, grad_shift_two = norm_back(cotangent.astype(F32), gain_two, unit_two, inv_two)
    grad_b_down = jnp.sum(grad_pre_out, axis=0)
    grad_low = lax.optimization_barrier(grad_pre_out.astype(BF16))
    unit_low = lax.optimization_barrier(unit_one.astype(BF16))

    sums = []

    def weigh_own(grads, backs):
        blocks = [(acts[n][0], grads[n], lows[n], backs[n][0]) for n in range(4)]
        sums.extend(up_down_weights(at_own, blocks))
        return sums[0]

    grads, backs, back_normed, owed = feed(
        grad_low,
        lambda blocks, n: up_down_back([(b, acts[n + i][1]) for i, b in enumerate(blocks)], w_up, w_down),
        weigh_own,
    )
    blocks = [(acts[n][0], grads[n], lows[n], backs[n][0]) for n in range(4, 8)]
    blocks[0] = (after(blocks[0][0], owed), *blocks[0][1:])
    down_kept, down_sent, up_kept, up_sent, d_bias = up_down_weights(at_own, blocks, sums)
    back_normed = after(back_normed, down_sent, up_sent)
    down = Total(down_kept, down_sent, 0, "dp")
    up = Total(up_kept, up_sent, 1, "dp")
    grad_pre_norm, grad_gain_one, grad_shift_one = norm_back(
        grad_low.astype(F32) + back_normed, gain_one, unit_low.astype(F32), inv_one
    )
    grad_b_out = jnp.sum(grad_pre_norm, axis=0)
    top = lax.optimization_barrier(grad_pre_norm.astype(BF16))
    near = swap(top, 1)
    over = swap(top, 2)

    def values(at, mine, theirs, saved, prev=()):
        return attend_back_values(at, mine, theirs, sequences, taps_back, w_out, segments, saved, prev)

    def queries(at, saved, part, prev=()):
        return attend_back_queries(at, sequences, segments, marks, saved, part, prev)

    def both(*others):
        return down.step(*others), up.step(*others)

    norms = jnp.stack([grad_gain_one, grad_shift_one, grad_b_out, grad_gain_two, grad_shift_two, grad_b_down])
    own_v = values(after(at_own, *both(top)), top, near, own[4:])
    own_q = queries(after(at_own, *both(own_v[0])), own[4:], own_v[3:6])
    norms = norms + after(swap(norms, 1), own_q[0])
    far_v = values(after(at_far, own_q[0]), over, swap(over, 1), far[4:], own_v[0:2])
    norms = norms + after(swap(norms, 2), far_v[0])
    one = Total(far_v[0], far_v[1], 0, "dp")
    far_q = queries(after(at_far, *both(far_v[0])), far[4:], far_v[4:7], own_q[0:2])
    two = Total(far_q[0], far_q[1], 1, "dp")
    far_x = attend_back_tokens(at_far, (far_q[3], far_q[4], far_v[3]), (wq, wk, wv))
    owed = far_x[0] + swap(far_x[1], 1)
    through = swap(owed, 2)
    own_x = attend_back_tokens(at_own, (after(own_q[2], owed), own_q[3], own_v[2]), (wq, wk, wv))
    near = swap(own_x[1], 1)
    small = jnp.concatenate(
        [norms, d_bias[0:1], jnp.pad((far_v[2] + far_q[2])[0 : heads + 2], ((0, 0), (0, dim - WINDOW)))], axis=0
    )
    one.step(far_q[0])
    down.got, up.got, one.got, two.got = lax.optimization_barrier((down.got, up.got, one.got, two.got))
    for part in (two, one, up, down):
        part.step()
    mask = 1
    while mask < lax.axis_size("dp"):
        got = swap(small, mask, "dp")
        if mask == 1:
            got, one.got, two.got = lax.optimization_barrier((got, one.got, two.got))
            two.step()
            one.step()
            down.got, up.got, two.got = lax.optimization_barrier((down.got, up.got, two.got))
        elif mask == 2:
            got, one.got, two.got = lax.optimization_barrier((got, one.got, two.got))
            two.step()
            one.step()
        elif mask == 4:
            got, one.got, two.got, through = lax.optimization_barrier((got, one.got, two.got, through))
            two.step()
        small = small + got
        mask *= 2
    input_grad = top.astype(F32) + own_x[0].astype(F32) + near.astype(F32) + through.astype(F32)
    value_out = one.finish().astype(F32)
    query_key = two.finish().astype(F32)
    down_sum = down.finish().astype(F32)
    up_sum = up.finish().astype(F32)

    return (
        output,
        input_grad,
        query_key[0:width].T,
        query_key[width:].T,
        value_out[0:width].T,
        small[7 + heads, 0:width],
        small[8 + heads, 0:width],
        small[7 : 7 + heads, 0:CONV_TAPS],
        value_out[width:],
        small[2],
        small[0],
        small[1],
        up_sum,
        small[6, 0:units],
        down_sum,
        small[5],
        small[3],
        small[4],
    )


def solution(mesh):
    rows = P(("dp", "tensor"), None)
    columns = P(None, "tensor")
    split_rows = P("tensor", None)
    vector = P("tensor")
    return jax.shard_map(
        per_device,
        mesh=mesh,
        in_specs=(
            P("dp", None), columns, columns, columns, vector, vector, split_rows, split_rows, P(), P(), P(),
            columns, vector, split_rows, P(), P(), P(), rows, P("dp"), P("dp"),
        ),
        out_specs=(
            rows, rows, columns, columns, columns, vector, vector, split_rows, split_rows, P(), P(), P(),
            columns, vector, split_rows, P(), P(), P(),
        ),
        check_vma=False,
    )
```

```python
import functools

import jax
import jax.numpy as jnp
from jax import lax
from jax.experimental import pallas as pl
from jax.experimental.pallas import tpu as pltpu
from jax.sharding import PartitionSpec as P

HEAD_DIM = 64
LANDMARKS = 64
CONV_TAPS = 33
PINV_STEPS = 6
DOCS = 8
PER_DOC = LANDMARKS // DOCS
SEQ_LEN = 1024
EPSILON = 1e-05
SCALE = HEAD_DIM ** -0.5
HALF = CONV_TAPS // 2
BLOCK = 128
WINDOW = 256
CHUNK = 256
F32 = jnp.float32
BF16 = jnp.bfloat16
NN = (((1,), (0,)), ((), ()))
NT = (((1,), (1,)), ((), ()))
TN = (((0,), (0,)), ((), ()))


def takes(microseconds):
    return pl.CostEstimate(flops=int(microseconds * 1.1e9), bytes_accessed=1, transcendentals=0)


def mm(left, right, dims=NN):
    return lax.dot_general(left, right, dims, preferred_element_type=F32)


def split(value):
    high = value.astype(BF16)
    return high, (value - high.astype(F32)).astype(BF16)


def mm3(left, right, dims=NN):
    lh, ll = left
    rh, rl = right
    return mm(lh, rh, dims) + mm(ll, rh, dims) + mm(lh, rl, dims)


def iota(shape, dim):
    return lax.broadcasted_iota(jnp.int32, shape, dim)


def head_count(width):
    return width // HEAD_DIM


def block_mask(heads):
    shape = (heads * LANDMARKS, heads * HEAD_DIM)
    return iota(shape, 0) // LANDMARKS == iota(shape, 1) // HEAD_DIM


def spread(rows, heads):
    return jnp.where(block_mask(heads), jnp.concatenate([rows] * heads, axis=0), 0.0)


def fold(full, heads):
    return jnp.concatenate(
        [full[h * 64 : (h + 1) * 64, h * 64 : (h + 1) * 64] for h in range(heads)], axis=0
    )


def stack(rows, heads):
    return jnp.concatenate([rows[:, h * 64 : (h + 1) * 64] for h in range(heads)], axis=0)


def unstack(rows, heads):
    return jnp.concatenate([rows[h * 64 : (h + 1) * 64] for h in range(heads)], axis=1)


def block_diag(rows, heads):
    return jnp.where(block_mask(heads), jnp.concatenate([rows] * heads, axis=1), 0.0)


def doc_masks(segment):
    return [jnp.broadcast_to(segment == d, (PER_DOC, segment.shape[1])) for d in range(DOCS)]


def pick(full, masks, heads):
    out = []
    for h in range(heads):
        kept = jnp.zeros(masks[0].shape, F32)
        for d in range(DOCS):
            row = h * LANDMARKS + d * PER_DOC
            kept = jnp.where(masks[d], full[row : row + PER_DOC], kept)
        out.append(kept)
    return out


def place(compact, masks, heads):
    return jnp.concatenate(
        [jnp.where(masks[d], compact[h], 0.0) for h in range(heads) for d in range(DOCS)], axis=0
    )


def per_doc(rows, masks):
    out = jnp.zeros(masks[0].shape, F32)
    for d in range(DOCS):
        out = jnp.where(masks[d], rows[d * PER_DOC : (d + 1) * PER_DOC], out)
    return out


def rows_to_lanes(full, scratch, heads):
    rows = heads * LANDMARKS
    lane_doc = (iota((rows, 128), 1) // PER_DOC) % DOCS
    row_doc = (iota((rows, 128), 0) // PER_DOC) % DOCS
    kept = jnp.where(lane_doc == row_doc, full, 0.0)
    for shift in (8, 16, 32):
        kept = kept + pltpu.roll(kept, shift, 1)
    scratch[0:rows, :] = kept
    count = heads * DOCS
    group = iota((count, 128), 1) // PER_DOC
    out = jnp.zeros((count, 128), F32)
    for i in range(PER_DOC):
        out = jnp.where(group == i, scratch[pl.ds(i, count, stride=PER_DOC), :], out)
    return jnp.concatenate([out, jnp.zeros((128 - count, 128), F32)], axis=0).T[0:64]


def lanes_to_rows(blocks, heads):
    full = jnp.concatenate([blocks, jnp.zeros((64, 128), F32)], axis=0).T
    return full[0 : heads * DOCS]


def apply_blocks(coef, operand_ref, result_ref, heads, transposed):
    count = heads * DOCS
    pieces = [operand_ref[pl.ds(j, count, stride=PER_DOC), :] for j in range(PER_DOC)]
    for i in range(PER_DOC):
        total = jnp.zeros(pieces[0].shape, F32)
        for j in range(PER_DOC):
            k = j * PER_DOC + i if transposed else i * PER_DOC + j
            total = total + coef[:, k : k + 1] * pieces[j]
        result_ref[pl.ds(i, count, stride=PER_DOC), :] = total


def bm(left, right):
    a = left.reshape(8, 8, -1)
    b = right.reshape(8, 8, -1)
    total = a[:, 0:1] * b[0:1]
    for k in range(1, 8):
        total = total + a[:, k : k + 1] * b[k : k + 1]
    return total.reshape(64, -1)


def bm_tn(left, right):
    rows = []
    for i in range(8):
        total = left[i : i + 1] * right[0:8]
        for k in range(1, 8):
            total = total + left[k * 8 + i : k * 8 + i + 1] * right[k * 8 : k * 8 + 8]
        rows.append(total)
    return jnp.concatenate(rows, axis=0)


def flip(blocks, scratch):
    scratch[0:64, :] = blocks
    return jnp.concatenate([scratch[pl.ds(i, 8, stride=8), :] for i in range(8)], axis=0)


def lane_eye():
    row = iota((64, 128), 0)
    return jnp.where(row // 8 == row % 8, 1.0, 0.0)


def column_sums(blocks):
    total = blocks[0:8]
    for i in range(1, 8):
        total = total + blocks[i * 8 : i * 8 + 8]
    return total


def row_sums(blocks):
    return jnp.concatenate(
        [jnp.sum(blocks[i * 8 : i * 8 + 8], axis=0, keepdims=True) for i in range(8)], axis=0
    )


def head_lanes(h):
    return iota((8, 128), 1) // DOCS == h


def head_most(sums, heads):
    out = jnp.ones((1, 128), F32)
    for h in range(heads):
        mask = head_lanes(h)
        most = jnp.max(jnp.max(jnp.where(mask, sums, -1e30), axis=1, keepdims=True), axis=0, keepdims=True)
        out = jnp.where(mask[0:1], most, out)
    return out


def head_total(values, heads):
    out = jnp.zeros((1, 128), F32)
    for h in range(heads):
        mask = head_lanes(h)
        total = jnp.sum(jnp.sum(jnp.where(mask, values, 0.0), axis=1, keepdims=True), axis=0, keepdims=True)
        out = jnp.where(mask[0:1], total, out)
    return out


def same_document(segment, seg_pad, start):
    rows = jnp.broadcast_to(segment[:, start : start + BLOCK], (BLOCK, BLOCK)).T
    return jnp.concatenate([rows, rows], axis=1) == seg_pad[0:1, start : start + WINDOW]


def toeplitz(taps_ref, h, scratch):
    scratch[0:8, 0:WINDOW] = jnp.zeros((8, WINDOW), F32)
    scratch[0:1, 0:CONV_TAPS] = taps_ref[h : h + 1, :]
    taps_row = scratch[0:1, 0:WINDOW]
    return pltpu.roll(jnp.broadcast_to(taps_row, (BLOCK, WINDOW)), 0, 1, stride=1, stride_axis=0)


def pad_segment(seg_pad, segment):
    seg_pad[:, 0:128] = jnp.zeros((8, 128), F32)
    seg_pad[:, 0:SEQ_LEN] = jnp.broadcast_to(pltpu.roll(segment, HALF, 1), (8, SEQ_LEN))
    seg_pad[:, SEQ_LEN:] = jnp.broadcast_to(segment[:, SEQ_LEN - 1 : SEQ_LEN], (8, WINDOW))


def attend_forward_kernel(
    where_ref, tokens_ref, wq_ref, wk_ref, wv_ref, bq_ref, bv_ref, taps_ref, w_out_ref, seg_ref, mark_ref,
    keep_a_ref, keep_b_ref, send_a_ref, send_b_ref, q_ref, k_ref, v_ref, att_ref, p1_ref, p3_ref, qm_ref, km_ref, ctx_ref, bl_ref, count_ref, mid_ref, steps_ref, inverse_ref,
    padded, seg_pad, scratch, band,
):
    width = wq_ref.shape[0]
    heads = head_count(width)
    tokens = tokens_ref.at[0]
    rows = 256

    def project(i, carry):
        at = pl.ds(pl.multiple_of(i * rows, rows), rows)
        x = tokens[at, :]
        q_ref[at, :] = (mm(x, wq_ref[...], NT) + bq_ref[...]).astype(BF16)
        k_ref[at, :] = mm(x, wk_ref[...], NT).astype(BF16)
        value = (mm(x, wv_ref[...], NT) + bv_ref[...]).astype(BF16)
        v_ref[at, :] = value
        padded[pl.ds(pl.multiple_of(i * rows + HALF, 16), rows), :] = value
        return carry

    padded[0:HALF, :] = jnp.zeros((HALF, width), BF16)
    padded[SEQ_LEN + HALF :, :] = jnp.zeros((WINDOW - HALF, width), BF16)
    lax.fori_loop(0, SEQ_LEN // rows, project, 0)

    segment = seg_ref[0].astype(F32)
    masks = doc_masks(segment)
    one_hot = mark_ref[0] == iota((LANDMARKS, SEQ_LEN), 0)
    counts = jnp.sum(one_hot.astype(F32), axis=1, keepdims=True)
    pool = one_hot.astype(BF16)
    q_marks = mm(pool, q_ref[...]) / counts
    k_marks = mm(pool, k_ref[...]) / counts
    count_ref[...] = jnp.broadcast_to(counts, (LANDMARKS, 128))
    qm_ref[...] = q_marks
    km_ref[...] = k_marks
    k_block = split(spread(k_marks, heads))
    q_wide = spread(q_marks, heads)
    q_block = split(q_wide)

    queries = q_ref[...]
    scores = pick(mm(k_block[0], queries, NT) + mm(k_block[1], queries, NT), masks, heads)
    first = []
    for h in range(heads):
        s = scores[h] * SCALE
        e = jnp.exp(s - jnp.max(s, axis=0, keepdims=True))
        first.append(e / jnp.sum(e, axis=0, keepdims=True))
    p1_ref[...] = jnp.concatenate(first, axis=0)

    keys = k_ref[...]
    scores = pick(mm(q_block[0], keys, NT) + mm(q_block[1], keys, NT), masks, heads)
    last = []
    for h in range(heads):
        s = scores[h] * SCALE
        most = jnp.concatenate(
            [jnp.max(jnp.where(masks[d], s, -1e30), axis=1, keepdims=True) for d in range(DOCS)], axis=0
        )
        e = jnp.exp(s - per_doc(most, masks))
        total = jnp.concatenate(
            [jnp.sum(jnp.where(masks[d], e, 0.0), axis=1, keepdims=True) for d in range(DOCS)], axis=0
        )
        last.append(e / per_doc(total, masks))
    p3_ref[...] = jnp.concatenate(last, axis=0)

    weights = split(place(last, masks, heads))
    values = v_ref[...]
    context = fold(mm(weights[0], values) + mm(weights[1], values), heads)
    ctx_ref[...] = context

    twice = jnp.concatenate([k_marks, k_marks], axis=0)
    grid = lax.dot_general(q_wide, twice, NT, precision=lax.Precision.HIGHEST, preferred_element_type=F32)
    scores = (rows_to_lanes(grid, scratch, heads) * SCALE).reshape(8, 8, 128)
    e = jnp.exp(scores - jnp.max(scores, axis=1, keepdims=True))
    middle = (e / jnp.sum(e, axis=1, keepdims=True)).reshape(64, 128)
    used = iota((64, 128), 1) < heads * DOCS
    middle = jnp.where(used, middle, 0.0)
    mid_ref[...] = middle
    norm = head_most(column_sums(middle), heads) * head_most(row_sums(middle), heads)
    eye = lane_eye()

    def step(n, inverse):
        product = bm(middle, inverse)
        second = 15.0 * eye - bm(product, 7.0 * eye - product)
        third = 13.0 * eye - bm(product, second)
        steps_ref[n, 0] = inverse
        steps_ref[n, 1] = product
        steps_ref[n, 2] = second
        steps_ref[n, 3] = third
        return 0.25 * bm(inverse, third)

    inverse = lax.fori_loop(0, PINV_STEPS, step, flip(middle, scratch) / norm)
    inverse_ref[...] = inverse
    coef = lanes_to_rows(inverse, heads)
    apply_blocks(coef, ctx_ref, bl_ref, heads, False)
    blended = split(block_diag(bl_ref[...], heads))
    weights = split(place(first, masks, heads))
    attended = mm3(weights, blended, TN)

    for h in range(heads):
        band[h] = toeplitz(taps_ref, h, seg_pad).astype(BF16)
    pad_segment(seg_pad, segment)
    att_ref[...] = attended.astype(BF16)
    lane_head = iota((BLOCK, width), 1) // HEAD_DIM
    scratch_f = attended

    for b in range(SEQ_LEN // BLOCK):
        start = b * BLOCK
        rows_at = pl.ds(start, BLOCK)
        same = same_document(segment, seg_pad, start)
        window = padded[pl.ds(start, WINDOW), :]
        total = scratch_f[start : start + BLOCK]
        for h in range(heads):
            part = mm(jnp.where(same, band[h], 0), window)
            total = total + jnp.where(lane_head == h, part, 0.0)
        att_ref[rows_at, :] = total.astype(BF16)

    half = SEQ_LEN // 2
    core = where_ref[1]
    weight = w_out_ref[...]
    for base, refs in ((core, (keep_a_ref, keep_b_ref)), (1 - core, (send_a_ref, send_b_ref))):
        for i, ref in enumerate(refs):
            at = pl.ds(pl.multiple_of(base * half + i * CHUNK, CHUNK), CHUNK)
            ref[...] = mm(att_ref[at, :], weight).astype(BF16)


def attend_forward(where, tokens, wq, wk, wv, bq, bv, taps, w_out, segments, marks):
    dim = tokens.shape[2]
    width = wq.shape[0]
    heads = head_count(width)

    def whole(*shape):
        return pl.BlockSpec(shape, lambda i, w: (0,) * len(shape))

    def one(*shape):
        return pl.BlockSpec((1,) + shape, lambda i, w: (w[0],) + (0,) * len(shape))

    outs = [
        *[((CHUNK, dim), BF16)] * 4,
        ((SEQ_LEN, width), BF16), ((SEQ_LEN, width), BF16), ((SEQ_LEN, width), BF16), ((SEQ_LEN, width), BF16),
        ((heads * 8, SEQ_LEN), F32), ((heads * 8, SEQ_LEN), F32),
        ((LANDMARKS, width), F32), ((LANDMARKS, width), F32),
        ((heads * LANDMARKS, HEAD_DIM), F32), ((heads * LANDMARKS, HEAD_DIM), F32),
        ((LANDMARKS, 128), F32), ((64, 128), F32), ((PINV_STEPS, 4, 64, 128), F32), ((64, 128), F32),
    ]
    return pl.pallas_call(
        attend_forward_kernel,
        out_shape=[jax.ShapeDtypeStruct(s, t) for s, t in outs],
        grid_spec=pltpu.PrefetchScalarGridSpec(
            num_scalar_prefetch=1,
            grid=(1,),
            in_specs=[
                one(SEQ_LEN, dim), whole(width, dim), whole(width, dim), whole(width, dim), whole(1, width), whole(1, width),
                whole(heads, CONV_TAPS), whole(width, dim), one(1, SEQ_LEN), one(1, SEQ_LEN),
            ],
            out_specs=[whole(*s) for s, t in outs],
            scratch_shapes=[
                pltpu.VMEM((SEQ_LEN + WINDOW, width), BF16),
                pltpu.VMEM((8, SEQ_LEN + WINDOW), F32),
                pltpu.VMEM((heads * LANDMARKS, 128), F32),
                pltpu.VMEM((heads, BLOCK, WINDOW), BF16),
            ],
        ),
        compiler_params=pltpu.CompilerParams(vmem_limit_bytes=56 << 20),
        cost_estimate=takes(12),
    )(where, tokens, wq, wk, wv, bq, bv, taps, w_out, segments, marks)


def diagonal_sums(band):
    row = iota(band.shape, 0)
    for bit in range(7):
        shift = 1 << bit
        moved = pltpu.roll(band, WINDOW - shift, 1)
        band = jnp.where((row // shift) % 2 == 1, moved, band)
    return jnp.sum(band, axis=0, keepdims=True)


def plus(ref, at, value):
    return value if ref is None else ref[at] + value


def sums_refs(final, where_ref, refs, turn):
    if not final:
        weights_ref, *refs = refs
        return None, None, weights_ref, refs, lambda: None
    prev_ref, prev_small_ref, kept_ref, sent_ref, *refs = refs
    *refs, weights_ref = refs

    def finish():
        half = kept_ref.shape[0]
        bit = where_ref[2 + turn]
        kept_ref[...] = weights_ref[pl.ds(pl.multiple_of(bit * half, half), half), :]
        sent_ref[...] = weights_ref[pl.ds(pl.multiple_of((1 - bit) * half, half), half), :].astype(BF16)

    return prev_ref, prev_small_ref, weights_ref, refs, finish


def attend_back_values_kernel(
    final, where_ref, mine_ref, theirs_ref, tokens_ref, taps_ref, w_out_ref, seg_ref,
    v_ref, att_ref, p1_ref, p3_ref, ctx_ref, bl_ref, inverse_ref, *refs
):
    prev_ref, prev_small_ref, weights_ref, refs, finish = sums_refs(final, where_ref, refs, 0)
    small_ref, dv_ref, ds1_ref, ds3_ref, dbl_ref, dctx_ref, grad_ref, up_ref, value_ref, seg_pad, band, corr = refs
    width = v_ref.shape[1]
    heads = head_count(width)
    half = SEQ_LEN // 2
    core = where_ref[1]

    grad_ref[0:HALF, :] = jnp.zeros((HALF, width), BF16)
    grad_ref[SEQ_LEN + HALF :, :] = jnp.zeros((WINDOW - HALF, width), BF16)
    value_ref[0:HALF, :] = jnp.zeros((HALF, width), BF16)
    value_ref[SEQ_LEN + HALF :, :] = jnp.zeros((WINDOW - HALF, width), BF16)
    value_ref[HALF : SEQ_LEN + HALF, :] = v_ref[...]
    for base, ref in ((core, mine_ref), (1 - core, theirs_ref)):
        for i in range(half // CHUNK):
            at = pl.ds(i * CHUNK, CHUNK)
            to = pl.multiple_of(base * half + i * CHUNK, CHUNK)
            up_ref[pl.ds(to, CHUNK), :] = ref[at, :]
            grad_ref[pl.ds(pl.multiple_of(to + HALF, HALF), CHUNK), :] = mm(ref[at, :], w_out_ref[...], NT).astype(BF16)
    at = (slice(width, 2 * width), slice(None))
    weights_ref[at] = plus(prev_ref, at, mm(att_ref[...], up_ref[...], TN))

    segment = seg_ref[0].astype(F32)
    masks = doc_masks(segment)
    first = [p1_ref[h * 8 : h * 8 + 8, :] for h in range(heads)]
    last = [p3_ref[h * 8 : h * 8 + 8, :] for h in range(heads)]
    gradient = grad_ref[HALF : SEQ_LEN + HALF, :]
    values = v_ref[...]

    first_wide = split(place(first, masks, heads))
    dbl = fold(mm(first_wide[0], gradient) + mm(first_wide[1], gradient), heads)
    dbl_ref[...] = dbl
    blended = split(block_diag(bl_ref[...], heads))
    dfirst = pick(mm(blended[0], gradient, NT) + mm(blended[1], gradient, NT), masks, heads)
    for h in range(heads):
        ds1_ref[h * 8 : h * 8 + 8, :] = (
            SCALE * first[h] * (dfirst[h] - jnp.sum(first[h] * dfirst[h], axis=0, keepdims=True))
        )

    apply_blocks(lanes_to_rows(inverse_ref[...], heads), dbl_ref, dctx_ref, heads, True)
    dctx = dctx_ref[...]
    dctx_wide = split(block_diag(dctx, heads))
    dlast = pick(mm(dctx_wide[0], values, NT) + mm(dctx_wide[1], values, NT), masks, heads)
    inner = jnp.sum(dctx * ctx_ref[...], axis=1, keepdims=True)
    for h in range(heads):
        ds3_ref[h * 8 : h * 8 + 8, :] = (
            SCALE * last[h] * (dlast[h] - per_doc(inner[h * 64 : (h + 1) * 64], masks))
        )
    last_wide = place(last, masks, heads).astype(BF16)
    dvalue = mm(last_wide, dctx_wide[0], TN) + mm(last_wide, dctx_wide[1], TN)

    for h in range(heads):
        band[h] = toeplitz(taps_ref, h, seg_pad).astype(BF16)
        corr[h] = jnp.zeros((BLOCK, WINDOW), F32)
    pad_segment(seg_pad, segment)
    lane_head = iota((BLOCK, width), 1) // HEAD_DIM
    for b in range(SEQ_LEN // BLOCK):
        begin = b * BLOCK
        same = same_document(segment, seg_pad, begin)
        window = grad_ref[begin : begin + WINDOW, :]
        near = value_ref[begin : begin + WINDOW, :]
        block = grad_ref[begin + HALF : begin + HALF + BLOCK, :]
        total = dvalue[begin : begin + BLOCK]
        for h in range(heads):
            taps = jnp.where(same, band[h], 0)
            part = mm(taps, window)
            total = total + jnp.where(lane_head == h, part, 0.0)
            mine = lane_head == h
            part = mm(jnp.where(mine, block, 0), near, NT)
            corr[h] = corr[h] + jnp.where(same, part, 0.0)
        dv_ref[begin : begin + BLOCK, :] = total.astype(BF16)

    small_ref[...] = jnp.zeros(small_ref.shape, F32)
    for h in range(heads):
        at = (slice(h, h + 1), slice(None))
        small_ref[at] = plus(prev_small_ref, at, diagonal_sums(corr[h]))
    at = (slice(heads + 1, heads + 2), slice(0, width))
    small_ref[at] = plus(prev_small_ref, at, jnp.sum(dv_ref[...].astype(F32), axis=0, keepdims=True))
    at = (slice(0, width), slice(None))
    weights_ref[at] = plus(prev_ref, at, mm(dv_ref[...], tokens_ref[0], TN))
    finish()


def attend_back_queries_kernel(
    final, where_ref, tokens_ref, seg_ref, mark_ref,
    q_ref, k_ref, qm_ref, km_ref, ctx_ref, count_ref, mid_ref, steps_ref, ds1_ref, ds3_ref, dbl_ref, *refs
):
    prev_ref, prev_small_ref, weights_ref, refs, finish = sums_refs(final, where_ref, refs, 1)
    small_ref, dq_ref, dk_ref, scratch, scratch_b, dqm_ref, dkm_ref, stack_ref = refs
    width = q_ref.shape[1]
    heads = head_count(width)
    masks = doc_masks(seg_ref[0].astype(F32))
    pool = (mark_ref[0] == iota((LANDMARKS, SEQ_LEN), 0)).astype(BF16)
    queries = q_ref[...]
    keys = k_ref[...]
    dscore_one = split(place([ds1_ref[h * 8 : h * 8 + 8, :] for h in range(heads)], masks, heads))
    dscore_last = split(place([ds3_ref[h * 8 : h * 8 + 8, :] for h in range(heads)], masks, heads))
    dkm = fold(mm(dscore_one[0], queries) + mm(dscore_one[1], queries), heads)
    dqm = fold(mm(dscore_last[0], keys) + mm(dscore_last[1], keys), heads)

    context = unstack(ctx_ref[...], heads)
    grid = lax.dot_general(
        block_diag(dbl_ref[...], heads), jnp.concatenate([context, context], axis=0), NT,
        precision=lax.Precision.HIGHEST, preferred_element_type=F32,
    )
    dinverse = rows_to_lanes(grid, scratch, heads)
    middle = mid_ref[...]
    eye = lane_eye()

    def step(n, carry):
        dz, dmid = carry
        n = PINV_STEPS - 1 - n
        z = steps_ref[n, 0]
        product = steps_ref[n, 1]
        second = steps_ref[n, 2]
        third = steps_ref[n, 3]
        dthird = 0.25 * bm_tn(z, dz)
        dz_next = 0.25 * bm(dz, flip(third, scratch_b.at[0]))
        dsecond = -bm_tn(product, dthird)
        dprod = -bm(dthird, flip(second, scratch_b.at[1])) - bm(dsecond, flip(7.0 * eye - product, scratch_b.at[2]))
        dprod = dprod + bm_tn(product, dsecond)
        dmid = dmid + bm(dprod, flip(z, scratch_b.at[3]))
        dz_next = dz_next + bm_tn(middle, dprod)
        return dz_next, dmid

    dz, dmid = lax.fori_loop(0, PINV_STEPS, step, (dinverse, jnp.zeros((64, 128), F32)))
    columns = column_sums(middle)
    across = row_sums(middle)
    column_most = head_most(columns, heads)
    row_most = head_most(across, heads)
    start = flip(middle, scratch) / (column_most * row_most)
    dmid = dmid + flip(dz, scratch) / (column_most * row_most)
    total = jnp.sum(dz * start, axis=0, keepdims=True)
    total = head_total(jnp.where(iota((8, 128), 0) == 0, jnp.broadcast_to(total, (8, 128)), 0.0), heads)
    hit = jnp.where(columns == column_most, 1.0, 0.0)
    dcolumns = -total / column_most * hit / jnp.maximum(head_total(hit, heads), 1.0)
    hit = jnp.where(across == row_most, 1.0, 0.0)
    drows = -total / row_most * hit / jnp.maximum(head_total(hit, heads), 1.0)
    dmid = dmid + jnp.concatenate([dcolumns + drows[i : i + 1] for i in range(8)], axis=0)
    dgrid = jnp.concatenate(
        [
            SCALE * middle[i * 8 : i * 8 + 8]
            * (dmid[i * 8 : i * 8 + 8] - jnp.sum(middle[i * 8 : i * 8 + 8] * dmid[i * 8 : i * 8 + 8], axis=0, keepdims=True))
            for i in range(8)
        ],
        axis=0,
    )
    coef = lanes_to_rows(dgrid, heads)
    q_stack = stack(qm_ref[...], heads)
    k_stack = stack(km_ref[...], heads)
    stack_ref[...] = k_stack
    apply_blocks(coef, stack_ref, dqm_ref, heads, False)
    stack_ref[...] = q_stack
    apply_blocks(coef, stack_ref, dkm_ref, heads, True)

    dqm = dqm + dqm_ref[...]
    dkm = dkm + dkm_ref[...]
    counts = count_ref[:, 0:1]
    dqm = split(unstack(dqm, heads) / counts)
    dkm = split(unstack(dkm, heads) / counts)
    k_wide = split(spread(km_ref[...], heads))
    q_wide = split(spread(qm_ref[...], heads))

    def pulled(scores, wide, marks):
        left = jnp.concatenate([scores[0], pool], axis=0)
        return mm(left, jnp.concatenate([wide[0], marks[0]], axis=0), TN) + mm(
            left, jnp.concatenate([wide[1], marks[1]], axis=0), TN
        )

    dq_ref[...] = pulled(dscore_one, k_wide, dqm).astype(BF16)
    dk_ref[...] = pulled(dscore_last, q_wide, dkm).astype(BF16)

    small_ref[...] = jnp.zeros(small_ref.shape, F32)
    at = (slice(heads, heads + 1), slice(0, width))
    small_ref[...] = plus(prev_small_ref, (slice(None), slice(None)), small_ref[...])
    small_ref[at] = plus(prev_small_ref, at, jnp.sum(dq_ref[...].astype(F32), axis=0, keepdims=True))
    tokens = tokens_ref[0]
    for n, ref in enumerate((dq_ref, dk_ref)):
        at = (slice(n * width, (n + 1) * width), slice(None))
        weights_ref[at] = plus(prev_ref, at, mm(ref[...], tokens, TN))
    finish()


def attend_back_tokens_kernel(where_ref, *refs):
    ins, weights, outs = refs[:6], [ref[...] for ref in refs[6:9]], refs[9:]
    for n in range(2):
        outs[n][...] = sum(mm(ref[...], w) for ref, w in zip(ins[3 * n : 3 * n + 3], weights)).astype(BF16)


def attend_back_tokens(where, parts, weights):
    width, dim = weights[0].shape
    step = 256
    count = SEQ_LEN // 2 // step

    def rows(near):
        def at(i, w):
            return ((w[1] if near else 1 - w[1]) * count + i, 0)

        return pl.BlockSpec((step, width), at)

    return pl.pallas_call(
        attend_back_tokens_kernel,
        out_shape=[jax.ShapeDtypeStruct((SEQ_LEN // 2, dim), BF16)] * 2,
        grid_spec=pltpu.PrefetchScalarGridSpec(
            num_scalar_prefetch=1,
            grid=(count,),
            in_specs=[rows(True)] * 3 + [rows(False)] * 3 + [pl.BlockSpec((width, dim), lambda i, w: (0, 0))] * 3,
            out_specs=[pl.BlockSpec((step, dim), lambda i, w: (i, 0))] * 2,
        ),
        compiler_params=pltpu.CompilerParams(vmem_limit_bytes=40 << 20),
        cost_estimate=takes(3),
    )(where, *parts, *parts, *weights)


def whole(shape):
    return pl.BlockSpec(shape, lambda i, w: (0,) * len(shape))


def chosen(shape):
    return pl.BlockSpec((1,) + shape, lambda i, w: (w[0],) + (0,) * len(shape))


def sums_outs(width, dim, final):
    return [((width, dim), F32), ((width, dim), BF16)] if final else [((2 * width, dim), F32)]


def back_call(kernel, where, ins, specs, outs, scratch, final):
    return pl.pallas_call(
        kernel,
        out_shape=[jax.ShapeDtypeStruct(s, t) for s, t in outs],
        grid_spec=pltpu.PrefetchScalarGridSpec(
            num_scalar_prefetch=1, grid=(1,), in_specs=specs, out_specs=[whole(s) for s, t in outs], scratch_shapes=scratch
        ),
        compiler_params=pltpu.CompilerParams(vmem_limit_bytes=56 << 20),
        cost_estimate=takes(0.1 if final else 11),
    )(where, *ins)


def attend_back_values(where, mine, theirs, tokens, taps, w_out, segments, saved, prev=()):
    dim = tokens.shape[2]
    q, k, v, att, p1, p3, qm, km, ctx, bl, count, mid, steps, inverse = saved
    width = v.shape[1]
    heads = head_count(width)
    final = len(prev) > 0
    rest = (v, att, p1, p3, ctx, bl, inverse, *prev)
    specs = [
        whole(mine.shape), whole(theirs.shape), chosen((SEQ_LEN, dim)), whole(taps.shape), whole(w_out.shape), chosen((1, SEQ_LEN)),
        *[whole(x.shape) for x in rest],
    ]
    outs = [
        *sums_outs(width, dim, final), ((8, WINDOW), F32), ((SEQ_LEN, width), BF16), (p1.shape, F32), (p3.shape, F32),
        (bl.shape, F32), (ctx.shape, F32),
    ]
    scratch = [
        pltpu.VMEM((SEQ_LEN + WINDOW, width), BF16),
        pltpu.VMEM((SEQ_LEN, dim), BF16),
        pltpu.VMEM((SEQ_LEN + WINDOW, width), BF16),
        pltpu.VMEM((8, SEQ_LEN + WINDOW), F32),
        pltpu.VMEM((heads, BLOCK, WINDOW), BF16),
        pltpu.VMEM((heads, BLOCK, WINDOW), F32),
        *([pltpu.VMEM((2 * width, dim), F32)] if final else []),
    ]
    kernel = functools.partial(attend_back_values_kernel, final)
    return back_call(kernel, where, (mine, theirs, tokens, taps, w_out, segments, *rest), specs, outs, scratch, final)


def attend_back_queries(where, tokens, segments, marks, saved, part, prev=()):
    dim = tokens.shape[2]
    q, k, v, att, p1, p3, qm, km, ctx, bl, count, mid, steps, inverse = saved
    ds1, ds3, dbl = part
    width = q.shape[1]
    heads = head_count(width)
    final = len(prev) > 0
    rest = (q, k, qm, km, ctx, count, mid, steps, ds1, ds3, dbl, *prev)
    specs = [chosen((SEQ_LEN, dim)), chosen((1, SEQ_LEN)), chosen((1, SEQ_LEN)), *[whole(x.shape) for x in rest]]
    outs = [*sums_outs(width, dim, final), ((8, WINDOW), F32), ((SEQ_LEN, width), BF16), ((SEQ_LEN, width), BF16)]
    scratch = [
        pltpu.VMEM((heads * LANDMARKS, 128), F32),
        pltpu.VMEM((4, 64, 128), F32),
        *[pltpu.VMEM((heads * LANDMARKS, HEAD_DIM), F32)] * 3,
        *([pltpu.VMEM((2 * width, dim), F32)] if final else []),
    ]
    kernel = functools.partial(attend_back_queries_kernel, final)
    return back_call(kernel, where, (tokens, segments, marks, *rest), specs, outs, scratch, final)


ERFC = (
    0.12694266047513267, 0.12694157407364748, 0.11413597639508828, 0.08762459251766126, 0.05998263605520133,
    -0.01120062503236582, 0.07123816174906503, -0.1503297151041413, 0.09536518640917925, -0.020700440227622966,
)


def normal_cdf(value):
    size = jnp.abs(value)
    t = 1.0 / (1.0 + 0.31819805153394637 * size)
    poly = ERFC[-1]
    for coef in ERFC[-2::-1]:
        poly = poly * t + coef
    bell = jnp.exp(-0.5 * size * size)
    tail = bell * (t * poly)
    return jnp.where(value > 0.0, 1.0 - tail, tail), bell


def up_down_kernel(*refs):
    count = (len(refs) - 3) // 4
    w_up_ref, b_up_ref, w_down_ref = refs[count : count + 3]
    outs = refs[count + 3 :]
    for n in range(count):
        act_ref, slope_ref, part_ref = outs[3 * n : 3 * n + 3]
        hidden = mm(refs[n][...], w_up_ref[...]) + b_up_ref[...]
        below, bell = normal_cdf(hidden)
        act = (hidden * below).astype(BF16)
        act_ref[...] = act
        slope_ref[...] = (below + hidden * (bell * 0.3989422804014327)).astype(BF16)
        part_ref[...] = mm(act, w_down_ref[...]).astype(BF16)


def fixed(*shape):
    return pl.BlockSpec(shape, lambda i: (0,) * len(shape), pipeline_mode=pl.Buffered(1))


def strip(rows, width):
    return pl.BlockSpec((rows, width), lambda i: (i, 0))


def up_down(blocks, w_up, b_up, w_down):
    rows, dim = blocks[0].shape
    units = w_up.shape[1]
    step = 256
    total = rows * len(blocks)
    out = pl.pallas_call(
        up_down_kernel,
        out_shape=[jax.ShapeDtypeStruct((rows, w), BF16) for w in (units, units, dim)] * len(blocks),
        grid=(rows // step,),
        in_specs=[strip(step, dim)] * len(blocks) + [fixed(dim, units), fixed(1, units), fixed(units, dim)],
        out_specs=[strip(step, units), strip(step, units), strip(step, dim)] * len(blocks),
        compiler_params=pltpu.CompilerParams(vmem_limit_bytes=40 << 20),
        cost_estimate=takes(total * 0.007),
    )(*blocks, w_up, b_up, w_down)
    return [out[3 * n : 3 * n + 3] for n in range(len(blocks))]


def up_down_back_kernel(*refs):
    count = (len(refs) - 2) // 4
    w_up_ref, w_down_ref = refs[2 * count : 2 * count + 2]
    outs = refs[2 * count + 2 :]
    for n in range(count):
        grad_ref, slope_ref = refs[2 * n : 2 * n + 2]
        hidden = (mm(grad_ref[...], w_down_ref[...], NT) * slope_ref[...].astype(F32)).astype(BF16)
        outs[2 * n][...] = hidden
        outs[2 * n + 1][...] = mm(hidden, w_up_ref[...], NT).astype(BF16)


def up_down_back(pairs, w_up, w_down):
    rows, dim = pairs[0][0].shape
    units = w_up.shape[1]
    step = 256
    total = rows * len(pairs)
    out = pl.pallas_call(
        up_down_back_kernel,
        out_shape=[jax.ShapeDtypeStruct((rows, w), BF16) for w in (units, dim)] * len(pairs),
        grid=(rows // step,),
        in_specs=[strip(step, dim), strip(step, units)] * len(pairs) + [fixed(dim, units), fixed(units, dim)],
        out_specs=[strip(step, units), strip(step, dim)] * len(pairs),
        compiler_params=pltpu.CompilerParams(vmem_limit_bytes=40 << 20),
        cost_estimate=takes(total * 0.007),
    )(*[x for pair in pairs for x in pair], w_up, w_down)
    return [out[2 * n : 2 * n + 2] for n in range(len(pairs))]


def up_down_weights_kernel(final, bits_ref, *refs):
    outs = refs[-7:] if final else refs[-3:]
    ins = refs[: len(refs) - len(outs)]
    prev, ins = (ins[-3:], ins[:-3]) if final else ((), ins)
    down_ref, up_ref = outs[-2:] if final else outs[:2]
    bias_ref = outs[4] if final else outs[2]

    @pl.when(pl.program_id(0) == 0)
    def _():
        for n, ref in enumerate((down_ref, up_ref, bias_ref)):
            ref[...] = prev[n][...] if final else jnp.zeros(ref.shape, F32)

    for n in range(len(ins) // 4):
        act_ref, grad_ref, low_ref, hidden_ref = ins[4 * n : 4 * n + 4]
        hidden = hidden_ref[...]
        down_ref[...] += mm(act_ref[...], grad_ref[...], TN)
        up_ref[...] += mm(low_ref[...], hidden, TN)
        bias_ref[0:1, :] += jnp.sum(hidden.astype(F32), axis=0, keepdims=True)

    if final:

        @pl.when(pl.program_id(0) == pl.num_programs(0) - 1)
        def _():
            for n, ref in enumerate((down_ref, up_ref)):
                half = ref.shape[0] // 2
                bit = bits_ref[2 + n]
                outs[2 * n][...] = ref[pl.ds(pl.multiple_of(bit * half, half), half), :]
                outs[2 * n + 1][...] = ref[pl.ds(pl.multiple_of((1 - bit) * half, half), half), :].astype(BF16)


def up_down_weights(bits, blocks, prev=()):
    rows, units = blocks[0][0].shape
    dim = blocks[0][1].shape[1]
    step = 256
    final = len(prev) > 0
    sums = [((units, dim), F32), ((dim, units), F32)]
    outs = sums
    if final:
        outs = [o for (r, c), t in sums for o in (((r // 2, c), F32), ((r // 2, c), BF16))]
    outs = [*outs, ((8, units), F32)]

    def strips(width):
        return pl.BlockSpec((step, width), lambda i, w: (i, 0))

    def once(shape):
        return pl.BlockSpec(shape, lambda i, w: (0, 0), pipeline_mode=pl.Buffered(1))

    return pl.pallas_call(
        functools.partial(up_down_weights_kernel, final),
        out_shape=[jax.ShapeDtypeStruct(s, t) for s, t in outs],
        grid_spec=pltpu.PrefetchScalarGridSpec(
            num_scalar_prefetch=1,
            grid=(rows // step,),
            in_specs=[strips(units), strips(dim), strips(dim), strips(units)] * len(blocks) + [once(p.shape) for p in prev],
            out_specs=[once(s) for s, t in outs],
            scratch_shapes=[pltpu.VMEM(s, t) for s, t in sums] if final else [],
        ),
        compiler_params=pltpu.CompilerParams(vmem_limit_bytes=40 << 20),
        cost_estimate=takes(5),
    )(bits, *[x for block in blocks for x in block], *prev)


def swap(value, mask, axis="tensor"):
    count = lax.axis_size(axis)
    return lax.ppermute(value, axis, [(i, i ^ mask) for i in range(count)])


class Total:
    def __init__(self, kept, sent, first, axis):
        masks = [1 << n for n in range(lax.axis_size(axis).bit_length() - 1)]
        masks.insert(0, masks.pop(first))
        self.order = masks + masks[-2::-1]
        self.count = len(masks)
        self.axis = axis
        self.index = lax.axis_index(axis)
        self.kept = kept
        self.level = 0
        self.begin(sent)

    def bit(self, n):
        return ((self.index & self.order[n]) != 0).astype(jnp.int32)

    def begin(self, sent):
        self.sent = sent
        self.got = swap(sent, self.order[self.level], self.axis)
        self.level += 1

    def step(self, *others):
        got = after(self.got, *others)
        if self.level < self.count - 1:
            half = got.shape[0] // 2
            bit = self.bit(self.level)

            def rows(which):
                at = which * half
                kept = lax.dynamic_slice_in_dim(self.kept, at, half, 0)
                return kept + lax.dynamic_slice_in_dim(got, at, half, 0).astype(F32)

            sent = rows(1 - bit).astype(BF16)
            self.kept = rows(bit)
        elif self.level == self.count - 1:
            sent = self.kept = (self.kept + got.astype(F32)).astype(BF16)
        elif self.level == self.count:
            sent = self.kept = (self.kept.astype(F32) + got.astype(F32)).astype(BF16)
        else:
            bit = self.bit(self.level - 1) > 0
            sent = self.kept = jnp.concatenate([jnp.where(bit, got, self.kept), jnp.where(bit, self.kept, got)], axis=0)
        if self.level < len(self.order):
            self.begin(sent)
        return sent

    def finish(self):
        while self.level < len(self.order):
            self.step()
        return self.step()


def swap_pieces(value):
    step = value.shape[0] // 4
    return jnp.concatenate([swap(value[n * step : (n + 1) * step], 1) for n in range(4)], axis=0)


def after(value, *others):
    return lax.optimization_barrier((value,) + others)[0]


def normalize(value):
    centered = value - jnp.mean(value, axis=-1, keepdims=True)
    inv = lax.rsqrt(jnp.mean(centered * centered, axis=-1, keepdims=True) + EPSILON)
    return centered * inv, inv


def norm_back(grad, gain, unit, inv):
    r = grad * gain
    back = (r - jnp.mean(r, axis=-1, keepdims=True) - unit * jnp.mean(r * unit, axis=-1, keepdims=True)) * inv
    return back, jnp.sum(grad * unit, axis=0), jnp.sum(grad, axis=0)


def per_device(
    tokens, w_query, w_key, w_value, b_query, b_value, conv_taps, w_out, b_out, gain_one, shift_one, w_up, b_up, w_down,
    b_down, gain_two, shift_two, cotangent, segment_ids, landmark_ids,
):
    dim = tokens.shape[1]
    width = w_query.shape[1]
    units = w_up.shape[1]
    heads = head_count(width)
    seqs = tokens.shape[0] // SEQ_LEN
    me = lax.axis_index("tensor")
    core, chip = me % 2, me // 2
    own_rows = cotangent.shape[0]
    sequences = tokens.reshape(seqs, SEQ_LEN, dim)
    segments = segment_ids.reshape(seqs, 1, SEQ_LEN)
    marks = landmark_ids.reshape(seqs, 1, SEQ_LEN)
    place_dp = lax.axis_index("dp")
    bits = [place_dp % 2, place_dp // 2 % 2]
    at_own = jnp.stack([chip, core, *bits]).astype(jnp.int32)
    at_far = jnp.stack([1 - chip, core, *bits]).astype(jnp.int32)
    taps_back = conv_taps[:, ::-1]
    wq, wk, wv = w_query.T, w_key.T, w_value.T
    bias = b_up[None]

    def forward(at):
        return attend_forward(
            at, sequences, wq, wk, wv, b_query[None], b_value[None], conv_taps, w_out, segments, marks
        )

    def halves(first, second):
        return jnp.concatenate([first, second], axis=0)

    far = forward(at_far)
    owed = halves(far[0], far[1]) + halves(swap(far[2], 1), swap(far[3], 1))
    own = forward(after(at_own, owed))
    through = swap(owed, 2)
    near = halves(swap(own[2], 1), swap(own[3], 1))
    summed = halves(own[0], own[1]).astype(F32) + near.astype(F32) + through.astype(F32)
    own_tokens = lax.dynamic_slice_in_dim(tokens, me * own_rows, own_rows, 0).astype(F32)
    unit_one, inv_one = normalize(own_tokens + summed + b_out)
    normed = unit_one * gain_one + shift_one

    def feed(whole_mine, run, meanwhile=None):
        mine = [whole_mine[:CHUNK], whole_mine[CHUNK:]]
        near = [swap(m, 1) for m in mine]
        got = [swap(m, 2) for m in mine]
        blocks = [*mine, *near]
        results = run(blocks, 0)
        gate = results[0][-1] if meanwhile is None else meanwhile(blocks, results)
        through = []
        for c in range(2):
            pair = [after(got[c], gate)]
            pair.append(swap_pieces(pair[0]))
            done = run(pair, len(blocks))
            blocks, results = blocks + pair, results + done
            gate = done[0][-1] + swap_pieces(done[1][-1])
            if c > 0:
                through[0], gate = lax.optimization_barrier((through[0], gate))
            through.append(swap(gate, 2))
        sums = [
            results[c][-1].astype(F32) + swap(results[2 + c][-1], 1).astype(F32) + through[c].astype(F32) for c in range(2)
        ]
        return blocks, results, halves(*sums), gate

    lows, acts, branch, _ = feed(normed.astype(BF16), lambda blocks, n: up_down(blocks, w_up, bias, w_down))
    unit_two, inv_two = normalize(normed + branch + b_down)
    output = (unit_two * gain_two + shift_two).astype(BF16)
    grad_pre_out, grad_gain_two, grad_shift_two = norm_back(cotangent.astype(F32), gain_two, unit_two, inv_two)
    grad_b_down = jnp.sum(grad_pre_out, axis=0)
    grad_low = lax.optimization_barrier(grad_pre_out.astype(BF16))
    unit_low = lax.optimization_barrier(unit_one.astype(BF16))

    sums = []

    def weigh_own(grads, backs):
        blocks = [(acts[n][0], grads[n], lows[n], backs[n][0]) for n in range(4)]
        sums.extend(up_down_weights(at_own, blocks))
        return sums[0]

    grads, backs, back_normed, owed = feed(
        grad_low,
        lambda blocks, n: up_down_back([(b, acts[n + i][1]) for i, b in enumerate(blocks)], w_up, w_down),
        weigh_own,
    )
    blocks = [(acts[n][0], grads[n], lows[n], backs[n][0]) for n in range(4, 8)]
    blocks[0] = (after(blocks[0][0], owed), *blocks[0][1:])
    down_kept, down_sent, up_kept, up_sent, d_bias = up_down_weights(at_own, blocks, sums)
    back_normed = after(back_normed, down_sent, up_sent)
    down = Total(down_kept, down_sent, 0, "dp")
    up = Total(up_kept, up_sent, 1, "dp")
    grad_pre_norm, grad_gain_one, grad_shift_one = norm_back(
        grad_low.astype(F32) + back_normed, gain_one, unit_low.astype(F32), inv_one
    )
    grad_b_out = jnp.sum(grad_pre_norm, axis=0)
    top = lax.optimization_barrier(grad_pre_norm.astype(BF16))
    near = swap(top, 1)
    over = swap(top, 2)

    def values(at, mine, theirs, saved, prev=()):
        return attend_back_values(at, mine, theirs, sequences, taps_back, w_out, segments, saved, prev)

    def queries(at, saved, part, prev=()):
        return attend_back_queries(at, sequences, segments, marks, saved, part, prev)

    def both(*others):
        return down.step(*others), up.step(*others)

    norms = jnp.stack([grad_gain_one, grad_shift_one, grad_b_out, grad_gain_two, grad_shift_two, grad_b_down])
    own_v = values(after(at_own, *both(top)), top, near, own[4:])
    own_q = queries(after(at_own, *both(own_v[0])), own[4:], own_v[3:6])
    norms = norms + after(swap(norms, 1), own_q[0])
    far_v = values(after(at_far, own_q[0]), over, swap(over, 1), far[4:], own_v[0:2])
    norms = norms + after(swap(norms, 2), far_v[0])
    one = Total(far_v[0], far_v[1], 0, "dp")
    far_q = queries(after(at_far, *both(far_v[0])), far[4:], far_v[4:7], own_q[0:2])
    two = Total(far_q[0], far_q[1], 1, "dp")
    far_x = attend_back_tokens(at_far, (far_q[3], far_q[4], far_v[3]), (wq, wk, wv))
    owed = far_x[0] + swap(far_x[1], 1)
    through = swap(owed, 2)
    own_x = attend_back_tokens(at_own, (after(own_q[2], owed), own_q[3], own_v[2]), (wq, wk, wv))
    near = swap(own_x[1], 1)
    small = jnp.concatenate(
        [norms, d_bias[0:1], jnp.pad((far_v[2] + far_q[2])[0 : heads + 2], ((0, 0), (0, dim - WINDOW)))], axis=0
    )
    one.step(far_q[0])
    down.got, up.got, one.got, two.got = lax.optimization_barrier((down.got, up.got, one.got, two.got))
    for part in (two, one, up, down):
        part.step()
    mask = 1
    while mask < lax.axis_size("dp"):
        got = swap(small, mask, "dp")
        if mask == 1:
            got, one.got, two.got = lax.optimization_barrier((got, one.got, two.got))
            two.step()
            one.step()
            down.got, up.got, two.got = lax.optimization_barrier((down.got, up.got, two.got))
        elif mask == 2:
            got, one.got, two.got = lax.optimization_barrier((got, one.got, two.got))
            two.step()
            one.step()
        elif mask == 4:
            got, one.got, two.got, through = lax.optimization_barrier((got, one.got, two.got, through))
            two.step()
        small = small + got
        mask *= 2
    input_grad = top.astype(F32) + own_x[0].astype(F32) + near.astype(F32) + through.astype(F32)
    value_out = one.finish().astype(F32)
    query_key = two.finish().astype(F32)
    down_sum = down.finish().astype(F32)
    up_sum = up.finish().astype(F32)

    return (
        output,
        input_grad,
        query_key[0:width].T,
        query_key[width:].T,
        value_out[0:width].T,
        small[7 + heads, 0:width],
        small[8 + heads, 0:width],
        small[7 : 7 + heads, 0:CONV_TAPS],
        value_out[width:],
        small[2],
        small[0],
        small[1],
        up_sum,
        small[6, 0:units],
        down_sum,
        small[5],
        small[3],
        small[4],
    )


def solution(mesh):
    rows = P(("dp", "tensor"), None)
    columns = P(None, "tensor")
    split_rows = P("tensor", None)
    vector = P("tensor")
    return jax.shard_map(
        per_device,
        mesh=mesh,
        in_specs=(
            P("dp", None), columns, columns, columns, vector, vector, split_rows, split_rows, P(), P(), P(),
            columns, vector, split_rows, P(), P(), P(), rows, P("dp"), P("dp"),
        ),
        out_specs=(
            rows, rows, columns, columns, columns, vector, vector, split_rows, split_rows, P(), P(), P(),
            columns, vector, split_rows, P(), P(), P(),
        ),
        check_vma=False,
    )
```
